32 devices in a mesh: tm: 4 (over y, x), space: 8 (over z, core).
Axes of the slice: x: 2, y: 2, z: 4, core: 2. Of those that a mesh axis runs over, the one named last changes fastest.
Arguments:
- init_state: float32 [512, 512], P('space'), may hold values from -6 to 6
- guess: float32 [4, 512, 512], P('tm', 'space'), may hold values from -6 to 6
- source: float32 [4, 2, 512, 512], P('tm', None, 'space'), may hold values from -6 to 6
- remap: int32 [512], P('space'), may hold values from 0 to 511, as said below
- neighbors: int32 [512, 6], P('space'), may hold values from -1 to 511, as said below
- block_class: int32 [512], P('space'), may hold values from 0 to 3
- step_number: float32 [4], replicated, may hold values from 0.3 to 3
- coarse_inverse: float32 [4, 64, 64], replicated, may hold values from -0.02 to 0.9
- coarse_step: float32 [4, 64, 64], replicated, may hold values from -0.02 to 0.99
Outputs:
- c_states: float32 [4, 512, 512], P('tm', 'space')
- f_states: float32 [4, 512, 512], P('tm', 'space')
The draws below stay inside these ranges and needn't reach their ends.
Inputs may be any that keep to these rules, and one draw needn't show every extreme that they name: `remap`: the entries are a permutation of 0 to 511. The old blocks held by one device of space (aligned runs of 64) send at most 16 blocks to the new blocks held by any one device, and every device sends exactly 16 to some device. `neighbors`: entry [b, f] is the block beside block b across face f (the planes x = 0, x = 7, y = 0, y = 7, z = 0, z = 7 of the block), or -1 at the domain's boundary or at a wall. Links are mutual. Across faces 0 to 3 the neighbour lies in the same aligned run of 64 blocks; across face 4 in the run before, across face 5 in the run after.
All inputs are finite; a program needn't handle non-finite values.
Results may differ from the reference program's by a relative error of at most 0.00018.
Values sent between devices are 32-bit elements; how exact they have to be, the bound alone decides.
A program may use at most 64 MiB of HBM per device.

```python
import math
import jax
import jax.numpy as jnp
from jax import lax

BLK = 64
CELLS = 512
FACE = 64
COARSE = 64
CLASSES = 4
FINE = 2
ITERS = 2
NB = 512
SLOTS = 16
N_TM = 4
N_SPACE = 8


def draw_remap(key, part):
    subkeys = jax.random.split(jax.random.fold_in(key, 7), 4)
    offsets = jax.random.permutation(subkeys[0], N_SPACE)
    half_size = SLOTS // 2
    imbalance = jax.random.randint(subkeys[1], (N_SPACE // 2,), -(half_size - 1), half_size)
    imbalance = imbalance.at[0].set(half_size)
    group_sizes = jnp.stack([half_size + imbalance, half_size - imbalance], axis=1).reshape(-1)
    bounds = jnp.cumsum(group_sizes)
    position = jnp.arange(BLK)
    group_of = jnp.sum((position[:, None] >= bounds[None, :]).astype(jnp.int32), axis=1)
    old_order = jax.vmap(lambda subkey: jax.random.permutation(subkey, BLK))(jax.random.split(subkeys[2], N_SPACE))
    new_order = jax.vmap(lambda subkey: jax.random.permutation(subkey, BLK))(jax.random.split(subkeys[3], N_SPACE))
    device = jnp.arange(N_SPACE)[:, None]
    target = (device + offsets[group_of][None, :]) % N_SPACE
    new_index = target * BLK + new_order[target, position[None, :]]
    old_index = device * BLK + old_order
    result = jnp.zeros((NB,), jnp.int32).at[old_index.reshape(-1)].set(new_index.reshape(-1))
    return result.astype(jnp.int32)


def draw_neighbors(key, part):
    subkeys = jax.random.split(jax.random.fold_in(key, 11), 4)
    lattice_rows = BLK // 8
    order = jax.vmap(lambda subkey: jax.random.permutation(subkey, BLK))(jax.random.split(subkeys[0], N_SPACE))
    open_x = jax.random.randint(subkeys[1], (N_SPACE, BLK), 0, 8) != 0
    open_y = jax.random.randint(subkeys[2], (N_SPACE, BLK), 0, 8) != 0
    open_z = jax.random.randint(subkeys[3], (N_SPACE, BLK), 0, 8) != 0
    site = jnp.arange(BLK)[None, :]
    layer = jnp.arange(N_SPACE)[:, None]
    site_x = site % 8
    site_y = site // 8

    def global_of(layer_at, site_at):
        layer_clip = jnp.clip(layer_at + 0 * site_at, 0, N_SPACE - 1)
        site_clip = jnp.clip(site_at + 0 * layer_at, 0, BLK - 1)
        return layer_clip * BLK + order[layer_clip, site_clip]

    def linked(valid, layer_at, site_at):
        return jnp.where(valid, global_of(layer_at, site_at), -1)
    below_layer = jnp.clip(layer - 1, 0, N_SPACE - 1)
    faces = [linked((site_x > 0) & open_x[layer, jnp.clip(site - 1, 0, BLK - 1)], layer, site - 1), linked((site_x < 7) & open_x[layer, site], layer, site + 1), linked((site_y > 0) & open_y[layer, jnp.clip(site - 8, 0, BLK - 1)], layer, site - 8), linked((site_y < lattice_rows - 1) & open_y[layer, site], layer, site + 8), linked((layer > 0) & open_z[below_layer, site], layer - 1, site), linked((layer < N_SPACE - 1) & open_z[layer, site], layer + 1, site)]
    stacked = jnp.stack(faces, axis=2)
    row_index = layer * BLK + order
    table = jnp.full((NB, 6), -1, jnp.int32).at[row_index.reshape(-1)].set(stacked.reshape(-1, 6))
    return table.astype(jnp.int32)


def coarse_matrix(key, lowest, topmost, off_spread):
    subkeys = jax.random.split(key, 2)
    diagonal = jax.random.uniform(subkeys[0], (CLASSES, COARSE), jnp.float32, lowest, topmost)
    offdiag = jax.random.uniform(subkeys[1], (CLASSES, COARSE, COARSE), jnp.float32, -off_spread, off_spread)
    identity = jnp.eye(COARSE, dtype=jnp.float32)
    return offdiag * (1.0 - identity) + identity * diagonal[:, :, None]


def draw_coarse_inverse(key, part):
    matrix = coarse_matrix(jax.random.fold_in(key, 31), 0.15, 0.6, 0.02)
    return matrix


def draw_coarse_step(key, part):
    matrix = coarse_matrix(jax.random.fold_in(key, 37), 0.55, 0.97, 0.02)
    return matrix


def set_ends(array, own_key, low, largest):
    index_at = [jax.random.randint(jax.random.fold_in(own_key, axis), (), 0, length) for axis, length in enumerate(array.shape)]
    widest = array.shape.index(max(array.shape))
    beside = index_at[:widest] + [(index_at[widest] + 1) % array.shape[widest]] + index_at[widest + 1:]
    return array.at[tuple(index_at)].set(low).at[tuple(beside)].set(largest)


def steps_of(own_key, dims, shards, least, top_value):
    gain, own = 1.0, jax.random.fold_in(own_key, 6)
    for dim, blocks in shards:
        draws = jnp.exp(jax.random.uniform(jax.random.fold_in(own, dim), (blocks,), jnp.float32, least / len(shards), top_value / len(shards)))
        gain = gain * jnp.repeat(draws, dims[dim] // blocks).reshape([-1 if axis == dim else 1 for axis in range(len(dims))])
    return gain


def noise(key, dims, spread, reach, shards=(), held_as=jnp.bfloat16):
    gain = steps_of(key, dims, shards, -0.22, 0.18) if shards else 1.0
    drawn = jax.random.normal(key, dims, jnp.float32) * spread * gain
    return jnp.minimum(jnp.maximum(drawn, -reach), reach).astype(held_as)


def setup_inputs(seed: int = 0) -> dict:
    seeds = jax.random.split(jax.random.key(seed), 10)
    init_state = noise(seeds[0], (NB, CELLS), 1.0, 6.0, ((0, 8),), jnp.float32)
    guess = noise(seeds[1], (N_TM, NB, CELLS), 1.0, 6.0, ((0, 4), (1, 8)), jnp.float32)
    source = noise(seeds[2], (N_TM, FINE, NB, CELLS), 1.0, 6.0, ((0, 4), (2, 8)), jnp.float32)
    remap = draw_remap(jax.random.fold_in(seeds[9], 71), 0)
    neighbors = draw_neighbors(jax.random.fold_in(seeds[9], 71), 0)
    block_class = set_ends(jax.random.randint(seeds[5], (NB,), 0, CLASSES), jax.random.fold_in(seeds[5], 1), 0, CLASSES - 1).astype(jnp.int32)
    step_number = jnp.clip(jnp.exp(jax.random.uniform(seeds[6], (CLASSES,), jnp.float32, math.log(0.3), math.log(3.0))), 0.3, 3.0)
    coarse_inverse = draw_coarse_inverse(jax.random.fold_in(seeds[9], 71), 0)
    coarse_step = draw_coarse_step(jax.random.fold_in(seeds[9], 71), 0)
    return dict(init_state=init_state, guess=guess, source=source, remap=remap, neighbors=neighbors, block_class=block_class, step_number=step_number, coarse_inverse=coarse_inverse, coarse_step=coarse_step)


damping = 0.8
highest = lax.Precision.HIGHEST


def block_faces(state_now):
    num_blocks = state_now.shape[0]
    cube = state_now.reshape(num_blocks, 8, 8, 8)
    planes = [cube[:, 0], cube[:, 7], cube[:, :, 0], cube[:, :, 7], cube[:, :, :, 0], cube[:, :, :, 7]]
    return [plane.reshape(num_blocks, FACE) for plane in planes]


def ghost_faces(state_now, neighbors):
    own_faces = block_faces(state_now)
    ghosts = []
    for face_no in range(6):
        neighbor_ids = neighbors[:, face_no]
        picked = jnp.take(own_faces[face_no ^ 1], jnp.clip(neighbor_ids, 0, None), axis=0)
        ghosts.append(jnp.where(neighbor_ids[:, None] >= 0, picked, 0.0))
    return ghosts


def operate(state_now, neighbors, diffusion):
    num_blocks = state_now.shape[0]
    cube = state_now.reshape(num_blocks, 8, 8, 8)
    planes = [ghost.reshape(num_blocks, 8, 8) for ghost in ghost_faces(state_now, neighbors)]
    along_x = jnp.concatenate([planes[0][:, None], cube[:, :-1]], 1) + jnp.concatenate([cube[:, 1:], planes[1][:, None]], 1)
    along_y = jnp.concatenate([planes[2][:, :, None], cube[:, :, :-1]], 2) + jnp.concatenate([cube[:, :, 1:], planes[3][:, :, None]], 2)
    along_z = jnp.concatenate([planes[4][:, :, :, None], cube[:, :, :, :-1]], 3) + jnp.concatenate([cube[:, :, :, 1:], planes[5][:, :, :, None]], 3)
    beside_all = (along_x + along_y + along_z).reshape(num_blocks, CELLS)
    return (1.0 + 6.0 * diffusion) * state_now - diffusion * beside_all


def restrict(state_now):
    num_blocks = state_now.shape[0]
    return state_now.reshape(num_blocks, 4, 2, 4, 2, 4, 2).mean(axis=(2, 4, 6)).reshape(num_blocks, COARSE)


def prolong(coarse):
    num_blocks = coarse.shape[0]
    cube = coarse.reshape(num_blocks, 4, 4, 4)
    cube = jnp.repeat(jnp.repeat(jnp.repeat(cube, 2, axis=1), 2, axis=2), 2, axis=3)
    return cube.reshape(num_blocks, CELLS)


def apply_classes(matrices, coarse, block_class):
    summed = jnp.zeros_like(coarse)
    for class_no in range(CLASSES):
        product = jnp.dot(coarse, matrices[class_no].T, precision=highest)
        summed = summed + jnp.where(block_class[:, None] == class_no, product, 0.0)
    return summed


def vcycle(driving, neighbors, diffusion, block_class, coarse_inverse):
    diagonal = 1.0 + 6.0 * diffusion
    iterate = damping * driving / diagonal
    iterate = iterate + damping * (driving - operate(iterate, neighbors, diffusion)) / diagonal
    residue = driving - operate(iterate, neighbors, diffusion)
    iterate = iterate + prolong(apply_classes(coarse_inverse, restrict(residue), block_class))
    for sweep_no in range(2):
        iterate = iterate + damping * (driving - operate(iterate, neighbors, diffusion)) / diagonal
    return iterate


def reference(init_state, guess, source, remap, neighbors, block_class, step_number, coarse_inverse, coarse_step):
    moved_start = jnp.zeros_like(init_state).at[remap].set(init_state)
    moved_guess = jnp.zeros_like(guess).at[:, remap].set(guess)
    diffusion = step_number[block_class][:, None]
    states = [moved_guess[slice_no] for slice_no in range(N_TM)]
    fine_list = []
    for sweep_no in range(ITERS):
        fine_list = []
        residuals = []
        for slice_no in range(N_TM):
            before = moved_start if slice_no == 0 else states[slice_no - 1]
            fine_state = vcycle(before + source[slice_no, 0], neighbors, diffusion, block_class, coarse_inverse)
            residual = vcycle(fine_state + source[slice_no, 1], neighbors, diffusion, block_class, coarse_inverse) - states[slice_no]
            fine_list.append(fine_state)
            residuals.append(residual)
        carried = jnp.zeros((init_state.shape[0], COARSE), jnp.float32)
        updated = []
        for slice_no in range(N_TM):
            pushed = apply_classes(coarse_step, carried, block_class)
            updated.append(states[slice_no] + (prolong(pushed) + residuals[slice_no]))
            carried = pushed + restrict(residuals[slice_no])
        states = updated
    return jnp.stack(states), jnp.stack(fine_list)
```

```python
import functools

import jax
import jax.numpy as jnp
from jax import lax
from jax.experimental import pallas as pl
from jax.experimental.pallas import tpu as pltpu
from jax.sharding import PartitionSpec as P

CELLS = 512
COARSE = 64
CLASSES = 4
ITERS = 2
DAMP = 0.8
MESH = pl.DeviceIdType.MESH
F32 = jnp.float32
BF16 = jnp.bfloat16


def split(value):
    high = value.astype(BF16)
    return high, (value - high.astype(F32)).astype(BF16)


def dot(left, right):
    return jnp.dot(left, right, preferred_element_type=F32)


def roll(value, shift):
    shift = shift % 128
    return value if shift == 0 else pltpu.roll(value, shift, 1)


def lanes_from(value, index):
    return jnp.take_along_axis(value, index, axis=1)


def iota(shape, dim):
    return lax.broadcasted_iota(jnp.int32, shape, dim)


def kernel(
    n_tm, n_sp, bk,
    init_ref, guess_ref, source_ref, remap_ref, nb_ref, class_ref, step_ref, inv_ref, cstep_ref,
    c_ref, f_ref,
    gb, ib, gr, br, hs, hr, st, hsrc, hand, cs, cr,
    ohl, ohn, oh4, oh5, oh4t, oh5t, rm, pm, mi, ms, xs, ws, bs, zs, ps, scale, near,
    slots_out, slots_in, so_sem, si_sem,
    gs_sem, gr_sem, ps_sem, is_sem, br_sem, hs_sem, hr_sem, ts_sem, tr_sem, cs_sem, cr_sem,
):
    k = lax.axis_index("tm")
    s = lax.axis_index("space")
    nb = init_ref.shape[0]
    rows = n_sp * bk
    bits = nb.bit_length() - 1
    setup = ITERS * 4

    hr[...] = jnp.zeros_like(hr)
    barrier = pltpu.get_barrier_semaphore()
    for off in range(1, n_sp):
        pl.semaphore_signal(barrier, inc=1, device_id=(k, lax.rem(s + off, n_sp)), device_id_type=MESH)
    for off in range(1, n_tm):
        pl.semaphore_signal(barrier, inc=1, device_id=(lax.rem(k + off, n_tm), s), device_id_type=MESH)

    @pl.when(k < n_tm - 1)
    def _():
        for off in range(1, n_sp):
            pl.semaphore_signal(barrier, inc=1, device_id=(k + 1, lax.rem(s + off, n_sp)), device_id_type=MESH)

    @pl.when(k > 0)
    def _():
        for off in range(1, n_sp):
            pl.semaphore_signal(barrier, inc=1, device_id=(k - 1, lax.rem(s + off, n_sp)), device_id_type=MESH)

    eye = iota((nb, nb), 0) == iota((nb, nb), 1)

    def column(row):
        return jnp.sum(jnp.where(eye, row, 0.0), axis=1, keepdims=True)

    remap_row = remap_ref[...]
    target_row = lax.shift_right_logical(remap_row, bits)
    slot_row = (remap_row - lax.shift_left(target_row, bits)).astype(F32)
    target_f = target_row.astype(F32)
    same = (column(target_f) == target_f) & (iota((nb, nb), 0) < iota((nb, nb), 1))
    pos_row = jnp.sum(jnp.where(same, 1.0, 0.0), axis=0, keepdims=True)
    send_row = target_f * float(bk) + pos_row
    chosen = iota((rows, nb), 0).astype(F32) == send_row
    send_mat = jnp.where(chosen, 1.0, 0.0)
    slot_col = jnp.sum(jnp.where(chosen, slot_row + 1.0, 0.0), axis=1, keepdims=True) - 1.0
    send_mat = jnp.concatenate([send_mat, send_mat], axis=1).astype(BF16)

    def bucketed(value):
        return dot(send_mat, jnp.concatenate(split(value), axis=0)).reshape(n_sp, bk, CELLS)

    spot = iota((n_sp, bk, 128), 1) == iota((n_sp, bk, 128), 2)
    slot_wide = jnp.broadcast_to(slot_col, (rows, 128)).reshape(n_sp, bk, 128)
    slot_lanes = jnp.sum(jnp.where(spot, slot_wide, 0.0), axis=1, keepdims=True)
    slots_out[...] = jnp.broadcast_to(slot_lanes, (n_sp, 8, 128))
    gb[...] = bucketed(guess_ref[0])

    @pl.when(k == 0)
    def _():
        ib[...] = bucketed(init_ref[...])

    sides = jnp.minimum(k, 1) + jnp.minimum(n_tm - 1 - k, 1)
    pl.semaphore_wait(barrier, (n_sp - 1) * (1 + sides) + n_tm - 1)

    def spread_copy(src, ssem, off, col):
        to = lax.rem(s + off, n_sp)
        return pltpu.make_async_remote_copy(
            src_ref=src.at[to], dst_ref=br.at[s], send_sem=ssem.at[off], recv_sem=br_sem.at[s],
            device_id=(col, to), device_id_type=MESH)

    def own_copy(off):
        to = lax.rem(s + off, n_sp)
        return pltpu.make_async_remote_copy(
            src_ref=gb.at[to], dst_ref=gr.at[s], send_sem=gs_sem.at[off],
            recv_sem=gr_sem.at[s], device_id=(k, to), device_id_type=MESH)

    def spread_landed(off):
        origin = lax.rem(s + off, n_sp)
        pltpu.make_async_remote_copy(
            src_ref=gb.at[origin], dst_ref=br.at[origin], send_sem=ps_sem.at[off],
            recv_sem=br_sem.at[origin], device_id=(lax.rem(k + 1, n_tm), origin),
            device_id_type=MESH).wait_recv()

    def own_landed(off):
        origin = lax.rem(s + off, n_sp)
        pltpu.make_async_remote_copy(
            src_ref=gb.at[origin], dst_ref=gr.at[origin],
            send_sem=gs_sem.at[off], recv_sem=gr_sem.at[origin], device_id=(k, origin),
            device_id_type=MESH).wait_recv()

    def slots_copy(off):
        to = lax.rem(s + off, n_sp)
        return pltpu.make_async_remote_copy(
            src_ref=slots_out.at[to], dst_ref=slots_in.at[s], send_sem=so_sem.at[off],
            recv_sem=si_sem.at[s], device_id=(k, to), device_id_type=MESH)

    def slots_landed(off):
        origin = lax.rem(s + off, n_sp)
        pltpu.make_async_remote_copy(
            src_ref=slots_out.at[origin], dst_ref=slots_in.at[origin], send_sem=so_sem.at[off],
            recv_sem=si_sem.at[origin], device_id=(k, origin), device_id_type=MESH).wait_recv()

    for off in range(1, n_sp):
        slots_copy(off).start()
    slots_in[s] = slots_out[s]

    @pl.when(k == 0)
    def _():
        for off in range(1, n_sp):
            spread_copy(ib, is_sem, off, k).start()
        br[s] = ib[s]

    @pl.when(k < n_tm - 1)
    def _():
        for off in range(n_sp):
            spread_copy(gb, ps_sem, off, lax.rem(k + 1, n_tm)).start()

    class_col = column(class_ref[...].astype(F32))
    diffusion = jnp.zeros((nb, 1), F32)
    for cl in range(CLASSES):
        diffusion = diffusion + jnp.where(class_col == float(cl), step_ref[:, cl:cl + 1], 0.0)
    dif = jnp.broadcast_to(diffusion, (nb, 128))
    scale[0] = DAMP * dif / (1.0 + 6.0 * dif)
    scale[1] = DAMP / (1.0 + 6.0 * dif)
    scale[2] = (1.0 + 6.0 * dif) / DAMP
    lane = iota((nb, 128), 1)
    linked = [column(nb_ref[face:face + 1, :].astype(F32)).astype(jnp.int32) for face in range(6)]
    table = jnp.where(lane == 4, dif, -1.0)
    for face in range(4):
        table = jnp.where(lane == face, (linked[face] - s * nb).astype(F32), table)
    hs[setup, 0] = table
    hs[setup, 1] = table

    def halo_up(slot):
        return pltpu.make_async_remote_copy(
            src_ref=hs.at[slot, 0], dst_ref=hr.at[slot, 0], send_sem=hs_sem.at[slot, 0],
            recv_sem=hr_sem.at[slot, 0], device_id=(k, lax.rem(s + 1, n_sp)), device_id_type=MESH)

    def halo_down(slot):
        return pltpu.make_async_remote_copy(
            src_ref=hs.at[slot, 1], dst_ref=hr.at[slot, 1], send_sem=hs_sem.at[slot, 1],
            recv_sem=hr_sem.at[slot, 1], device_id=(k, lax.rem(s + n_sp - 1, n_sp)), device_id_type=MESH)

    def exchange(slot):
        @pl.when(s < n_sp - 1)
        def _():
            halo_up(slot).start()

        @pl.when(s > 0)
        def _():
            halo_down(slot).start()

    def exchanged(slot):
        @pl.when(s > 0)
        def _():
            halo_up(slot).wait_recv()

        @pl.when(s < n_sp - 1)
        def _():
            halo_down(slot).wait_recv()

    exchange(setup)
    gr[s] = gb[s]

    lane_nb = iota((nb, nb), 1)
    for face in range(6):
        shift = s * nb + (0 if face < 4 else (-nb if face == 4 else nb))
        ids = linked[face]
        hot = jnp.where((ids - shift == lane_nb) & (ids >= 0), 1.0, 0.0)
        if face >= 4:
            turned = hot.T
            turned = jnp.concatenate([turned, turned], axis=1).astype(BF16)
            (oh4t if face == 4 else oh5t)[...] = turned
        hot = jnp.concatenate([hot, hot], axis=1).astype(BF16)
        if face < 4:
            ohl[face * nb:(face + 1) * nb] = hot
        elif face == 4:
            oh4[...] = hot
        else:
            oh5[...] = hot

    def parent(cell):
        return (lax.shift_right_logical(cell, 7) * 16
                + (lax.shift_right_logical(cell, 4) & 3) * 4
                + lax.shift_right_logical(cell & 7, 1))

    rm[...] = jnp.where(parent(iota((CELLS, 128), 0)) == iota((CELLS, 128), 1), 0.125, 0.0).astype(BF16)
    pm[...] = jnp.where(parent(iota((128, CELLS), 1)) == (iota((128, CELLS), 0) & 63), 1.0, 0.0).astype(BF16)
    for src, dst in ((inv_ref, mi), (cstep_ref, ms)):
        high, low = split(src[...].T)
        dst[...] = jnp.concatenate([high, high, low, jnp.zeros_like(low)], axis=0)

    zz = lane & 7
    yy = lax.shift_right_logical(lane, 3) & 7
    left = lane < 64

    def classes(coarse, mat):
        high = coarse.astype(BF16).astype(F32)
        both = high + roll(coarse - high, 64)
        product = dot(jnp.concatenate([both, high], axis=1).astype(BF16), mat[...])
        low_c = jnp.where(left, 0.0, 1.0)
        picked = (jnp.where(class_col == low_c, product[:, :128], 0.0)
                  + jnp.where(class_col == low_c + 2.0, product[:, 128:], 0.0))
        return jnp.where(left, picked + roll(picked, 64), 0.0)

    def prolong(coarse):
        high = coarse.astype(BF16).astype(F32)
        return dot((high + roll(coarse - high, 64)).astype(BF16), pm[...])

    def restrict(value):
        both = dot(jnp.concatenate(split(value), axis=0), rm[...])
        return both[:nb] + both[nb:]

    def tiles_of(value):
        return [value[:, 128 * j:128 * j + 128] for j in range(4)]

    def gathered(hot, value):
        return dot(hot, jnp.concatenate(split(value), axis=0))

    def planes(tiles):
        top = bottom = jnp.zeros((nb, 128), F32)
        for j in range(4):
            top = jnp.where(zz == j, roll(tiles[j], j - 7), top)
            top = jnp.where(zz == 4 + j, roll(tiles[j], j - 2), top)
            bottom = jnp.where(zz == j, roll(tiles[j], j), bottom)
            bottom = jnp.where(zz == 4 + j, roll(tiles[j], j + 3), bottom)
        return top, bottom

    def plane_step(plane, driven, side, cross):
        w = gathered(ohn[side], plane)
        turned = lanes_from(plane, lax.rem(lane + 64, 128))
        total = turned + jnp.where(
            left, jnp.where(zz == 0, roll(w[:nb], -67), roll(turned, 1)),
            jnp.where(zz == 3, roll(w[nb:2 * nb], 67), roll(turned, -1)))
        total = total + jnp.where(yy == 0, roll(w[2 * nb:3 * nb], -56), roll(plane, 8))
        total = total + jnp.where(yy == 7, roll(w[3 * nb:], 56), roll(plane, -8))
        total = total + roll(plane, -4) + cross
        return (1.0 - DAMP) * plane + driven + near[side] * total

    def inside(tiles):
        xface = jnp.where(left, roll(tiles[3], 64), roll(tiles[0], 64))
        yface = jnp.zeros((nb, 128), F32)
        for j in range(4):
            yface = jnp.where(yy == j, roll(tiles[j], 8 * j - 56), yface)
            yface = jnp.where(yy == 4 + j, roll(tiles[j], 32 + 8 * j), yface)
        ghosts = gathered(ohl[...], jnp.concatenate([xface, yface], axis=1))
        turned = [roll(tile, 64) for tile in tiles]
        turned = [ghosts[:nb, :128]] + turned + [ghosts[nb:2 * nb, :128]]
        g2 = ghosts[2 * nb:3 * nb, 128:]
        g3 = ghosts[3 * nb:, 128:]
        sums = []
        for j in range(4):
            total = turned[j + 1] + jnp.where(left, turned[j], turned[j + 2])
            total = total + jnp.where(yy == 0, roll(g2, -8 * j), roll(tiles[j], 8))
            total = total + jnp.where(yy == 7, roll(g3, 24 - 8 * j), roll(tiles[j], -8))
            total = total + jnp.where(zz == 0, 0.0, roll(tiles[j], 1))
            total = total + jnp.where(zz == 7, 0.0, roll(tiles[j], -1))
            sums.append(total)
        return sums

    def with_ends(sums, below, above):
        g4 = gathered(oh4[...], below)
        g5 = gathered(oh5[...], above)
        return [
            sums[j] + jnp.where(zz == 0, roll(g4, -j), 0.0) + jnp.where(zz == 7, roll(g5, 7 - j), 0.0)
            for j in range(4)
        ]

    def swept(tiles, driven, sums):
        return [(1.0 - DAMP) * tiles[j] + driven[j] + scale[0] * sums[j] for j in range(4)]

    def vcycle(base):
        driven = tiles_of(ws[...])
        for stage in range(2):
            slot = base + stage
            tiles = driven if stage == 0 else tiles_of(xs[...])
            top, bottom = planes(tiles)
            hs[slot, 0] = top
            hs[slot, 1] = bottom
            exchange(slot)
            for off in range(1, n_sp):
                turn = (off - 1) * 4 // (n_sp - 1)

                @pl.when((k == n_tm - 1) & (slot == turn))
                def _():
                    own_copy(off).start()
            sums = inside(tiles)
            up_cross = gathered(oh4t[...], bottom)
            down_cross = gathered(oh5t[...], top)
            exchanged(slot)
            below, above = hr[slot, 0], hr[slot, 1]
            tiles = swept(tiles, driven, with_ends(sums, below, above))
            below = plane_step(below, hr[base, 0], 0, up_cross)
            above = plane_step(above, hr[base, 1], 1, down_cross)
            sums = with_ends(inside(tiles), below, above)
            if stage == 0:
                rest = jnp.concatenate(
                    [driven[j] - DAMP * tiles[j] + scale[0] * sums[j] for j in range(4)], axis=1)
                fix = prolong(classes(scale[2] * restrict(rest), mi))
                xs[...] = jnp.concatenate(tiles, axis=1) + fix
            else:
                xs[...] = jnp.concatenate(swept(tiles, driven, sums), axis=1)

    def drive(value):
        ws[...] = value * jnp.concatenate([scale[1]] * 4, axis=1)

    exchanged(setup)
    for side in range(2):
        table = hr[setup, side]
        far = table[:, 4:5]
        near[side] = jnp.broadcast_to(DAMP * far / (1.0 + 6.0 * far), (nb, 128))
        for face in range(4):
            hot = jnp.where(table[:, face:face + 1] == lane_nb.astype(F32), 1.0, 0.0)
            ohn[side, face * nb:(face + 1) * nb] = jnp.concatenate([hot, hot], axis=1).astype(BF16)

    for off in range(1, n_sp):
        spread_landed(off)

    @pl.when(k > 0)
    def _():
        spread_landed(0)

    for off in range(1, n_sp):
        slots_landed(off)
    slots = jnp.sum(jnp.where(spot, slots_in[:, :1], 0.0), axis=2, keepdims=True)
    slots = jnp.broadcast_to(slots, (n_sp, bk, nb)).reshape(rows, nb)
    take = jnp.where(slots == iota((rows, nb), 1).astype(F32), 1.0, 0.0).T.astype(BF16)

    def settled(value):
        high, low = split(value)
        return dot(take, high) + dot(take, low)

    bs[...] = settled(br[...].reshape(rows, CELLS))

    def hand_copy(it):
        return pltpu.make_async_remote_copy(
            src_ref=hsrc.at[it], dst_ref=hand.at[it], send_sem=ts_sem.at[it], recv_sem=tr_sem.at[it],
            device_id=(lax.rem(k + 1, n_tm), s), device_id_type=MESH)

    def back_copy():
        return pltpu.make_async_remote_copy(
            src_ref=hsrc.at[ITERS - 1], dst_ref=st.at[0], send_sem=ts_sem.at[ITERS - 1],
            recv_sem=tr_sem.at[ITERS - 1], device_id=(lax.rem(k + n_tm - 1, n_tm), s),
            device_id_type=MESH)

    @pl.when(k > 0)
    def _():
        hsrc[ITERS - 1] = bs[...]
        back_copy().start()

    def coarse_copy(it, off):
        return pltpu.make_async_remote_copy(
            src_ref=cs.at[it], dst_ref=cr.at[it, k], send_sem=cs_sem.at[it, off],
            recv_sem=cr_sem.at[it, k], device_id=(lax.rem(k + off, n_tm), s), device_id_type=MESH)

    def coarse_landed(it, origin):
        pltpu.make_async_remote_copy(
            src_ref=cs.at[it], dst_ref=cr.at[it, origin], send_sem=cs_sem.at[it, 0],
            recv_sem=cr_sem.at[it, origin], device_id=(lax.rem(k + 1, n_tm), s),
            device_id_type=MESH).wait_recv()

    def iteration(it, carry):
        drive(bs[...] + source_ref[0, 0])

        def one(v, c):
            vcycle((it * 2 + v) * 2)

            @pl.when(v == 0)
            def _():
                f_ref[0] = xs[...]
                drive(xs[...] + source_ref[0, 1])
            return c

        lax.fori_loop(0, 2, one, 0)

        @pl.when((it == 0) & (k < n_tm - 1))
        def _():
            back_copy().wait_recv()

        @pl.when((it == 0) & (k == n_tm - 1))
        def _():
            for off in range(1, n_sp):
                own_landed(off)
            st[0] = settled(gr[...].reshape(rows, CELLS))

        residual = xs[...] - st[it]
        cs[it] = restrict(residual)
        for off in range(1, n_tm):
            @pl.when(k + off < n_tm)
            def _():
                coarse_copy(it, off).start()

        @pl.when((k < n_tm - 1) & (it < ITERS - 1))
        def _():
            hsrc[it] = xs[...]
            hand_copy(it).start()

        zs[...] = jnp.zeros_like(zs)
        ps[...] = jnp.zeros_like(ps)
        for j in range(n_tm - 1):
            @pl.when(j < k)
            def _():
                coarse_landed(it, j)
                pushed = classes(zs[...], ms)
                ps[...] = pushed
                zs[...] = pushed + cr[it, j]
        st[it + 1] = st[it] + (prolong(classes(zs[...], ms)) + residual)

        @pl.when((k > 0) & (it < ITERS - 1))
        def _():
            hand_copy(it).wait_recv()
            bs[...] = hand[it] + prolong(ps[...])
        return carry

    lax.fori_loop(0, ITERS, iteration, 0)
    c_ref[0] = st[ITERS]

    for off in range(1, n_sp):
        slots_copy(off).wait_send()

    @pl.when(k == n_tm - 1)
    def _():
        for off in range(1, n_sp):
            own_copy(off).wait_send()

    @pl.when(k > 0)
    def _():
        back_copy().wait_send()

    @pl.when(k == 0)
    def _():
        for off in range(1, n_sp):
            spread_copy(ib, is_sem, off, k).wait_send()

    @pl.when(k < n_tm - 1)
    def _():
        for off in range(n_sp):
            spread_copy(gb, ps_sem, off, lax.rem(k + 1, n_tm)).wait_send()

    def drain(slot, carry):
        @pl.when(s < n_sp - 1)
        def _():
            halo_up(slot).wait_send()

        @pl.when(s > 0)
        def _():
            halo_down(slot).wait_send()
        return carry

    lax.fori_loop(0, setup + 1, drain, 0)
    for it in range(ITERS):
        if it < ITERS - 1:
            @pl.when(k < n_tm - 1)
            def _():
                hand_copy(it).wait_send()
        for off in range(1, n_tm):
            @pl.when(k + off < n_tm)
            def _():
                coarse_copy(it, off).wait_send()


def solution(mesh):
    n_tm, n_sp = mesh.shape["tm"], mesh.shape["space"]

    def body(init_state, guess, source, remap, neighbors, block_class, step_number, inverse, cstep):
        nb = init_state.shape[0]
        bk = -(-(2 * nb // n_sp) // 8) * 8
        slots = ITERS * 4 + 1
        dma = pltpu.SemaphoreType.DMA
        out = jax.ShapeDtypeStruct((1, nb, CELLS), F32)
        return pl.pallas_call(
            functools.partial(kernel, n_tm, n_sp, bk),
            name="mgrit",
            out_shape=(out, out),
            in_specs=[pl.BlockSpec(memory_space=pltpu.VMEM)] * 9,
            out_specs=[pl.BlockSpec(memory_space=pltpu.VMEM)] * 2,
            scratch_shapes=[
                pltpu.VMEM((n_sp, bk, CELLS), F32),
                pltpu.VMEM((n_sp, bk, CELLS), F32),
                pltpu.VMEM((n_sp, bk, CELLS), F32),
                pltpu.VMEM((n_sp, bk, CELLS), F32),
                pltpu.VMEM((slots, 2, nb, 128), F32),
                pltpu.VMEM((slots, 2, nb, 128), F32),
                pltpu.VMEM((ITERS + 1, nb, CELLS), F32),
                pltpu.VMEM((ITERS, nb, CELLS), F32),
                pltpu.VMEM((ITERS, nb, CELLS), F32),
                pltpu.VMEM((ITERS, nb, 128), F32),
                pltpu.VMEM((ITERS, n_tm, nb, 128), F32),
                pltpu.VMEM((4 * nb, 2 * nb), BF16),
                pltpu.VMEM((2, 4 * nb, 2 * nb), BF16),
                pltpu.VMEM((nb, 2 * nb), BF16),
                pltpu.VMEM((nb, 2 * nb), BF16),
                pltpu.VMEM((nb, 2 * nb), BF16),
                pltpu.VMEM((nb, 2 * nb), BF16),
                pltpu.VMEM((CELLS, 128), BF16),
                pltpu.VMEM((128, CELLS), BF16),
                pltpu.VMEM((4 * COARSE, CLASSES * COARSE), BF16),
                pltpu.VMEM((4 * COARSE, CLASSES * COARSE), BF16),
                pltpu.VMEM((nb, CELLS), F32),
                pltpu.VMEM((nb, CELLS), F32),
                pltpu.VMEM((nb, CELLS), F32),
                pltpu.VMEM((nb, 128), F32),
                pltpu.VMEM((nb, 128), F32),
                pltpu.VMEM((3, nb, 128), F32),
                pltpu.VMEM((2, nb, 128), F32),
                pltpu.VMEM((n_sp, 8, 128), F32),
                pltpu.VMEM((n_sp, 8, 128), F32),
                dma((n_sp,)), dma((n_sp,)),
                dma((n_sp,)), dma((n_sp,)), dma((n_sp,)), dma((n_sp,)), dma((n_sp,)),
                dma((slots, 2)), dma((slots, 2)),
                dma((ITERS,)), dma((ITERS,)),
                dma((ITERS, n_tm)), dma((ITERS, n_tm)),
            ],
            compiler_params=pltpu.CompilerParams(collective_id=0, has_side_effects=True),
        )(
            init_state, guess, source, remap.reshape(1, nb), neighbors.T, block_class.reshape(1, nb),
            step_number.reshape(1, CLASSES), inverse.reshape(CLASSES * COARSE, COARSE),
            cstep.reshape(CLASSES * COARSE, COARSE),
        )

    placed = (
        P("space", None), P("tm", "space", None), P("tm", None, "space", None), P("space"),
        P("space", None), P("space"), P(), P(), P(),
    )
    return jax.shard_map(
        body, mesh=mesh, in_specs=placed,
        out_specs=(P("tm", "space", None), P("tm", "space", None)), check_vma=False,
    )
```

```python
import functools

import jax
import jax.numpy as jnp
from jax import lax
from jax.experimental import pallas as pl
from jax.experimental.pallas import tpu as pltpu
from jax.sharding import PartitionSpec as P

CELLS = 512
COARSE = 64
CLASSES = 4
ITERS = 2
DAMP = 0.8
PLANE = 32
MESH = pl.DeviceIdType.MESH
F32 = jnp.float32
BF16 = jnp.bfloat16


def split(value):
    high = value.astype(BF16)
    return high, (value - high.astype(F32)).astype(BF16)


def dot(left, right):
    return jnp.dot(left, right, preferred_element_type=F32)


def iota(shape, dim):
    return lax.broadcasted_iota(jnp.int32, shape, dim)


def turn(value):
    return pltpu.roll(value, 64, 1)


def along_y(value, shift):
    rows = value.shape[0]
    return pltpu.roll(value.reshape(rows // 8, 8, 128), shift % 8, 1).reshape(rows, 128)


def tiled(table, rows):
    return jnp.broadcast_to(table[None], (rows // 8, 8, 128)).reshape(rows, 128)


def lanes_from(value, index):
    return jnp.take_along_axis(
        value, tiled(index, value.shape[0]), axis=1, mode="promise_in_bounds")


def kernel(
    n_tm, n_sp, bk,
    init_ref, guess_ref, source_ref, remap_ref, nb_ref, class_ref, step_ref, inv_ref, cstep_ref,
    c_ref, f_ref,
    gb, ib, gr, br, tab_s, tab_r, tidx, tmask, tscale, src, srch, shuffle,
    bs, drv, drv2, x3a, x3b, e1, e2, e4, st, xf, hsrc, hand, cs, cr, zs, ps, mi, ms,
    slots_out, slots_in, so_sem, si_sem,
    gs_sem, gr_sem, ps_sem, is_sem, br_sem, hs_sem, hr_sem, ts_sem, tr_sem, bk_sem, bq_sem, cs_sem, cr_sem,
):
    k = lax.axis_index("tm")
    s = lax.axis_index("space")
    nb = init_ref.shape[0]
    rows = n_sp * bk
    bits = nb.bit_length() - 1
    last = n_tm - 1

    barrier = pltpu.get_barrier_semaphore()
    for off in range(1, n_sp):
        pl.semaphore_signal(barrier, inc=1, device_id=(k, lax.rem(s + off, n_sp)), device_id_type=MESH)
    for off in range(1, n_tm):
        pl.semaphore_signal(barrier, inc=1, device_id=(lax.rem(k + off, n_tm), s), device_id_type=MESH)

    @pl.when(k < last)
    def _():
        for off in range(1, n_sp):
            pl.semaphore_signal(barrier, inc=1, device_id=(k + 1, lax.rem(s + off, n_sp)), device_id_type=MESH)

    @pl.when(k > 0)
    def _():
        for off in range(1, n_sp):
            pl.semaphore_signal(barrier, inc=1, device_id=(k - 1, lax.rem(s + off, n_sp)), device_id_type=MESH)

    eye = iota((nb, nb), 0) == iota((nb, nb), 1)

    def column(row):
        return jnp.sum(jnp.where(eye, row, 0.0), axis=1, keepdims=True)

    remap_row = remap_ref[...]
    target_row = lax.shift_right_logical(remap_row, bits)
    slot_row = (remap_row - lax.shift_left(target_row, bits)).astype(F32)
    target_f = target_row.astype(F32)
    same = (column(target_f) == target_f) & (iota((nb, nb), 0) < iota((nb, nb), 1))
    pos_row = jnp.sum(jnp.where(same, 1.0, 0.0), axis=0, keepdims=True)
    send_row = target_f * float(bk) + pos_row
    chosen = iota((rows, nb), 0).astype(F32) == send_row
    send_mat = jnp.where(chosen, 1.0, 0.0)
    slot_col = jnp.sum(jnp.where(chosen, slot_row + 1.0, 0.0), axis=1, keepdims=True) - 1.0
    send_mat = jnp.concatenate([send_mat, send_mat], axis=1).astype(BF16)

    def bucketed(value):
        return dot(send_mat, jnp.concatenate(split(value), axis=0)).reshape(n_sp, bk, CELLS)

    spot = iota((n_sp, bk, 128), 1) == iota((n_sp, bk, 128), 2)
    slot_wide = jnp.broadcast_to(slot_col, (rows, 128)).reshape(n_sp, bk, 128)
    slot_lanes = jnp.sum(jnp.where(spot, slot_wide, 0.0), axis=1, keepdims=True)
    slots_out[...] = jnp.broadcast_to(slot_lanes, (n_sp, 8, 128))
    gb[...] = bucketed(guess_ref[0])

    @pl.when(k == 0)
    def _():
        ib[...] = bucketed(init_ref[...])

    linked = nb_ref[...]
    face_no = iota((6, nb), 0)
    run = s + jnp.where(face_no == 4, -1, jnp.where(face_no == 5, 1, 0))
    linked = jnp.where(linked >= 0, linked - run * nb, -1)
    tab_s[0, 0:6] = jnp.concatenate([linked, linked], axis=1)
    kind = class_ref[...]
    tab_s[0, 6:7] = jnp.concatenate([kind, kind], axis=1)
    tab_s[0, 7:8] = jnp.zeros((1, 128), jnp.int32)
    tab_s[1] = tab_s[0]

    sides = jnp.minimum(k, 1) + jnp.minimum(last - k, 1)
    pl.semaphore_wait(barrier, (n_sp - 1) * (1 + sides) + n_tm - 1)

    up_to = (k, lax.rem(s + 1, n_sp))
    down_to = (k, lax.rem(s + n_sp - 1, n_sp))

    def halo_up(slot, source, target):
        return pltpu.make_async_remote_copy(
            src_ref=source, dst_ref=target, send_sem=hs_sem.at[slot, 0],
            recv_sem=hr_sem.at[slot, 0], device_id=up_to, device_id_type=MESH)

    def halo_down(slot, source, target):
        return pltpu.make_async_remote_copy(
            src_ref=source, dst_ref=target, send_sem=hs_sem.at[slot, 1],
            recv_sem=hr_sem.at[slot, 1], device_id=down_to, device_id_type=MESH)

    def planes_message(slot, state, depth, target):
        size = depth * PLANE
        return (halo_up(slot, state.at[pl.ds(8 * PLANE - size, size)], target.at[0]),
                halo_down(slot, state.at[pl.ds(0, size)], target.at[1]))

    def exchange(message):
        up, down = message

        @pl.when(s < n_sp - 1)
        def _():
            up.start()

        @pl.when(s > 0)
        def _():
            down.start()

    def exchanged(message):
        up, down = message

        @pl.when(s > 0)
        def _():
            up.wait_recv()

        @pl.when(s < n_sp - 1)
        def _():
            down.wait_recv()

    def drained(message):
        up, down = message

        @pl.when(s < n_sp - 1)
        def _():
            up.wait_send()

        @pl.when(s > 0)
        def _():
            down.wait_send()

    table_message = (halo_up(0, tab_s.at[0], tab_r.at[0]), halo_down(0, tab_s.at[1], tab_r.at[1]))
    source_message = planes_message(1, src.at[1], 2, srch)

    def first_message(it):
        return planes_message(2 + 3 * it, drv.at[it], 3, e1.at[it])

    def deep_message(it):
        return planes_message(3 + 3 * it, x3a.at[it], 4, e2.at[it])

    def second_message(it):
        return planes_message(4 + 3 * it, x3b.at[it], 2, e4.at[it])

    def spread_copy(buckets, ssem, off, col):
        to = lax.rem(s + off, n_sp)
        return pltpu.make_async_remote_copy(
            src_ref=buckets.at[to], dst_ref=br.at[s], send_sem=ssem.at[off], recv_sem=br_sem.at[s],
            device_id=(col, to), device_id_type=MESH)

    def own_copy(off):
        to = lax.rem(s + off, n_sp)
        return pltpu.make_async_remote_copy(
            src_ref=gb.at[to], dst_ref=gr.at[s], send_sem=gs_sem.at[off],
            recv_sem=gr_sem.at[s], device_id=(k, to), device_id_type=MESH)

    def spread_landed(off):
        origin = lax.rem(s + off, n_sp)
        pltpu.make_async_remote_copy(
            src_ref=gb.at[origin], dst_ref=br.at[origin], send_sem=ps_sem.at[off],
            recv_sem=br_sem.at[origin], device_id=(lax.rem(k + 1, n_tm), origin),
            device_id_type=MESH).wait_recv()

    def own_landed(off):
        origin = lax.rem(s + off, n_sp)
        pltpu.make_async_remote_copy(
            src_ref=gb.at[origin], dst_ref=gr.at[origin],
            send_sem=gs_sem.at[off], recv_sem=gr_sem.at[origin], device_id=(k, origin),
            device_id_type=MESH).wait_recv()

    def slots_copy(off):
        to = lax.rem(s + off, n_sp)
        return pltpu.make_async_remote_copy(
            src_ref=slots_out.at[to], dst_ref=slots_in.at[s], send_sem=so_sem.at[off],
            recv_sem=si_sem.at[s], device_id=(k, to), device_id_type=MESH)

    def slots_landed(off):
        origin = lax.rem(s + off, n_sp)
        pltpu.make_async_remote_copy(
            src_ref=slots_out.at[origin], dst_ref=slots_in.at[origin], send_sem=so_sem.at[off],
            recv_sem=si_sem.at[origin], device_id=(k, origin), device_id_type=MESH).wait_recv()

    for off in range(1, n_sp):
        slots_copy(off).start()
    slots_in[s] = slots_out[s]
    exchange(table_message)

    @pl.when(k == 0)
    def _():
        for off in range(1, n_sp):
            spread_copy(ib, is_sem, off, k).start()
        br[s] = ib[s]

    @pl.when(k < last)
    def _():
        for off in range(n_sp):
            spread_copy(gb, ps_sem, off, lax.rem(k + 1, n_tm)).start()

    gr[s] = gb[s]

    lane = iota((8, 128), 1)
    sub = iota((8, 128), 0)
    left = lane < 64
    half = lane & 64

    def blocks_in_lanes(value):
        return jnp.concatenate([value[:, :CELLS // 2], value[:, CELLS // 2:]], axis=0).T

    for fine in range(2):
        shuffle[0:256] = blocks_in_lanes(source_ref[0, fine])
        for z in range(8):
            src[fine, z * PLANE:(z + 1) * PLANE] = shuffle[pl.ds(z, PLANE, stride=8), :]
    exchange(source_message)

    def make_tables(at, table):
        faces = [jnp.broadcast_to(table[face:face + 1], (8, 128)) for face in range(7)]
        inside = [jnp.maximum(face, 0) for face in faces]
        index = [
            jnp.where(left, inside[0] + 64, lane - 64), jnp.where(left, lane + 64, inside[1]),
            jnp.where(sub == 0, half + inside[2], lane), jnp.where(sub == 7, half + inside[3], lane),
            half + inside[4], half + inside[5],
        ]
        known = [jnp.where(face >= 0, 1.0, 0.0) for face in faces[:6]]
        mask = [
            jnp.where(left, known[0], 1.0), jnp.where(left, 1.0, known[1]),
            jnp.where(sub == 0, known[2], 1.0), jnp.where(sub == 7, known[3], 1.0),
            known[4], known[5],
        ]
        for face in range(6):
            tidx[at, face] = index[face]
            tmask[at, face] = mask[face]
        dif = jnp.zeros((8, 128), F32)
        for cl in range(CLASSES):
            dif = dif + jnp.where(faces[6] == cl, step_ref[:, cl:cl + 1], 0.0)
        tscale[at, 0] = DAMP * dif / (1.0 + 6.0 * dif)
        tscale[at, 1] = DAMP / (1.0 + 6.0 * dif)
        tscale[at, 2] = (1.0 + 6.0 * dif) / DAMP

    make_tables(0, tab_s[0])

    def coarse_of(row):
        high = lax.shift_right_logical(row, 6) * 2 + (lax.shift_right_logical(row, 3) & 1)
        return high * 16 + lax.shift_right_logical(row & 7, 1) * 4 + (lax.shift_right_logical(row, 4) & 3)

    tall = jnp.where(coarse_of(iota((128, COARSE), 0)) == iota((128, COARSE), 1), 1.0, 0.0).astype(BF16)
    wide = jnp.where(coarse_of(iota((COARSE, 128), 1)) == iota((COARSE, 128), 0), 0.125, 0.0).astype(BF16)
    for given, made in ((inv_ref, mi), (cstep_ref, ms)):
        for part, piece in enumerate(split(given[...])):
            broad = dot(piece, wide).astype(BF16)
            for cl in range(CLASSES):
                made[cl * 128:(cl + 1) * 128, part * 128:(part + 1) * 128] = dot(
                    tall, broad[cl * COARSE:(cl + 1) * COARSE]).astype(BF16)

    def classes(coarse, mat):
        n = coarse.shape[0]
        high = coarse.astype(BF16).astype(F32)
        low = coarse - high
        here = tiled(left, n)
        turned = turn(high)
        right = jnp.concatenate([
            jnp.where(here, high, turn(low)), jnp.where(here, turned, low),
            jnp.where(here, high, 0.0), jnp.where(here, turned, 0.0)], axis=0).astype(BF16)
        product = dot(mat[...], right)
        kinds = jnp.broadcast_to(tab_s[0, 6:7], (128, 128))
        picked = jnp.where(kinds == 0, product[:128], 0.0)
        for cl in range(1, CLASSES):
            picked = jnp.where(kinds == cl, product[cl * 128:(cl + 1) * 128], picked)
        picked = picked + turn(picked)
        return jnp.where(here, picked[:64], picked[64:])

    def restrict(value):
        pairs = value.reshape(4, 2, 2, 2, 8, 128)
        pairs = pairs[:, 0] + pairs[:, 1]
        return (pairs[:, :, 0] + pairs[:, :, 1]).reshape(64, 128)

    def prolong(coarse):
        return jnp.broadcast_to(
            coarse.reshape(4, 1, 2, 1, 8, 128), (4, 2, 2, 2, 8, 128)).reshape(256, 128)

    def ghost(plane, face, at):
        return jnp.where(tiled(tmask[at, face], PLANE) > 0.0, lanes_from(plane, tidx[at, face]), 0.0)

    def picked_from(value, face, at):
        return jnp.where(
            tiled(tmask[at, face], value.shape[0]) > 0.0, lanes_from(value, tidx[at, face]), 0.0)

    def beside_xy(value, at):
        size = value.shape[0]
        n = size // PLANE
        cube = value.reshape(n, 4, 8, 128)
        low = picked_from(cube[:, 3].reshape(n * 8, 128), 0, at).reshape(n, 1, 8, 128)
        high = picked_from(cube[:, 0].reshape(n * 8, 128), 1, at).reshape(n, 1, 8, 128)
        total = (jnp.concatenate([low, cube[:, :3]], axis=1)
                 + jnp.concatenate([cube[:, 1:], high], axis=1)).reshape(size, 128)
        total = total + picked_from(along_y(value, 1), 2, at)
        return total + picked_from(along_y(value, -1), 3, at)

    def inner(value):
        zero = jnp.zeros((PLANE, 128), F32)
        total = beside_xy(value, 0)
        total = total + jnp.concatenate([zero, value[:-PLANE]], axis=0)
        return total + jnp.concatenate([value[PLANE:], zero], axis=0)

    def ended(total, below, above):
        return jnp.concatenate([
            total[:PLANE] + ghost(below, 4, 0), total[PLANE:-PLANE],
            total[-PLANE:] + ghost(above, 5, 0)], axis=0)

    def scaled(which, at, size):
        return tiled(tscale[at, which], size)

    def relax(value, driven, total, at):
        return (1.0 - DAMP) * value + driven + scaled(0, at, value.shape[0]) * total

    def slab_below(slab, driven, own):
        cross = ghost(own[:PLANE], 5, 1)
        near = slab[PLANE:]
        upper = jnp.concatenate([slab[2 * PLANE:], cross], axis=0) if slab.shape[0] > 2 * PLANE else cross
        return relax(near, driven, beside_xy(near, 1) + slab[:-PLANE] + upper, 1)

    def slab_above(slab, driven, own):
        cross = ghost(own[-PLANE:], 4, 2)
        near = slab[:-PLANE]
        lower = jnp.concatenate([cross, slab[:-2 * PLANE]], axis=0) if slab.shape[0] > 2 * PLANE else cross
        return relax(near, driven, beside_xy(near, 2) + slab[PLANE:] + lower, 2)

    def corrected(driven, total, below, above):
        x2 = relax(driven, driven, ended(total, below[-PLANE:], above[:PLANE]), 0)
        below2 = slab_below(below, below[PLANE:], driven)
        above2 = slab_above(above, above[:-PLANE], driven)
        total = ended(inner(x2), below2[-PLANE:], above2[:PLANE])
        rest = driven - DAMP * x2 + scaled(0, 0, 256) * total
        return x2 + prolong(classes(scaled(2, 0, 64) * restrict(rest), mi))

    def swept(x3, driven, total, below, below_d, above, above_d):
        x4 = relax(x3, driven, ended(total, below[-PLANE:], above[:PLANE]), 0)
        below4 = slab_below(below, below_d, x3)
        above4 = slab_above(above, above_d, x3)
        x5 = relax(x4, driven, ended(inner(x4), below4[-PLANE:], above4[:PLANE]), 0)
        return x4, x5, below4, above4

    exchanged(table_message)
    for side in range(2):
        reached = (s > 0) if side == 0 else (s < n_sp - 1)
        make_tables(1 + side, jnp.where(reached, tab_r[side], -1))

    for off in range(1, n_sp):
        slots_landed(off)
    slots = jnp.sum(jnp.where(spot, slots_in[:, :1], 0.0), axis=2, keepdims=True)
    slots = jnp.broadcast_to(slots, (n_sp, bk, 128)).reshape(rows, 128)
    hit = slots == (iota((rows, 128), 1) & 63).astype(F32)
    place = jnp.sum(jnp.where(hit, iota((rows, 128), 0).astype(F32), 0.0), axis=0, keepdims=True)
    place = jnp.broadcast_to(place, (8, 128)).astype(jnp.int32)

    def settle(given, put):
        tiles = rows // 128
        for tile in range(tiles):
            shuffle[tile * CELLS:(tile + 1) * CELLS] = given[tile * 128:(tile + 1) * 128].T
        for z in range(8):
            plane = None
            for tile in range(tiles):
                both = shuffle[pl.ds(tile * CELLS + z, 64, stride=8), :]
                both = lanes_from(both, place & 127)
                both = jnp.where(tiled(left, PLANE), both[:PLANE], both[PLANE:])
                chosen_tile = tiled(lax.shift_right_logical(place, 7), PLANE) == tile
                plane = both if plane is None else jnp.where(chosen_tile, both, plane)
            put(z, plane)

    for off in range(1, n_sp):
        spread_landed(off)

    @pl.when(k > 0)
    def _():
        spread_landed(0)

    def put_start(z, plane):
        bs[0, z * PLANE:(z + 1) * PLANE] = plane

    settle(br[...].reshape(rows, CELLS), put_start)

    def back_copy():
        return pltpu.make_async_remote_copy(
            src_ref=bs.at[0], dst_ref=st.at[0], send_sem=bk_sem.at[0], recv_sem=bq_sem.at[0],
            device_id=(lax.rem(k + n_tm - 1, n_tm), s), device_id_type=MESH)

    def hand_copy(it):
        return pltpu.make_async_remote_copy(
            src_ref=hsrc.at[it], dst_ref=hand.at[it], send_sem=ts_sem.at[it], recv_sem=tr_sem.at[it],
            device_id=(lax.rem(k + 1, n_tm), s), device_id_type=MESH)

    def coarse_copy(it, off):
        return pltpu.make_async_remote_copy(
            src_ref=cs.at[it], dst_ref=cr.at[it, k], send_sem=cs_sem.at[it, off],
            recv_sem=cr_sem.at[it, k], device_id=(lax.rem(k + off, n_tm), s), device_id_type=MESH)

    def coarse_landed(it, origin):
        pltpu.make_async_remote_copy(
            src_ref=cs.at[it], dst_ref=cr.at[it, origin], send_sem=cs_sem.at[it, 0],
            recv_sem=cr_sem.at[it, origin], device_id=(lax.rem(k + 1, n_tm), s),
            device_id_type=MESH).wait_recv()

    for it in range(ITERS):
        drv[it] = scaled(1, 0, 256) * (bs[it] + src[0])
        exchange(first_message(it))
        if it == 0:
            @pl.when(k > 0)
            def _():
                back_copy().start()
            exchanged(source_message)
        driven = drv[it]
        total = inner(driven)
        exchanged(first_message(it))
        below_d, above_d = e1[it, 0], e1[it, 1]
        x3a[it] = corrected(driven, total, below_d[PLANE:], above_d[:-PLANE])
        exchange(deep_message(it))
        if it == 0:
            @pl.when(k == last)
            def _():
                for off in range(1, n_sp):
                    own_copy(off).start()
        x3 = x3a[it]
        total = inner(x3)
        exchanged(deep_message(it))
        below, above = e2[it, 0], e2[it, 1]
        x4, x5, below4, above4 = swept(x3, drv[it], total, below, e1[it, 0], above, e1[it, 1])
        below5 = slab_below(below4, e1[it, 0, PLANE:], x4)
        above5 = slab_above(above4, e1[it, 1, :-PLANE], x4)
        xf[...] = x5
        driven = scaled(1, 0, 256) * (x5 + src[1])
        below_d = scaled(1, 1, 2 * PLANE) * (below5 + srch[0])
        above_d = scaled(1, 2, 2 * PLANE) * (above5 + srch[1])
        drv2[...] = driven
        x3b[it] = corrected(driven, inner(driven), below_d, above_d)
        exchange(second_message(it))
        total = inner(x3b[it])
        if it == 0:
            @pl.when(k < last)
            def _():
                back_copy().wait_recv()

            @pl.when(k == last)
            def _():
                for off in range(1, n_sp):
                    own_landed(off)

                def put_guess(z, plane):
                    st[0, z * PLANE:(z + 1) * PLANE] = plane

                settle(gr[...].reshape(rows, CELLS), put_guess)
        if it == ITERS - 1:
            for z in range(8):
                shuffle[pl.ds(z, PLANE, stride=8), :] = xf[z * PLANE:(z + 1) * PLANE]
            flat = shuffle[0:256].T
            f_ref[0] = jnp.concatenate([flat[:64], flat[64:]], axis=1)
        exchanged(second_message(it))
        _, x5, _, _ = swept(
            x3b[it], drv2[...], total, e4[it, 0], below_d[PLANE:], e4[it, 1], above_d[:-PLANE])
        residual = x5 - st[it]
        cs[it] = restrict(residual)
        for off in range(1, n_tm):
            @pl.when(k + off < n_tm)
            def _():
                coarse_copy(it, off).start()
        if it < ITERS - 1:
            hsrc[it] = x5

            @pl.when(k < last)
            def _():
                hand_copy(it).start()

        zs[...] = jnp.zeros_like(zs)
        ps[...] = jnp.zeros_like(ps)
        for j in range(n_tm - 1):
            @pl.when(j < k)
            def _():
                coarse_landed(it, j)
                if j > 0:
                    pushed = classes(zs[...], ms)
                    ps[...] = pushed
                    zs[...] = 4.0 * pushed + cr[it, j]
                else:
                    zs[...] = cr[it, j]
        if it < ITERS - 1:
            @pl.when(k > 0)
            def _():
                hand_copy(it).wait_recv()
                bs[it + 1] = hand[it] + prolong(ps[...])

            @pl.when(k == 0)
            def _():
                bs[it + 1] = bs[it]
        st[it + 1] = st[it] + (prolong(classes(zs[...], ms)) + residual)

    for z in range(8):
        shuffle[pl.ds(z, PLANE, stride=8), :] = st[ITERS, z * PLANE:(z + 1) * PLANE]
    flat = shuffle[0:256].T
    c_ref[0] = jnp.concatenate([flat[:64], flat[64:]], axis=1)

    for off in range(1, n_sp):
        slots_copy(off).wait_send()

    @pl.when(k == last)
    def _():
        for off in range(1, n_sp):
            own_copy(off).wait_send()

    @pl.when(k > 0)
    def _():
        back_copy().wait_send()

    @pl.when(k == 0)
    def _():
        for off in range(1, n_sp):
            spread_copy(ib, is_sem, off, k).wait_send()

    @pl.when(k < last)
    def _():
        for off in range(n_sp):
            spread_copy(gb, ps_sem, off, lax.rem(k + 1, n_tm)).wait_send()

    drained(table_message)
    drained(source_message)
    for it in range(ITERS):
        drained(first_message(it))
        drained(deep_message(it))
        drained(second_message(it))
        if it < ITERS - 1:
            @pl.when(k < last)
            def _():
                hand_copy(it).wait_send()
        for off in range(1, n_tm):
            @pl.when(k + off < n_tm)
            def _():
                coarse_copy(it, off).wait_send()


def solution(mesh):
    n_tm, n_sp = mesh.shape["tm"], mesh.shape["space"]

    def body(init_state, guess, source, remap, neighbors, block_class, step_number, inverse, cstep):
        nb = init_state.shape[0]
        bk = -(-(2 * nb // n_sp) // 8) * 8
        tiles = n_sp * bk // 128
        slots = 2 + 3 * ITERS
        dma = pltpu.SemaphoreType.DMA
        out = jax.ShapeDtypeStruct((1, nb, CELLS), F32)
        full = 8 * PLANE

        def vmem(*shape, dtype=F32):
            return pltpu.VMEM(shape, dtype)

        return pl.pallas_call(
            functools.partial(kernel, n_tm, n_sp, bk),
            name="mgrit",
            out_shape=(out, out),
            in_specs=[pl.BlockSpec(memory_space=pltpu.VMEM)] * 9,
            out_specs=[pl.BlockSpec(memory_space=pltpu.VMEM)] * 2,
            scratch_shapes=[
                vmem(n_sp, bk, CELLS), vmem(n_sp, bk, CELLS), vmem(n_sp, bk, CELLS), vmem(n_sp, bk, CELLS),
                vmem(2, 8, 128, dtype=jnp.int32), vmem(2, 8, 128, dtype=jnp.int32),
                vmem(3, 6, 8, 128, dtype=jnp.int32), vmem(3, 6, 8, 128), vmem(3, 3, 8, 128),
                vmem(2, full, 128), vmem(2, 2 * PLANE, 128), vmem(tiles * CELLS, 128),
                vmem(ITERS, full, 128), vmem(ITERS, full, 128), vmem(full, 128), vmem(ITERS, full, 128), vmem(ITERS, full, 128),
                vmem(ITERS, 2, 3 * PLANE, 128), vmem(ITERS, 2, 4 * PLANE, 128), vmem(ITERS, 2, 2 * PLANE, 128),
                vmem(ITERS + 1, full, 128), vmem(full, 128),
                vmem(ITERS, full, 128), vmem(ITERS, full, 128),
                vmem(ITERS, 64, 128), vmem(ITERS, n_tm, 64, 128), vmem(64, 128), vmem(64, 128),
                vmem(CLASSES * 128, 256, dtype=BF16), vmem(CLASSES * 128, 256, dtype=BF16),
                vmem(n_sp, 8, 128), vmem(n_sp, 8, 128),
                dma((n_sp,)), dma((n_sp,)),
                dma((n_sp,)), dma((n_sp,)), dma((n_sp,)), dma((n_sp,)), dma((n_sp,)),
                dma((slots, 2)), dma((slots, 2)),
                dma((ITERS,)), dma((ITERS,)), dma((1,)), dma((1,)),
                dma((ITERS, n_tm)), dma((ITERS, n_tm)),
            ],
            compiler_params=pltpu.CompilerParams(collective_id=0, has_side_effects=True),
        )(
            init_state, guess, source, remap.reshape(1, nb), neighbors.T, block_class.reshape(1, nb),
            step_number.reshape(1, CLASSES), inverse.reshape(CLASSES * COARSE, COARSE),
            cstep.reshape(CLASSES * COARSE, COARSE),
        )

    placed = (
        P("space", None), P("tm", "space", None), P("tm", None, "space", None), P("space"),
        P("space", None), P("space"), P(), P(), P(),
    )
    return jax.shard_map(
        body, mesh=mesh, in_specs=placed,
        out_specs=(P("tm", "space", None), P("tm", "space", None)), check_vma=False,
    )
```

```python
import functools

import jax
import jax.numpy as jnp
from jax import lax
from jax.experimental import pallas as pl
from jax.experimental.pallas import tpu as pltpu
from jax.sharding import PartitionSpec as P

CELLS = 512
COARSE = 64
CLASSES = 4
ITERS = 2
DAMP = 0.8
PLANE = 32
MESH = pl.DeviceIdType.MESH
F32 = jnp.float32
BF16 = jnp.bfloat16


def split(value):
    high = value.astype(BF16)
    return high, (value - high.astype(F32)).astype(BF16)


def dot(left, right):
    return jnp.dot(left, right, preferred_element_type=F32)


def iota(shape, dim):
    return lax.broadcasted_iota(jnp.int32, shape, dim)


def turn(value):
    return pltpu.roll(value, 64, 1)


def along_y(value, shift):
    rows = value.shape[0]
    return pltpu.roll(value.reshape(rows // 8, 8, 128), shift % 8, 1).reshape(rows, 128)


def tiled(table, rows):
    return jnp.broadcast_to(table[None], (rows // 8, 8, 128)).reshape(rows, 128)


def lanes_from(value, index):
    return jnp.take_along_axis(
        value, tiled(index, value.shape[0]), axis=1, mode="promise_in_bounds")


def partner(s, off, n):
    if n & (n - 1):
        return lax.rem(s + off, n)
    to = s
    for bit in range(n.bit_length() - 1):
        if off >> bit & 1:
            to = to + (1 - 2 * lax.rem(lax.div(s, 1 << bit), 2)) * (1 << bit)
    return to


def kernel(
    n_tm, n_sp, bk,
    init_hbm, guess_hbm, source_hbm, remap_hbm, nb_hbm, class_hbm, step_hbm, inv_hbm, cstep_hbm,
    c_ref, f_ref,
    init_ref, guess_ref, source_ref, remap_ref, nb_ref, class_ref, step_ref, inv_ref, cstep_ref, c_out, f_out,
    gb, br, gr, tab_s, tab_r, tidx, tmask, tscale, src, srch, shuffle,
    bs, drv, drv2, x3a, x3b, e1, e2, e4, st, xf, hsrc, hand, cs, cr, mi, ms,
    slots_out, slots_in, in_sem, out_sem, so_sem, si_sem,
    gs_sem, gr_sem, ps_sem, br_sem, hs_sem, hr_sem, ts_sem, tr_sem, bk_sem, bq_sem, cs_sem, cr_sem,
):
    k = lax.axis_index("tm")
    s = lax.axis_index("space")
    nb = init_hbm.shape[0]
    rows = n_sp * bk
    bits = nb.bit_length() - 1
    last = n_tm - 1

    after, before = lax.rem(k + 1, n_tm), lax.rem(k + last, n_tm)

    barrier = pltpu.get_barrier_semaphore()

    def greet(tm, space):
        pl.semaphore_signal(barrier, inc=1, device_id=(tm, space), device_id_type=MESH)

    for off in range(n_sp):
        greet(before, partner(s, off, n_sp))

    @pl.when(s > 0)
    def _():
        greet(k, s - 1)

    @pl.when(s < n_sp - 1)
    def _():
        greet(k, s + 1)

    @pl.when(k < last)
    def _():
        greet(k + 1, s)

    for off in range(2, n_tm):
        @pl.when(k >= off)
        def _():
            greet(k - off, s)

    @pl.when(k == last)
    def _():
        for off in range(1, n_sp):
            greet(k, partner(s, off, n_sp))

    loads = [
        pltpu.make_async_copy(given, kept, in_sem.at[at]) for at, (given, kept) in enumerate((
            (remap_hbm, remap_ref), (guess_hbm, guess_ref), (init_hbm, init_ref), (nb_hbm, nb_ref),
            (class_hbm, class_ref), (step_hbm, step_ref), (source_hbm, source_ref), (inv_hbm, inv_ref),
            (cstep_hbm, cstep_ref)))]
    for load in loads:
        load.start()
    loads[0].wait()

    eye = iota((nb, nb), 0) == iota((nb, nb), 1)

    def column(row):
        return jnp.sum(jnp.where(eye, row, 0.0), axis=1, keepdims=True)

    remap_row = remap_ref[...]
    target_row = lax.shift_right_logical(remap_row, bits)
    slot_row = (remap_row - lax.shift_left(target_row, bits)).astype(F32)
    target_f = target_row.astype(F32)
    same = (column(target_f) == target_f) & (iota((nb, nb), 0) < iota((nb, nb), 1))
    pos_row = jnp.sum(jnp.where(same, 1.0, 0.0), axis=0, keepdims=True)
    send_row = target_f * float(bk) + pos_row
    chosen = iota((rows, nb), 0).astype(F32) == send_row
    send_mat = jnp.where(chosen, 1.0, 0.0)
    slot_col = jnp.sum(jnp.where(chosen, slot_row + 1.0, 0.0), axis=1, keepdims=True) - 1.0
    send_mat = jnp.concatenate([send_mat, send_mat], axis=1).astype(BF16)

    def bucketed(value):
        return dot(send_mat, jnp.concatenate(split(value), axis=0)).reshape(n_sp, bk, CELLS)

    spot = iota((n_sp, bk, 128), 1) == iota((n_sp, bk, 128), 2)
    slot_wide = jnp.broadcast_to(slot_col, (rows, 128)).reshape(n_sp, bk, 128)
    slot_lanes = jnp.sum(jnp.where(spot, slot_wide, 0.0), axis=1, keepdims=True)
    slots_out[...] = jnp.broadcast_to(slot_lanes, (n_sp, 8, 128))
    loads[1].wait()
    loads[2].wait()
    gb[0] = bucketed(guess_ref[0])

    @pl.when(k == last)
    def _():
        gb[1] = bucketed(init_ref[...])

    for load in loads[3:6]:
        load.wait()

    linked = nb_ref[...]
    face_no = iota((6, nb), 0)
    run = s + jnp.where(face_no == 4, -1, jnp.where(face_no == 5, 1, 0))
    linked = jnp.where(linked >= 0, linked - run * nb, -1)
    tab_s[0, 0:6] = jnp.concatenate([linked, linked], axis=1)
    kind = class_ref[...]
    tab_s[0, 6:7] = jnp.concatenate([kind, kind], axis=1)
    tab_s[0, 7:8] = jnp.zeros((1, 128), jnp.int32)
    tab_s[1] = tab_s[0]

    greeted = (n_sp + jnp.minimum(s, 1) + jnp.minimum(n_sp - 1 - s, 1) + jnp.minimum(k, 1)
               + jnp.maximum(last - 1 - k, 0) + jnp.maximum(k - last + 1, 0) * (n_sp - 1))
    pl.semaphore_wait(barrier, greeted)

    up_to = (k, lax.rem(s + 1, n_sp))
    down_to = (k, lax.rem(s + n_sp - 1, n_sp))

    def halo_up(slot, source, target):
        return pltpu.make_async_remote_copy(
            src_ref=source, dst_ref=target, send_sem=hs_sem.at[slot, 0],
            recv_sem=hr_sem.at[slot, 0], device_id=up_to, device_id_type=MESH)

    def halo_down(slot, source, target):
        return pltpu.make_async_remote_copy(
            src_ref=source, dst_ref=target, send_sem=hs_sem.at[slot, 1],
            recv_sem=hr_sem.at[slot, 1], device_id=down_to, device_id_type=MESH)

    def planes_message(slot, state, depth, target):
        size = depth * PLANE
        return (halo_up(slot, state.at[pl.ds(8 * PLANE - size, size)], target.at[0]),
                halo_down(slot, state.at[pl.ds(0, size)], target.at[1]))

    def exchange(message):
        up, down = message

        @pl.when(s < n_sp - 1)
        def _():
            up.start()

        @pl.when(s > 0)
        def _():
            down.start()

    def exchanged(message):
        up, down = message

        @pl.when(s > 0)
        def _():
            up.wait_recv()

        @pl.when(s < n_sp - 1)
        def _():
            down.wait_recv()

    def drained(message):
        up, down = message

        @pl.when(s < n_sp - 1)
        def _():
            up.wait_send()

        @pl.when(s > 0)
        def _():
            down.wait_send()

    table_message = (halo_up(0, tab_s.at[0], tab_r.at[0]), halo_down(0, tab_s.at[1], tab_r.at[1]))
    source_message = planes_message(1, src.at[1], 2, srch)

    def first_message(it):
        return planes_message(2 + 3 * it, drv.at[it], 3, e1.at[it])

    def deep_message(it):
        return planes_message(3 + 3 * it, x3a.at[it], 4, e2.at[it])

    def second_message(it):
        return planes_message(4 + 3 * it, x3b.at[it], 2, e4.at[it])

    which = jnp.maximum(k - last + 1, 0)

    def spread_copy(off):
        to = partner(s, off, n_sp)
        return pltpu.make_async_remote_copy(
            src_ref=gb.at[which, to], dst_ref=br.at[s], send_sem=ps_sem.at[off], recv_sem=br_sem.at[s],
            device_id=(after, to), device_id_type=MESH)

    def spread_landed(off):
        origin = partner(s, off, n_sp)
        pltpu.make_async_remote_copy(
            src_ref=gb.at[0, origin], dst_ref=br.at[origin], send_sem=ps_sem.at[off],
            recv_sem=br_sem.at[origin], device_id=(after, origin), device_id_type=MESH).wait_recv()

    def own_copy(off):
        to = partner(s, off, n_sp)
        return pltpu.make_async_remote_copy(
            src_ref=gb.at[0, to], dst_ref=gr.at[s], send_sem=gs_sem.at[off],
            recv_sem=gr_sem.at[s], device_id=(k, to), device_id_type=MESH)

    def own_landed(off):
        origin = partner(s, off, n_sp)
        pltpu.make_async_remote_copy(
            src_ref=gb.at[0, origin], dst_ref=gr.at[origin],
            send_sem=gs_sem.at[off], recv_sem=gr_sem.at[origin], device_id=(k, origin),
            device_id_type=MESH).wait_recv()

    def slots_copy(off):
        to = partner(s, off, n_sp)
        return pltpu.make_async_remote_copy(
            src_ref=slots_out.at[to], dst_ref=slots_in.at[s], send_sem=so_sem.at[off],
            recv_sem=si_sem.at[s], device_id=(after, to), device_id_type=MESH)

    def slots_landed(off):
        origin = partner(s, off, n_sp)
        pltpu.make_async_remote_copy(
            src_ref=slots_out.at[origin], dst_ref=slots_in.at[origin], send_sem=so_sem.at[off],
            recv_sem=si_sem.at[origin], device_id=(after, origin), device_id_type=MESH).wait_recv()

    for off in reversed(range(n_sp)):
        spread_copy(off).start()
        if off == n_sp // 2:
            for small in reversed(range(n_sp)):
                slots_copy(small).start()
            exchange(table_message)
    gr[s] = gb[0, s]

    lane = iota((8, 128), 1)
    sub = iota((8, 128), 0)
    left = lane < 64
    half = lane & 64

    def blocks_in_lanes(value):
        return jnp.concatenate([value[:, :CELLS // 2], value[:, CELLS // 2:]], axis=0).T

    for load in loads[6:]:
        load.wait()
    for fine in range(2):
        shuffle[0:256] = blocks_in_lanes(source_ref[0, fine])
        for z in range(8):
            src[fine, z * PLANE:(z + 1) * PLANE] = shuffle[pl.ds(z, PLANE, stride=8), :]

    def make_tables(at, table):
        faces = [jnp.broadcast_to(table[face:face + 1], (8, 128)) for face in range(7)]
        inside = [jnp.maximum(face, 0) for face in faces]
        index = [
            jnp.where(left, inside[0] + 64, lane - 64), jnp.where(left, lane + 64, inside[1]),
            jnp.where(sub == 0, half + inside[2], lane), jnp.where(sub == 7, half + inside[3], lane),
            half + inside[4], half + inside[5],
        ]
        known = [jnp.where(face >= 0, 1.0, 0.0) for face in faces[:6]]
        mask = [
            jnp.where(left, known[0], 1.0), jnp.where(left, 1.0, known[1]),
            jnp.where(sub == 0, known[2], 1.0), jnp.where(sub == 7, known[3], 1.0),
            known[4], known[5],
        ]
        for face in range(6):
            tidx[at, face] = index[face]
            tmask[at, face] = mask[face]
        dif = jnp.zeros((8, 128), F32)
        for cl in range(CLASSES):
            dif = dif + jnp.where(faces[6] == cl, step_ref[:, cl:cl + 1], 0.0)
        tscale[at, 0] = DAMP * dif / (1.0 + 6.0 * dif)
        tscale[at, 1] = DAMP / (1.0 + 6.0 * dif)
        tscale[at, 2] = (1.0 + 6.0 * dif) / DAMP

    make_tables(0, tab_s[0])

    def coarse_of(row):
        high = lax.shift_right_logical(row, 5) * 2 + (row & 1)
        return high * 16 + (lax.shift_right_logical(row, 1) & 3) * 4 + (lax.shift_right_logical(row, 3) & 3)

    size = CLASSES * COARSE
    in_class = (lax.shift_right_logical(iota((size, size), 0), 6)
                == lax.shift_right_logical(iota((size, size), 1), 6))
    tall = jnp.where(in_class & (coarse_of(iota((size, size), 0) & 63) == (iota((size, size), 1) & 63)),
                     1.0, 0.0).astype(BF16)
    wide = jnp.where(coarse_of(iota((COARSE, COARSE), 1)) == iota((COARSE, COARSE), 0), 0.125, 0.0).astype(BF16)

    def made(given):
        parts = [dot(tall, dot(piece, wide).astype(BF16)).astype(BF16) for piece in split(given)]
        return jnp.concatenate(parts, axis=1)

    mi[...] = made(inv_ref[...])
    power = cstep_ref[...]
    step_h, step_l = split(jnp.where(in_class, jnp.concatenate([power] * CLASSES, axis=1), 0.0))
    step_all = jnp.concatenate([step_h, step_h, step_l], axis=1)
    for d in range(last):
        if d > 0:
            power_h, power_l = split(power)
            power = dot(step_all, jnp.concatenate([power_h, power_l, power_h], axis=0))
        ms[:, d * 128:(d + 1) * 128] = made(power)

    def operands(coarse):
        high = coarse.astype(BF16).astype(F32)
        low = coarse - high
        here = tiled(left, PLANE)
        turned = turn(high)
        return jnp.concatenate([
            jnp.where(here, high, turn(low)), jnp.where(here, turned, low),
            jnp.where(here, high, 0.0), jnp.where(here, turned, 0.0)], axis=0).astype(BF16)

    def classes(mat, right):
        product = dot(mat, right)
        kinds = jnp.broadcast_to(tab_s[0, 6:7], (COARSE, 128))
        picked = jnp.where(kinds == 0, product[:COARSE], 0.0)
        for cl in range(1, CLASSES):
            picked = jnp.where(kinds == cl, product[cl * COARSE:(cl + 1) * COARSE], picked)
        picked = picked + turn(picked)
        return jnp.where(tiled(left, PLANE), picked[:PLANE], picked[PLANE:])

    even = (sub & 1) == 0

    def restrict(value):
        pairs = value.reshape(4, 2, 2, 2, 8, 128)
        pairs = pairs[:, 0] + pairs[:, 1]
        pairs = pairs[:, :, 0] + pairs[:, :, 1]
        first = pairs[:, 0].reshape(PLANE, 128)
        second = pairs[:, 1].reshape(PLANE, 128)
        return jnp.where(tiled(even, PLANE), first + along_y(first, -1), second + along_y(second, 1))

    def prolong(coarse):
        here = tiled(even, PLANE)
        first = jnp.where(here, coarse, along_y(coarse, 1)).reshape(4, 1, 1, 1, 8, 128)
        second = jnp.where(here, along_y(coarse, -1), coarse).reshape(4, 1, 1, 1, 8, 128)
        both = jnp.concatenate([first, second], axis=2)
        return jnp.broadcast_to(both, (4, 2, 2, 2, 8, 128)).reshape(256, 128)

    def ghost(plane, face, at):
        return jnp.where(tiled(tmask[at, face], PLANE) > 0.0, lanes_from(plane, tidx[at, face]), 0.0)

    def picked_from(value, face, at):
        return jnp.where(
            tiled(tmask[at, face], value.shape[0]) > 0.0, lanes_from(value, tidx[at, face]), 0.0)

    def beside_xy(value, at):
        size = value.shape[0]
        n = size // PLANE
        cube = value.reshape(n, 4, 8, 128)
        low = picked_from(cube[:, 3].reshape(n * 8, 128), 0, at).reshape(n, 1, 8, 128)
        high = picked_from(cube[:, 0].reshape(n * 8, 128), 1, at).reshape(n, 1, 8, 128)
        total = (jnp.concatenate([low, cube[:, :3]], axis=1)
                 + jnp.concatenate([cube[:, 1:], high], axis=1)).reshape(size, 128)
        total = total + picked_from(along_y(value, 1), 2, at)
        return total + picked_from(along_y(value, -1), 3, at)

    def inner(value):
        zero = jnp.zeros((PLANE, 128), F32)
        total = beside_xy(value, 0)
        total = total + jnp.concatenate([zero, value[:-PLANE]], axis=0)
        return total + jnp.concatenate([value[PLANE:], zero], axis=0)

    def ended(total, below, above):
        return jnp.concatenate([
            total[:PLANE] + ghost(below, 4, 0), total[PLANE:-PLANE],
            total[-PLANE:] + ghost(above, 5, 0)], axis=0)

    def scaled(which, at, size):
        return tiled(tscale[at, which], size)

    def relax(value, driven, total, at):
        return (1.0 - DAMP) * value + driven + scaled(0, at, value.shape[0]) * total

    def slab_below(slab, driven, own):
        cross = ghost(own[:PLANE], 5, 1)
        near = slab[PLANE:]
        upper = jnp.concatenate([slab[2 * PLANE:], cross], axis=0) if slab.shape[0] > 2 * PLANE else cross
        return relax(near, driven, beside_xy(near, 1) + slab[:-PLANE] + upper, 1)

    def slab_above(slab, driven, own):
        cross = ghost(own[-PLANE:], 4, 2)
        near = slab[:-PLANE]
        lower = jnp.concatenate([cross, slab[:-2 * PLANE]], axis=0) if slab.shape[0] > 2 * PLANE else cross
        return relax(near, driven, beside_xy(near, 2) + slab[PLANE:] + lower, 2)

    def corrected(driven, total, below, above):
        x2 = relax(driven, driven, ended(total, below[-PLANE:], above[:PLANE]), 0)
        below2 = slab_below(below, below[PLANE:], driven)
        above2 = slab_above(above, above[:-PLANE], driven)
        total = ended(inner(x2), below2[-PLANE:], above2[:PLANE])
        rest = driven - DAMP * x2 + scaled(0, 0, 256) * total
        return x2 + prolong(classes(mi[...], operands(scaled(2, 0, PLANE) * restrict(rest))))

    def swept(x3, driven, total, below, below_d, above, above_d):
        x4 = relax(x3, driven, ended(total, below[-PLANE:], above[:PLANE]), 0)
        below4 = slab_below(below, below_d, x3)
        above4 = slab_above(above, above_d, x3)
        x5 = relax(x4, driven, ended(inner(x4), below4[-PLANE:], above4[:PLANE]), 0)
        return x4, x5, below4, above4

    exchanged(table_message)
    for side in range(2):
        reached = (s > 0) if side == 0 else (s < n_sp - 1)
        make_tables(1 + side, jnp.where(reached, tab_r[side], -1))

    for off in range(n_sp):
        slots_landed(off)
    slots = jnp.sum(jnp.where(spot, slots_in[:, :1], 0.0), axis=2, keepdims=True)
    slots = jnp.broadcast_to(slots, (n_sp, bk, 128)).reshape(rows, 128)
    hit = slots == (iota((rows, 128), 1) & 63).astype(F32)
    place = jnp.sum(jnp.where(hit, iota((rows, 128), 0).astype(F32), 0.0), axis=0, keepdims=True)
    place = jnp.broadcast_to(place, (8, 128)).astype(jnp.int32)

    def settle(given, put):
        tiles = rows // 128
        for tile in range(tiles):
            shuffle[tile * CELLS:(tile + 1) * CELLS] = given[tile * 128:(tile + 1) * 128].T
        for z in range(8):
            plane = None
            for tile in range(tiles):
                both = shuffle[pl.ds(tile * CELLS + z, 64, stride=8), :]
                both = lanes_from(both, place & 127)
                both = jnp.where(tiled(left, PLANE), both[:PLANE], both[PLANE:])
                chosen_tile = tiled(lax.shift_right_logical(place, 7), PLANE) == tile
                plane = both if plane is None else jnp.where(chosen_tile, both, plane)
            put(z, plane)

    for off in range(n_sp):
        spread_landed(off)

    def put_start(z, plane):
        bs[z * PLANE:(z + 1) * PLANE] = plane

    settle(br[...].reshape(rows, CELLS), put_start)

    def back_copy():
        return pltpu.make_async_remote_copy(
            src_ref=bs, dst_ref=st.at[0], send_sem=bk_sem.at[0], recv_sem=bq_sem.at[0],
            device_id=(before, s), device_id_type=MESH)

    ends = ((0, 3 * PLANE), (5 * PLANE, 3 * PLANE))
    middle = ((3 * PLANE, 2 * PLANE),)

    def hand_copy(at):
        first, count = (ends + middle)[at]
        return pltpu.make_async_remote_copy(
            src_ref=hsrc.at[pl.ds(first, count)], dst_ref=hand.at[pl.ds(first, count)],
            send_sem=ts_sem.at[at], recv_sem=tr_sem.at[at], device_id=(after, s), device_id_type=MESH)

    def coarse_copy(it, off):
        return pltpu.make_async_remote_copy(
            src_ref=cs.at[it], dst_ref=cr.at[it, off - 1], send_sem=cs_sem.at[it, off - 1],
            recv_sem=cr_sem.at[it, off - 1], device_id=(lax.rem(k + off, n_tm), s), device_id_type=MESH)

    def coarse_landed(it):
        rights = []
        for off in range(1, n_tm):
            @pl.when(k >= off)
            def _():
                coarse_copy(it, off).wait_recv()
            rights.append(operands(jnp.where(k >= off, cr[it, off - 1], 0.0)))
        return jnp.concatenate(rights, axis=0)

    def rows_of(part):
        return pl.ds(part[0], part[1])

    def plane_out(state, kept):
        for z in range(8):
            shuffle[pl.ds(z, PLANE, stride=8), :] = state[z * PLANE:(z + 1) * PLANE]
        flat = shuffle[0:256].T
        kept[0] = jnp.concatenate([flat[:64], flat[64:]], axis=1)

    store_f = pltpu.make_async_copy(f_out, f_ref, out_sem.at[0])
    store_c = pltpu.make_async_copy(c_out, c_ref, out_sem.at[1])

    rights = None
    for it in range(ITERS):
        if it == 0:
            drv[0] = scaled(1, 0, 256) * (bs[...] + src[0])
            exchange(first_message(0))

            @pl.when(k > 0)
            def _():
                back_copy().start()
            exchange(source_message)
        else:
            rights = coarse_landed(it - 1)
            pushed = prolong(classes(ms[:, :(last - 1) * 128], rights[128:]))
            for parts in (ends, middle):
                if parts is ends:
                    wait_for = (0, 1)
                else:
                    wait_for = (2,)

                @pl.when(k > 0)
                def _():
                    for at in wait_for:
                        hand_copy(at).wait_recv()
                for part in parts:
                    first, count = part
                    given = jnp.where(k > 0, hand[rows_of(part)] + pushed[first:first + count], bs[rows_of(part)])
                    drv[it, rows_of(part)] = scaled(1, 0, count) * (given + src[0, rows_of(part)])
                if parts is ends:
                    exchange(first_message(it))
        driven = drv[it]
        total = inner(driven)
        exchanged(first_message(it))
        below_d, above_d = e1[it, 0], e1[it, 1]
        x3a[it] = corrected(driven, total, below_d[PLANE:], above_d[:-PLANE])
        exchange(deep_message(it))
        x3 = x3a[it]
        total = inner(x3)
        if it == 0:
            exchanged(source_message)
        else:
            @pl.when(k == last)
            def _():
                for off in range(1, n_sp):
                    own_landed(off)

                def put_guess(z, plane):
                    st[0, z * PLANE:(z + 1) * PLANE] = plane

                settle(gr[...].reshape(rows, CELLS), put_guess)
            st[it] = st[it - 1] + (prolong(classes(ms[...], rights)) + (hsrc[...] - st[it - 1]))
        exchanged(deep_message(it))
        below, above = e2[it, 0], e2[it, 1]
        x4, x5, below4, above4 = swept(x3, drv[it], total, below, e1[it, 0], above, e1[it, 1])
        below5 = slab_below(below4, e1[it, 0, PLANE:], x4)
        above5 = slab_above(above4, e1[it, 1, :-PLANE], x4)
        xf[...] = x5
        driven = scaled(1, 0, 256) * (x5 + src[1])
        below_d = scaled(1, 1, 2 * PLANE) * (below5 + srch[0])
        above_d = scaled(1, 2, 2 * PLANE) * (above5 + srch[1])
        drv2[...] = driven
        x3b[it] = corrected(driven, inner(driven), below_d, above_d)
        exchange(second_message(it))
        total = inner(x3b[it])
        if it == 0:
            @pl.when(k < last)
            def _():
                back_copy().wait_recv()
        if it == ITERS - 1:
            plane_out(xf, f_out)
            store_f.start()
        exchanged(second_message(it))
        _, x5, _, _ = swept(
            x3b[it], drv2[...], total, e4[it, 0], below_d[PLANE:], e4[it, 1], above_d[:-PLANE])
        if it < ITERS - 1:
            hsrc[...] = x5

            @pl.when(k < last)
            def _():
                cs[it] = restrict(hsrc[...] - st[it])
                for off in range(1, n_tm):
                    @pl.when(k + off < n_tm)
                    def _():
                        coarse_copy(it, off).start()
                for at in range(3):
                    hand_copy(at).start()

            @pl.when(k == last)
            def _():
                for off in range(1, n_sp):
                    own_copy(off).start()
        else:
            residual = x5 - st[it]
            cs[it] = restrict(residual)
            for off in range(1, n_tm):
                @pl.when(k + off < n_tm)
                def _():
                    coarse_copy(it, off).start()
            rights = coarse_landed(it)
            xf[...] = st[it] + (prolong(classes(ms[...], rights)) + residual)

    plane_out(xf, c_out)
    store_c.start()

    for off in range(n_sp):
        slots_copy(off).wait_send()
        spread_copy(off).wait_send()

    @pl.when(k == last)
    def _():
        for off in range(1, n_sp):
            own_copy(off).wait_send()

    @pl.when(k > 0)
    def _():
        back_copy().wait_send()

    drained(table_message)
    drained(source_message)
    for it in range(ITERS):
        drained(first_message(it))
        drained(deep_message(it))
        drained(second_message(it))
        for off in range(1, n_tm):
            @pl.when(k + off < n_tm)
            def _():
                coarse_copy(it, off).wait_send()

    @pl.when(k < last)
    def _():
        for at in range(3):
            hand_copy(at).wait_send()
    store_f.wait()
    store_c.wait()


def solution(mesh):
    n_tm, n_sp = mesh.shape["tm"], mesh.shape["space"]

    def body(init_state, guess, source, remap, neighbors, block_class, step_number, inverse, cstep):
        nb = init_state.shape[0]
        bk = -(-(2 * nb // n_sp) // 8) * 8
        tiles = n_sp * bk // 128
        slots = 2 + 3 * ITERS
        dma = pltpu.SemaphoreType.DMA
        out = jax.ShapeDtypeStruct((1, nb, CELLS), F32)
        full = 8 * PLANE

        def vmem(*shape, dtype=F32):
            return pltpu.VMEM(shape, dtype)

        return pl.pallas_call(
            functools.partial(kernel, n_tm, n_sp, bk),
            name="mgrit",
            out_shape=(out, out),
            in_specs=[pl.BlockSpec(memory_space=pl.ANY)] * 9,
            out_specs=[pl.BlockSpec(memory_space=pl.ANY)] * 2,
            scratch_shapes=[
                vmem(nb, CELLS), vmem(1, nb, CELLS), vmem(1, 2, nb, CELLS), vmem(1, nb, dtype=jnp.int32),
                vmem(6, nb, dtype=jnp.int32), vmem(1, nb, dtype=jnp.int32), vmem(1, CLASSES),
                vmem(CLASSES * COARSE, COARSE), vmem(CLASSES * COARSE, COARSE), vmem(1, nb, CELLS), vmem(1, nb, CELLS),
                vmem(2, n_sp, bk, CELLS), vmem(n_sp, bk, CELLS), vmem(n_sp, bk, CELLS),
                vmem(2, 8, 128, dtype=jnp.int32), vmem(2, 8, 128, dtype=jnp.int32),
                vmem(3, 6, 8, 128, dtype=jnp.int32), vmem(3, 6, 8, 128), vmem(3, 3, 8, 128),
                vmem(2, full, 128), vmem(2, 2 * PLANE, 128), vmem(tiles * CELLS, 128),
                vmem(full, 128), vmem(ITERS, full, 128), vmem(full, 128), vmem(ITERS, full, 128), vmem(ITERS, full, 128),
                vmem(ITERS, 2, 3 * PLANE, 128), vmem(ITERS, 2, 4 * PLANE, 128), vmem(ITERS, 2, 2 * PLANE, 128),
                vmem(ITERS, full, 128), vmem(full, 128), vmem(full, 128), vmem(full, 128),
                vmem(ITERS, PLANE, 128), vmem(ITERS, n_tm - 1, PLANE, 128),
                vmem(CLASSES * COARSE, 128, dtype=BF16), vmem(CLASSES * COARSE, (n_tm - 1) * 128, dtype=BF16),
                vmem(n_sp, 8, 128), vmem(n_sp, 8, 128),
                dma((9,)), dma((2,)), dma((n_sp,)), dma((n_sp,)),
                dma((n_sp,)), dma((n_sp,)), dma((n_sp,)), dma((n_sp,)),
                dma((slots, 2)), dma((slots, 2)),
                dma((3,)), dma((3,)), dma((1,)), dma((1,)),
                dma((ITERS, n_tm - 1)), dma((ITERS, n_tm - 1)),
            ],
            compiler_params=pltpu.CompilerParams(collective_id=0, has_side_effects=True),
        )(
            init_state, guess, source, remap.reshape(1, nb), neighbors.T, block_class.reshape(1, nb),
            step_number.reshape(1, CLASSES), inverse.reshape(CLASSES * COARSE, COARSE),
            cstep.reshape(CLASSES * COARSE, COARSE),
        )

    placed = (
        P("space", None), P("tm", "space", None), P("tm", None, "space", None), P("space"),
        P("space", None), P("space"), P(), P(), P(),
    )
    return jax.shard_map(
        body, mesh=mesh, in_specs=placed,
        out_specs=(P("tm", "space", None), P("tm", "space", None)), check_vma=False,
    )
```

```python
import functools

import jax
import jax.numpy as jnp
from jax import lax
from jax.experimental import pallas as pl
from jax.experimental.pallas import tpu as pltpu
from jax.sharding import PartitionSpec as P

CELLS = 512
COARSE = 64
CLASSES = 4
ITERS = 2
DAMP = 0.8
PLANE = 32
MESH = pl.DeviceIdType.MESH
F32 = jnp.float32
BF16 = jnp.bfloat16


def split(value):
    high = value.astype(BF16)
    return high, (value - high.astype(F32)).astype(BF16)


def dot(left, right):
    return jnp.dot(left, right, preferred_element_type=F32)


def iota(shape, dim):
    return lax.broadcasted_iota(jnp.int32, shape, dim)


def turn(value):
    return pltpu.roll(value, 64, 1)


def along_y(value, shift):
    rows = value.shape[0]
    return pltpu.roll(value.reshape(rows // 8, 8, 128), shift % 8, 1).reshape(rows, 128)


def tiled(table, rows):
    return jnp.broadcast_to(table[None], (rows // 8, 8, 128)).reshape(rows, 128)


def lanes_from(value, index):
    return jnp.take_along_axis(
        value, tiled(index, value.shape[0]), axis=1, mode="promise_in_bounds")


def partner(s, off, n):
    if n & (n - 1):
        return lax.rem(s + off, n)
    to = s
    for bit in range(n.bit_length() - 1):
        if off >> bit & 1:
            to = to + (1 - 2 * lax.rem(lax.div(s, 1 << bit), 2)) * (1 << bit)
    return to


def kernel(
    n_tm, n_sp, bk,
    init_hbm, guess_hbm, source_hbm, remap_hbm, nb_hbm, class_hbm, step_hbm, inv_hbm, cstep_hbm,
    c_ref, f_ref,
    init_ref, guess_ref, source_ref, remap_ref, nb_ref, class_ref, step_ref, inv_ref, cstep_ref,
    gb, br, gr, tab_s, tab_r, tidx, tmask, tscale, src, srch, shuffle,
    bs, drv, drv2, x3a, x3b, e1, e2, e4, st, xf, hsrc, hand, cs, cr, mi, ms,
    slots_out, slots_in, in_sem, so_sem, si_sem,
    gs_sem, gr_sem, ps_sem, br_sem, hs_sem, hr_sem, ts_sem, tr_sem, bk_sem, bq_sem, cs_sem, cr_sem,
):
    k = lax.axis_index("tm")
    s = lax.axis_index("space")
    nb = init_hbm.shape[0]
    rows = n_sp * bk
    bits = nb.bit_length() - 1
    last = n_tm - 1

    after, before = lax.rem(k + 1, n_tm), lax.rem(k + last, n_tm)

    barrier = pltpu.get_barrier_semaphore()

    def greet(tm, space):
        pl.semaphore_signal(barrier, inc=1, device_id=(tm, space), device_id_type=MESH)

    for off in range(n_sp):
        greet(before, partner(s, off, n_sp))

    @pl.when(s > 0)
    def _():
        greet(k, s - 1)

    @pl.when(s < n_sp - 1)
    def _():
        greet(k, s + 1)

    @pl.when(k < last)
    def _():
        greet(k + 1, s)

    for off in range(2, n_tm):
        @pl.when(k >= off)
        def _():
            greet(k - off, s)

    @pl.when(k == last)
    def _():
        for off in range(1, n_sp):
            greet(k, partner(s, off, n_sp))

    loads = [
        pltpu.make_async_copy(given, kept, in_sem.at[at]) for at, (given, kept) in enumerate((
            (remap_hbm, remap_ref), (guess_hbm, guess_ref), (init_hbm, init_ref), (nb_hbm, nb_ref),
            (class_hbm, class_ref), (step_hbm, step_ref), (source_hbm, source_ref), (inv_hbm, inv_ref),
            (cstep_hbm, cstep_ref)))]
    for load in loads:
        load.start()
    loads[0].wait()

    eye = iota((nb, nb), 0) == iota((nb, nb), 1)

    def column(row):
        return jnp.sum(jnp.where(eye, row, 0.0), axis=1, keepdims=True)

    remap_row = remap_ref[...]
    target_row = lax.shift_right_logical(remap_row, bits)
    slot_row = (remap_row - lax.shift_left(target_row, bits)).astype(F32)
    target_f = target_row.astype(F32)
    same = (column(target_f) == target_f) & (iota((nb, nb), 0) < iota((nb, nb), 1))
    pos_row = jnp.sum(jnp.where(same, 1.0, 0.0), axis=0, keepdims=True)
    send_row = target_f * float(bk) + pos_row
    chosen = iota((rows, nb), 0).astype(F32) == send_row
    send_mat = jnp.where(chosen, 1.0, 0.0)
    slot_col = jnp.sum(jnp.where(chosen, slot_row + 1.0, 0.0), axis=1, keepdims=True) - 1.0
    send_mat = jnp.concatenate([send_mat, send_mat], axis=1).astype(BF16)

    def bucketed(value):
        return dot(send_mat, jnp.concatenate(split(value), axis=0)).reshape(n_sp, bk, CELLS)

    spot = iota((n_sp, bk, 128), 1) == iota((n_sp, bk, 128), 2)
    slot_wide = jnp.broadcast_to(slot_col, (rows, 128)).reshape(n_sp, bk, 128)
    slot_lanes = jnp.sum(jnp.where(spot, slot_wide, 0.0), axis=1, keepdims=True)
    slots_out[...] = jnp.broadcast_to(slot_lanes, (n_sp, 8, 128))
    loads[1].wait()
    loads[2].wait()
    gb[0] = bucketed(guess_ref[0])

    @pl.when(k == last)
    def _():
        gb[1] = bucketed(init_ref[...])

    for load in loads[3:6]:
        load.wait()

    linked = nb_ref[...]
    face_no = iota((6, nb), 0)
    run = s + jnp.where(face_no == 4, -1, jnp.where(face_no == 5, 1, 0))
    linked = jnp.where(linked >= 0, linked - run * nb, -1)
    tab_s[0, 0:6] = jnp.concatenate([linked, linked], axis=1)
    kind = class_ref[...]
    tab_s[0, 6:7] = jnp.concatenate([kind, kind], axis=1)
    tab_s[0, 7:8] = jnp.zeros((1, 128), jnp.int32)
    tab_s[1] = tab_s[0]

    greeted = (n_sp + jnp.minimum(s, 1) + jnp.minimum(n_sp - 1 - s, 1) + jnp.minimum(k, 1)
               + jnp.maximum(last - 1 - k, 0) + jnp.maximum(k - last + 1, 0) * (n_sp - 1))
    pl.semaphore_wait(barrier, greeted)

    up_to = (k, lax.rem(s + 1, n_sp))
    down_to = (k, lax.rem(s + n_sp - 1, n_sp))

    def halo_up(slot, source, target):
        return pltpu.make_async_remote_copy(
            src_ref=source, dst_ref=target, send_sem=hs_sem.at[slot, 0],
            recv_sem=hr_sem.at[slot, 0], device_id=up_to, device_id_type=MESH)

    def halo_down(slot, source, target):
        return pltpu.make_async_remote_copy(
            src_ref=source, dst_ref=target, send_sem=hs_sem.at[slot, 1],
            recv_sem=hr_sem.at[slot, 1], device_id=down_to, device_id_type=MESH)

    def planes_message(slot, state, depth, target):
        size = depth * PLANE
        return (halo_up(slot, state.at[pl.ds(8 * PLANE - size, size)], target.at[0]),
                halo_down(slot, state.at[pl.ds(0, size)], target.at[1]))

    def exchange(message):
        up, down = message

        @pl.when(s < n_sp - 1)
        def _():
            up.start()

        @pl.when(s > 0)
        def _():
            down.start()

    def exchanged(message):
        up, down = message

        @pl.when(s > 0)
        def _():
            up.wait_recv()

        @pl.when(s < n_sp - 1)
        def _():
            down.wait_recv()

    def drained(message):
        up, down = message

        @pl.when(s < n_sp - 1)
        def _():
            up.wait_send()

        @pl.when(s > 0)
        def _():
            down.wait_send()

    table_message = (halo_up(0, tab_s.at[0], tab_r.at[0]), halo_down(0, tab_s.at[1], tab_r.at[1]))
    source_message = planes_message(1, src.at[1], 2, srch)

    def first_message(it):
        return planes_message(2 + 3 * it, drv.at[it], 3, e1.at[it])

    def deep_message(it):
        return planes_message(3 + 3 * it, x3a.at[it], 4, e2.at[it])

    def second_message(it):
        return planes_message(4 + 3 * it, x3b.at[it], 2, e4.at[it])

    which = jnp.maximum(k - last + 1, 0)

    def spread_copy(off):
        to = partner(s, off, n_sp)
        return pltpu.make_async_remote_copy(
            src_ref=gb.at[which, to], dst_ref=br.at[s], send_sem=ps_sem.at[off], recv_sem=br_sem.at[s],
            device_id=(after, to), device_id_type=MESH)

    def spread_landed(off):
        origin = partner(s, off, n_sp)
        pltpu.make_async_remote_copy(
            src_ref=gb.at[0, origin], dst_ref=br.at[origin], send_sem=ps_sem.at[off],
            recv_sem=br_sem.at[origin], device_id=(after, origin), device_id_type=MESH).wait_recv()

    def own_copy(off):
        to = partner(s, off, n_sp)
        return pltpu.make_async_remote_copy(
            src_ref=gb.at[0, to], dst_ref=gr.at[s], send_sem=gs_sem.at[off],
            recv_sem=gr_sem.at[s], device_id=(k, to), device_id_type=MESH)

    def own_landed(off):
        origin = partner(s, off, n_sp)
        pltpu.make_async_remote_copy(
            src_ref=gb.at[0, origin], dst_ref=gr.at[origin],
            send_sem=gs_sem.at[off], recv_sem=gr_sem.at[origin], device_id=(k, origin),
            device_id_type=MESH).wait_recv()

    def slots_copy(off):
        to = partner(s, off, n_sp)
        return pltpu.make_async_remote_copy(
            src_ref=slots_out.at[to], dst_ref=slots_in.at[s], send_sem=so_sem.at[off],
            recv_sem=si_sem.at[s], device_id=(after, to), device_id_type=MESH)

    def slots_landed(off):
        origin = partner(s, off, n_sp)
        pltpu.make_async_remote_copy(
            src_ref=slots_out.at[origin], dst_ref=slots_in.at[origin], send_sem=so_sem.at[off],
            recv_sem=si_sem.at[origin], device_id=(after, origin), device_id_type=MESH).wait_recv()

    for off in reversed(range(n_sp)):
        spread_copy(off).start()
        if off == n_sp // 2:
            for small in reversed(range(n_sp)):
                slots_copy(small).start()
            exchange(table_message)
    gr[s] = gb[0, s]

    lane = iota((8, 128), 1)
    sub = iota((8, 128), 0)
    left = lane < 64
    half = lane & 64

    def blocks_in_lanes(value):
        return jnp.concatenate([value[:, :CELLS // 2], value[:, CELLS // 2:]], axis=0).T

    for load in loads[6:]:
        load.wait()
    for fine in range(2):
        shuffle[0:256] = blocks_in_lanes(source_ref[0, fine])
        for z in range(8):
            src[fine, z * PLANE:(z + 1) * PLANE] = shuffle[pl.ds(z, PLANE, stride=8), :]

    def make_tables(at, table):
        faces = [jnp.broadcast_to(table[face:face + 1], (8, 128)) for face in range(7)]
        inside = [jnp.maximum(face, 0) for face in faces]
        index = [
            jnp.where(left, inside[0] + 64, lane - 64), jnp.where(left, lane + 64, inside[1]),
            half + jnp.where(sub < 4, inside[2], inside[3]), lane,
            half + inside[4], half + inside[5],
        ]
        known = [jnp.where(face >= 0, 1.0, 0.0) for face in faces[:6]]
        mask = [
            jnp.where(left, known[0], 1.0), jnp.where(left, 1.0, known[1]),
            jnp.where(sub < 4, known[2], known[3]), known[2],
            known[4], known[5],
        ]
        for face in range(6):
            tidx[at, face] = index[face]
            tmask[at, face] = mask[face]
        dif = jnp.zeros((8, 128), F32)
        for cl in range(CLASSES):
            dif = dif + jnp.where(faces[6] == cl, step_ref[:, cl:cl + 1], 0.0)
        tscale[at, 0] = DAMP * dif / (1.0 + 6.0 * dif)
        tscale[at, 1] = DAMP / (1.0 + 6.0 * dif)
        tscale[at, 2] = (1.0 + 6.0 * dif) / DAMP

    make_tables(0, tab_s[0])

    def coarse_of(row):
        high = lax.shift_right_logical(row, 5) * 2 + (row & 1)
        return high * 16 + (lax.shift_right_logical(row, 1) & 3) * 4 + (lax.shift_right_logical(row, 3) & 3)

    size = CLASSES * COARSE
    in_class = (lax.shift_right_logical(iota((size, size), 0), 6)
                == lax.shift_right_logical(iota((size, size), 1), 6))
    tall = jnp.where(in_class & (coarse_of(iota((size, size), 0) & 63) == (iota((size, size), 1) & 63)),
                     1.0, 0.0).astype(BF16)
    wide = jnp.where(coarse_of(iota((COARSE, COARSE), 1)) == iota((COARSE, COARSE), 0), 0.125, 0.0).astype(BF16)

    def made(given):
        parts = [dot(tall, dot(piece, wide).astype(BF16)).astype(BF16) for piece in split(given)]
        return jnp.concatenate(parts, axis=1)

    mi[...] = made(inv_ref[...])
    power = cstep_ref[...]
    step_h, step_l = split(jnp.where(in_class, jnp.concatenate([power] * CLASSES, axis=1), 0.0))
    step_all = jnp.concatenate([step_h, step_h, step_l], axis=1)
    for d in range(last):
        if d > 0:
            power_h, power_l = split(power)
            power = dot(step_all, jnp.concatenate([power_h, power_l, power_h], axis=0))
        ms[:, d * 128:(d + 1) * 128] = made(power)

    def operands(coarse):
        high = coarse.astype(BF16).astype(F32)
        low = coarse - high
        here = tiled(left, PLANE)
        turned = turn(high)
        return jnp.concatenate([
            jnp.where(here, high, turn(low)), jnp.where(here, turned, low),
            jnp.where(here, high, 0.0), jnp.where(here, turned, 0.0)], axis=0).astype(BF16)

    def classes(mat, right):
        product = dot(mat, right)
        kinds = jnp.broadcast_to(tab_s[0, 6:7], (COARSE, 128))
        picked = jnp.where(kinds == 0, product[:COARSE], 0.0)
        for cl in range(1, CLASSES):
            picked = jnp.where(kinds == cl, product[cl * COARSE:(cl + 1) * COARSE], picked)
        picked = picked + turn(picked)
        return jnp.where(tiled(left, PLANE), picked[:PLANE], picked[PLANE:])

    even = (sub & 1) == 0

    def restrict(value):
        pairs = value.reshape(4, 2, 2, 2, 8, 128)
        pairs = pairs[:, 0] + pairs[:, 1]
        pairs = pairs[:, :, 0] + pairs[:, :, 1]
        first = pairs[:, 0].reshape(PLANE, 128)
        second = pairs[:, 1].reshape(PLANE, 128)
        return jnp.where(tiled(even, PLANE), first + along_y(first, -1), second + along_y(second, 1))

    def prolong(coarse):
        here = tiled(even, PLANE)
        first = jnp.where(here, coarse, along_y(coarse, 1)).reshape(4, 1, 1, 1, 8, 128)
        second = jnp.where(here, along_y(coarse, -1), coarse).reshape(4, 1, 1, 1, 8, 128)
        both = jnp.concatenate([first, second], axis=2)
        return jnp.broadcast_to(both, (4, 2, 2, 2, 8, 128)).reshape(256, 128)

    def ghost(plane, face, at):
        return jnp.where(tiled(tmask[at, face], PLANE) > 0.0, lanes_from(plane, tidx[at, face]), 0.0)

    def picked_from(value, face, at):
        return jnp.where(
            tiled(tmask[at, face], value.shape[0]) > 0.0, lanes_from(value, tidx[at, face]), 0.0)

    def beside_xy(value, at):
        size = value.shape[0]
        n = size // PLANE
        cube = value.reshape(n, 4, 8, 128)
        part = [cube[:, j].reshape(n * 8, 128) for j in range(4)]
        low = picked_from(part[3], 0, at)
        high = picked_from(part[0], 1, at)
        here = tiled(sub, n * 8)
        edges = along_y(part[0], 1)
        for j in range(1, 8):
            edges = jnp.where(here == j, along_y(part[j % 4], j + 1 if j < 4 else j), edges)
        edges = picked_from(edges, 2, at)
        sums = []
        for j in range(4):
            total = (part[j - 1] if j > 0 else low) + (part[j + 1] if j < 3 else high)
            total = total + jnp.where(here == 0, along_y(edges, -j), along_y(part[j], 1))
            total = total + jnp.where(here == 7, along_y(edges, 3 - j), along_y(part[j], -1))
            sums.append(total.reshape(n, 1, 8, 128))
        return jnp.concatenate(sums, axis=1).reshape(size, 128)

    def inner(value):
        zero = jnp.zeros((PLANE, 128), F32)
        total = beside_xy(value, 0)
        total = total + jnp.concatenate([zero, value[:-PLANE]], axis=0)
        return total + jnp.concatenate([value[PLANE:], zero], axis=0)

    def ended(total, below, above):
        return jnp.concatenate([
            total[:PLANE] + ghost(below, 4, 0), total[PLANE:-PLANE],
            total[-PLANE:] + ghost(above, 5, 0)], axis=0)

    def scaled(which, at, size):
        return tiled(tscale[at, which], size)

    def relax(value, driven, total, at):
        return (1.0 - DAMP) * value + driven + scaled(0, at, value.shape[0]) * total

    def slab_below(slab, driven, own):
        cross = ghost(own[:PLANE], 5, 1)
        near = slab[PLANE:]
        upper = jnp.concatenate([slab[2 * PLANE:], cross], axis=0) if slab.shape[0] > 2 * PLANE else cross
        return relax(near, driven, beside_xy(near, 1) + slab[:-PLANE] + upper, 1)

    def slab_above(slab, driven, own):
        cross = ghost(own[-PLANE:], 4, 2)
        near = slab[:-PLANE]
        lower = jnp.concatenate([cross, slab[:-2 * PLANE]], axis=0) if slab.shape[0] > 2 * PLANE else cross
        return relax(near, driven, beside_xy(near, 2) + slab[PLANE:] + lower, 2)

    def corrected(driven, total, below, above):
        x2 = relax(driven, driven, ended(total, below[-PLANE:], above[:PLANE]), 0)
        below2 = slab_below(below, below[PLANE:], driven)
        above2 = slab_above(above, above[:-PLANE], driven)
        total = ended(inner(x2), below2[-PLANE:], above2[:PLANE])
        rest = driven - DAMP * x2 + scaled(0, 0, 256) * total
        return x2 + prolong(classes(mi[...], operands(scaled(2, 0, PLANE) * restrict(rest))))

    def swept(x3, driven, total, below, below_d, above, above_d):
        x4 = relax(x3, driven, ended(total, below[-PLANE:], above[:PLANE]), 0)
        below4 = slab_below(below, below_d, x3)
        above4 = slab_above(above, above_d, x3)
        x5 = relax(x4, driven, ended(inner(x4), below4[-PLANE:], above4[:PLANE]), 0)
        return x4, x5, below4, above4

    exchanged(table_message)
    for side in range(2):
        reached = (s > 0) if side == 0 else (s < n_sp - 1)
        make_tables(1 + side, jnp.where(reached, tab_r[side], -1))

    for off in range(n_sp):
        slots_landed(off)
    slots = jnp.sum(jnp.where(spot, slots_in[:, :1], 0.0), axis=2, keepdims=True)
    slots = jnp.broadcast_to(slots, (n_sp, bk, 128)).reshape(rows, 128)
    hit = slots == (iota((rows, 128), 1) & 63).astype(F32)
    place = jnp.sum(jnp.where(hit, iota((rows, 128), 0).astype(F32), 0.0), axis=0, keepdims=True)
    place = jnp.broadcast_to(place, (8, 128)).astype(jnp.int32)

    def settle(given, put):
        tiles = rows // 128
        for tile in range(tiles):
            shuffle[tile * CELLS:(tile + 1) * CELLS] = given[tile * 128:(tile + 1) * 128].T
        for z in range(8):
            plane = None
            for tile in range(tiles):
                both = shuffle[pl.ds(tile * CELLS + z, 64, stride=8), :]
                both = lanes_from(both, place & 127)
                both = jnp.where(tiled(left, PLANE), both[:PLANE], both[PLANE:])
                chosen_tile = tiled(lax.shift_right_logical(place, 7), PLANE) == tile
                plane = both if plane is None else jnp.where(chosen_tile, both, plane)
            put(z, plane)

    for off in range(n_sp):
        spread_landed(off)

    def put_start(z, plane):
        bs[z * PLANE:(z + 1) * PLANE] = plane

    settle(br[...].reshape(rows, CELLS), put_start)

    def back_copy():
        return pltpu.make_async_remote_copy(
            src_ref=bs, dst_ref=st.at[0], send_sem=bk_sem.at[0], recv_sem=bq_sem.at[0],
            device_id=(before, s), device_id_type=MESH)

    ends = ((0, 3 * PLANE), (5 * PLANE, 3 * PLANE))
    middle = ((3 * PLANE, 2 * PLANE),)

    def hand_copy(at):
        first, count = (ends + middle)[at]
        return pltpu.make_async_remote_copy(
            src_ref=hsrc.at[pl.ds(first, count)], dst_ref=hand.at[pl.ds(first, count)],
            send_sem=ts_sem.at[at], recv_sem=tr_sem.at[at], device_id=(after, s), device_id_type=MESH)

    def coarse_copy(it, off):
        return pltpu.make_async_remote_copy(
            src_ref=cs.at[it], dst_ref=cr.at[it, off - 1], send_sem=cs_sem.at[it, off - 1],
            recv_sem=cr_sem.at[it, off - 1], device_id=(lax.rem(k + off, n_tm), s), device_id_type=MESH)

    def coarse_landed(it):
        rights = []
        for off in range(1, n_tm):
            @pl.when(k >= off)
            def _():
                coarse_copy(it, off).wait_recv()
            rights.append(operands(jnp.where(k >= off, cr[it, off - 1], 0.0)))
        return jnp.concatenate(rights, axis=0)

    def rows_of(part):
        return pl.ds(part[0], part[1])

    def plane_out(state, kept):
        for z in range(8):
            shuffle[pl.ds(z, PLANE, stride=8), :] = state[z * PLANE:(z + 1) * PLANE]
        flat = shuffle[0:256].T
        kept[0] = jnp.concatenate([flat[:64], flat[64:]], axis=1)


    rights = None
    for it in range(ITERS):
        if it == 0:
            drv[0] = scaled(1, 0, 256) * (bs[...] + src[0])
            exchange(first_message(0))

            @pl.when(k > 0)
            def _():
                back_copy().start()
            exchange(source_message)
        else:
            rights = coarse_landed(it - 1)
            pushed = prolong(classes(ms[:, :(last - 1) * 128], rights[128:]))
            for parts in (ends, middle):
                if parts is ends:
                    wait_for = (0, 1)
                else:
                    wait_for = (2,)

                @pl.when(k > 0)
                def _():
                    for at in wait_for:
                        hand_copy(at).wait_recv()
                for part in parts:
                    first, count = part
                    given = jnp.where(k > 0, hand[rows_of(part)] + pushed[first:first + count], bs[rows_of(part)])
                    drv[it, rows_of(part)] = scaled(1, 0, count) * (given + src[0, rows_of(part)])
                if parts is ends:
                    exchange(first_message(it))
        driven = drv[it]
        total = inner(driven)
        exchanged(first_message(it))
        below_d, above_d = e1[it, 0], e1[it, 1]
        x3a[it] = corrected(driven, total, below_d[PLANE:], above_d[:-PLANE])
        exchange(deep_message(it))
        x3 = x3a[it]
        total = inner(x3)
        if it == 0:
            exchanged(source_message)
        else:
            @pl.when(k == last)
            def _():
                for off in range(1, n_sp):
                    own_landed(off)

                def put_guess(z, plane):
                    st[0, z * PLANE:(z + 1) * PLANE] = plane

                settle(gr[...].reshape(rows, CELLS), put_guess)
            st[it] = st[it - 1] + (prolong(classes(ms[...], rights)) + (hsrc[...] - st[it - 1]))
        exchanged(deep_message(it))
        below, above = e2[it, 0], e2[it, 1]
        x4, x5, below4, above4 = swept(x3, drv[it], total, below, e1[it, 0], above, e1[it, 1])
        below5 = slab_below(below4, e1[it, 0, PLANE:], x4)
        above5 = slab_above(above4, e1[it, 1, :-PLANE], x4)
        xf[...] = x5
        driven = scaled(1, 0, 256) * (x5 + src[1])
        below_d = scaled(1, 1, 2 * PLANE) * (below5 + srch[0])
        above_d = scaled(1, 2, 2 * PLANE) * (above5 + srch[1])
        drv2[...] = driven
        x3b[it] = corrected(driven, inner(driven), below_d, above_d)
        exchange(second_message(it))
        total = inner(x3b[it])
        if it == 0:
            @pl.when(k < last)
            def _():
                back_copy().wait_recv()
        if it == ITERS - 1:
            plane_out(xf, f_ref)
        exchanged(second_message(it))
        _, x5, _, _ = swept(
            x3b[it], drv2[...], total, e4[it, 0], below_d[PLANE:], e4[it, 1], above_d[:-PLANE])
        if it < ITERS - 1:
            hsrc[...] = x5

            @pl.when(k < last)
            def _():
                cs[it] = restrict(hsrc[...] - st[it])
                for off in range(1, n_tm):
                    @pl.when(k + off < n_tm)
                    def _():
                        coarse_copy(it, off).start()
                for at in range(3):
                    hand_copy(at).start()

            @pl.when(k == last)
            def _():
                for off in range(1, n_sp):
                    own_copy(off).start()
        else:
            residual = x5 - st[it]
            cs[it] = restrict(residual)
            for off in range(1, n_tm):
                @pl.when(k + off < n_tm)
                def _():
                    coarse_copy(it, off).start()
            rights = coarse_landed(it)
            xf[...] = st[it] + (prolong(classes(ms[...], rights)) + residual)

    plane_out(xf, c_ref)

    for off in range(n_sp):
        slots_copy(off).wait_send()
        spread_copy(off).wait_send()

    @pl.when(k == last)
    def _():
        for off in range(1, n_sp):
            own_copy(off).wait_send()

    @pl.when(k > 0)
    def _():
        back_copy().wait_send()

    drained(table_message)
    drained(source_message)
    for it in range(ITERS):
        drained(first_message(it))
        drained(deep_message(it))
        drained(second_message(it))
        for off in range(1, n_tm):
            @pl.when(k + off < n_tm)
            def _():
                coarse_copy(it, off).wait_send()

    @pl.when(k < last)
    def _():
        for at in range(3):
            hand_copy(at).wait_send()


def solution(mesh):
    n_tm, n_sp = mesh.shape["tm"], mesh.shape["space"]

    def body(init_state, guess, source, remap, neighbors, block_class, step_number, inverse, cstep):
        nb = init_state.shape[0]
        bk = -(-(2 * nb // n_sp) // 8) * 8
        tiles = n_sp * bk // 128
        slots = 2 + 3 * ITERS
        dma = pltpu.SemaphoreType.DMA
        full = 8 * PLANE

        def vmem(*shape, dtype=F32):
            return pltpu.VMEM(shape, dtype)

        return pl.pallas_call(
            functools.partial(kernel, n_tm, n_sp, bk),
            name="mgrit",
            out_shape=(vmem(1, nb, CELLS), vmem(1, nb, CELLS)),
            in_specs=[pl.BlockSpec(memory_space=pl.ANY)] * 9,
            out_specs=[pl.BlockSpec(memory_space=pltpu.VMEM)] * 2,
            scratch_shapes=[
                vmem(nb, CELLS), vmem(1, nb, CELLS), vmem(1, 2, nb, CELLS), vmem(1, nb, dtype=jnp.int32),
                vmem(6, nb, dtype=jnp.int32), vmem(1, nb, dtype=jnp.int32), vmem(1, CLASSES),
                vmem(CLASSES * COARSE, COARSE), vmem(CLASSES * COARSE, COARSE),
                vmem(2, n_sp, bk, CELLS), vmem(n_sp, bk, CELLS), vmem(n_sp, bk, CELLS),
                vmem(2, 8, 128, dtype=jnp.int32), vmem(2, 8, 128, dtype=jnp.int32),
                vmem(3, 6, 8, 128, dtype=jnp.int32), vmem(3, 6, 8, 128), vmem(3, 3, 8, 128),
                vmem(2, full, 128), vmem(2, 2 * PLANE, 128), vmem(tiles * CELLS, 128),
                vmem(full, 128), vmem(ITERS, full, 128), vmem(full, 128), vmem(ITERS, full, 128), vmem(ITERS, full, 128),
                vmem(ITERS, 2, 3 * PLANE, 128), vmem(ITERS, 2, 4 * PLANE, 128), vmem(ITERS, 2, 2 * PLANE, 128),
                vmem(ITERS, full, 128), vmem(full, 128), vmem(full, 128), vmem(full, 128),
                vmem(ITERS, PLANE, 128), vmem(ITERS, n_tm - 1, PLANE, 128),
                vmem(CLASSES * COARSE, 128, dtype=BF16), vmem(CLASSES * COARSE, (n_tm - 1) * 128, dtype=BF16),
                vmem(n_sp, 8, 128), vmem(n_sp, 8, 128),
                dma((9,)), dma((n_sp,)), dma((n_sp,)),
                dma((n_sp,)), dma((n_sp,)), dma((n_sp,)), dma((n_sp,)),
                dma((slots, 2)), dma((slots, 2)),
                dma((3,)), dma((3,)), dma((1,)), dma((1,)),
                dma((ITERS, n_tm - 1)), dma((ITERS, n_tm - 1)),
            ],
            compiler_params=pltpu.CompilerParams(collective_id=0, has_side_effects=True),
        )(
            init_state, guess, source, remap.reshape(1, nb), neighbors.T, block_class.reshape(1, nb),
            step_number.reshape(1, CLASSES), inverse.reshape(CLASSES * COARSE, COARSE),
            cstep.reshape(CLASSES * COARSE, COARSE),
        )

    placed = (
        P("space", None), P("tm", "space", None), P("tm", None, "space", None), P("space"),
        P("space", None), P("space"), P(), P(), P(),
    )
    return jax.shard_map(
        body, mesh=mesh, in_specs=placed,
        out_specs=(P("tm", "space", None), P("tm", "space", None)), check_vma=False,
    )
```

```python
import functools

import jax
import jax.numpy as jnp
from jax import lax
from jax.experimental import pallas as pl
from jax.experimental.pallas import tpu as pltpu
from jax.sharding import PartitionSpec as P

CELLS = 512
COARSE = 64
CLASSES = 4
ITERS = 2
DAMP = 0.8
PLANE = 32
MESH = pl.DeviceIdType.MESH
F32 = jnp.float32
BF16 = jnp.bfloat16


def split(value):
    high = value.astype(BF16)
    return high, (value - high.astype(F32)).astype(BF16)


def dot(left, right):
    return jnp.dot(left, right, preferred_element_type=F32)


def iota(shape, dim):
    return lax.broadcasted_iota(jnp.int32, shape, dim)


def turn(value):
    return pltpu.roll(value, 64, 1)


def along_y(value, shift):
    rows = value.shape[0]
    return pltpu.roll(value.reshape(rows // 8, 8, 128), shift % 8, 1).reshape(rows, 128)


def tiled(table, rows):
    return jnp.broadcast_to(table[None], (rows // 8, 8, 128)).reshape(rows, 128)


def lanes_from(value, index):
    return jnp.take_along_axis(
        value, tiled(index, value.shape[0]), axis=1, mode="promise_in_bounds")


def partner(s, off, n):
    if n & (n - 1):
        return lax.rem(s + off, n)
    to = s
    for bit in range(n.bit_length() - 1):
        if off >> bit & 1:
            to = to + (1 - 2 * lax.rem(lax.div(s, 1 << bit), 2)) * (1 << bit)
    return to


def kernel(
    n_tm, n_sp, bk,
    init_hbm, guess_hbm, source_hbm, remap_hbm, nb_hbm, class_hbm, step_hbm, inv_hbm, cstep_hbm,
    c_ref, f_ref,
    init_ref, guess_ref, source_ref, remap_ref, nb_ref, class_ref, step_ref, inv_ref, cstep_ref,
    gb, br, gr, far, tab_s, tab_r, tidx, tmask, tscale, src, srch, shuffle,
    bs, drv, drv2, x3a, x3b, e1, e2, e4, st, xf, hsrc, hand, mine, rg_s, rg_r, cs, cr, table, spread_rows, entries, ms,
    slots_out, slots_in, in_sem, so_sem, si_sem,
    gs_sem, gr_sem, ps_sem, br_sem, hs_sem, hr_sem, ts_sem, tr_sem, bk_sem, bq_sem, cs_sem, cr_sem, fs_sem, fr_sem,
):
    k = lax.axis_index("tm")
    s = lax.axis_index("space")
    nb = init_hbm.shape[0]
    rows = n_sp * bk
    bits = nb.bit_length() - 1
    last = n_tm - 1

    after, before = lax.rem(k + 1, n_tm), lax.rem(k + last, n_tm)

    barrier = pltpu.get_barrier_semaphore()

    def greet(tm, space):
        pl.semaphore_signal(barrier, inc=1, device_id=(tm, space), device_id_type=MESH)

    for off in range(1, n_sp):
        greet(k, partner(s, off, n_sp))
    for off in range(1, n_tm):
        greet(lax.rem(k + off, n_tm), s)

    loads = [
        pltpu.make_async_copy(given, kept, in_sem.at[at]) for at, (given, kept) in enumerate((
            (remap_hbm, remap_ref), (guess_hbm, guess_ref), (init_hbm, init_ref), (nb_hbm, nb_ref),
            (class_hbm, class_ref), (step_hbm, step_ref), (source_hbm, source_ref), (inv_hbm, inv_ref),
            (cstep_hbm, cstep_ref)))]
    for load in loads:
        load.start()
    loads[0].wait()

    eye = iota((nb, nb), 0) == iota((nb, nb), 1)

    def column(row):
        return jnp.sum(jnp.where(eye, row, 0.0), axis=1, keepdims=True)

    remap_row = remap_ref[...]
    target_row = lax.shift_right_logical(remap_row, bits)
    slot_row = (remap_row - lax.shift_left(target_row, bits)).astype(F32)
    target_f = target_row.astype(F32)
    same = (column(target_f) == target_f) & (iota((nb, nb), 0) < iota((nb, nb), 1))
    pos_row = jnp.sum(jnp.where(same, 1.0, 0.0), axis=0, keepdims=True)
    send_row = target_f * float(bk) + pos_row
    chosen = iota((rows, nb), 0).astype(F32) == send_row
    send_mat = jnp.where(chosen, 1.0, 0.0)
    slot_col = jnp.sum(jnp.where(chosen, slot_row + 1.0, 0.0), axis=1, keepdims=True) - 1.0
    send_mat = jnp.concatenate([send_mat, send_mat], axis=1).astype(BF16)

    def bucketed(value):
        return dot(send_mat, jnp.concatenate(split(value), axis=0)).reshape(n_sp, bk, CELLS)

    spot = iota((n_sp, bk, 128), 1) == iota((n_sp, bk, 128), 2)
    slot_wide = jnp.broadcast_to(slot_col, (rows, 128)).reshape(n_sp, bk, 128)
    slot_lanes = jnp.sum(jnp.where(spot, slot_wide, 0.0), axis=1, keepdims=True)
    slots_out[...] = jnp.broadcast_to(slot_lanes, (n_sp, 8, 128))
    loads[1].wait()
    loads[2].wait()
    gb[0] = bucketed(guess_ref[0])

    @pl.when(k == last)
    def _():
        gb[1] = bucketed(init_ref[...])

    for load in loads[3:6]:
        load.wait()

    linked = nb_ref[...]
    face_no = iota((6, nb), 0)
    run = s + jnp.where(face_no == 4, -1, jnp.where(face_no == 5, 1, 0))
    linked = jnp.where(linked >= 0, linked - run * nb, -1)
    tab_s[0, 0:6] = jnp.concatenate([linked, linked], axis=1)
    kind = class_ref[...]
    tab_s[0, 6:7] = jnp.concatenate([kind, kind], axis=1)
    tab_s[0, 7:8] = jnp.zeros((1, 128), jnp.int32)
    tab_s[1] = tab_s[0]

    pl.semaphore_wait(barrier, n_sp - 1 + n_tm - 1)

    up_to = (k, lax.rem(s + 1, n_sp))
    down_to = (k, lax.rem(s + n_sp - 1, n_sp))

    def halo_up(slot, source, target):
        return pltpu.make_async_remote_copy(
            src_ref=source, dst_ref=target, send_sem=hs_sem.at[slot, 0],
            recv_sem=hr_sem.at[slot, 0], device_id=up_to, device_id_type=MESH)

    def halo_down(slot, source, target):
        return pltpu.make_async_remote_copy(
            src_ref=source, dst_ref=target, send_sem=hs_sem.at[slot, 1],
            recv_sem=hr_sem.at[slot, 1], device_id=down_to, device_id_type=MESH)

    def planes_message(slot, state, depth, target):
        size = depth * PLANE
        return (halo_up(slot, state.at[pl.ds(8 * PLANE - size, size)], target.at[0]),
                halo_down(slot, state.at[pl.ds(0, size)], target.at[1]))

    def exchange(message):
        up, down = message

        @pl.when(s < n_sp - 1)
        def _():
            up.start()

        @pl.when(s > 0)
        def _():
            down.start()

    def exchanged(message):
        up, down = message

        @pl.when(s > 0)
        def _():
            up.wait_recv()

        @pl.when(s < n_sp - 1)
        def _():
            down.wait_recv()

    def drained(message):
        up, down = message

        @pl.when(s < n_sp - 1)
        def _():
            up.wait_send()

        @pl.when(s > 0)
        def _():
            down.wait_send()

    table_message = (halo_up(0, tab_s.at[0], tab_r.at[0]), halo_down(0, tab_s.at[1], tab_r.at[1]))

    def source_message(it):
        return planes_message(1 + it, src.at[it, 1], 2, srch.at[it])

    def first_message(it):
        return planes_message(3 + 3 * it, drv.at[it], 3, e1.at[it])

    def deep_message(it):
        return planes_message(4 + 3 * it, x3a.at[it], 4, e2.at[it])

    def second_message(it):
        return planes_message(5 + 3 * it, x3b.at[it], 2, e4.at[it])

    which = jnp.maximum(k - last + 1, 0)

    def spread_copy(off):
        to = partner(s, off, n_sp)
        return pltpu.make_async_remote_copy(
            src_ref=gb.at[which, to], dst_ref=br.at[s], send_sem=ps_sem.at[off], recv_sem=br_sem.at[s],
            device_id=(k, to), device_id_type=MESH)

    def spread_landed(off):
        origin = partner(s, off, n_sp)
        pltpu.make_async_remote_copy(
            src_ref=gb.at[0, origin], dst_ref=br.at[origin], send_sem=ps_sem.at[off],
            recv_sem=br_sem.at[origin], device_id=(k, origin), device_id_type=MESH).wait_recv()

    def own_copy(off):
        to = partner(s, off, n_sp)
        return pltpu.make_async_remote_copy(
            src_ref=gb.at[0, to], dst_ref=gr.at[s], send_sem=gs_sem.at[off],
            recv_sem=gr_sem.at[s], device_id=(k, to), device_id_type=MESH)

    def own_landed(off):
        origin = partner(s, off, n_sp)
        pltpu.make_async_remote_copy(
            src_ref=gb.at[0, origin], dst_ref=gr.at[origin],
            send_sem=gs_sem.at[off], recv_sem=gr_sem.at[origin], device_id=(k, origin),
            device_id_type=MESH).wait_recv()

    def slots_copy(off):
        to = partner(s, off, n_sp)
        return pltpu.make_async_remote_copy(
            src_ref=slots_out.at[to], dst_ref=slots_in.at[s], send_sem=so_sem.at[off],
            recv_sem=si_sem.at[s], device_id=(k, to), device_id_type=MESH)

    def slots_landed(off):
        origin = partner(s, off, n_sp)
        pltpu.make_async_remote_copy(
            src_ref=slots_out.at[origin], dst_ref=slots_in.at[origin], send_sem=so_sem.at[off],
            recv_sem=si_sem.at[origin], device_id=(k, origin), device_id_type=MESH).wait_recv()

    for off in reversed(range(1, n_sp)):
        spread_copy(off).start()
        if off == n_sp // 2:
            for small in reversed(range(1, n_sp)):
                slots_copy(small).start()
            exchange(table_message)

    def source_copy(fine):
        return pltpu.make_async_remote_copy(
            src_ref=source_ref.at[0, fine], dst_ref=far.at[fine], send_sem=fs_sem.at[fine],
            recv_sem=fr_sem.at[fine], device_id=(before, s), device_id_type=MESH)

    for load in loads[6:]:
        load.wait()
    for fine in range(2):
        source_copy(fine).start()
    br[s] = gb[which, s]
    slots_in[s] = slots_out[s]
    gr[s] = gb[0, s]

    lane = iota((8, 128), 1)
    sub = iota((8, 128), 0)
    left = lane < 64
    half = lane & 64

    def blocks_in_lanes(value):
        return jnp.concatenate([value[:, :CELLS // 2], value[:, CELLS // 2:]], axis=0).T

    def put_source(it, fine, value):
        shuffle[0:256] = blocks_in_lanes(value)
        for z in range(8):
            src[it, fine, z * PLANE:(z + 1) * PLANE] = shuffle[pl.ds(z, PLANE, stride=8), :]

    for fine in range(2):
        put_source(1, fine, source_ref[0, fine])

    def make_tables(at, table):
        faces = [jnp.broadcast_to(table[face:face + 1], (8, 128)) for face in range(7)]
        inside = [jnp.maximum(face, 0) for face in faces]
        index = [
            jnp.where(left, inside[0] + 64, lane - 64), jnp.where(left, lane + 64, inside[1]),
            half + jnp.where(sub < 4, inside[2], inside[3]), lane,
            half + inside[4], half + inside[5],
        ]
        known = [jnp.where(face >= 0, 1.0, 0.0) for face in faces[:6]]
        mask = [
            jnp.where(left, known[0], 1.0), jnp.where(left, 1.0, known[1]),
            jnp.where(sub < 4, known[2], known[3]), known[2],
            known[4], known[5],
        ]
        for face in range(6):
            tidx[at, face] = index[face]
            tmask[at, face] = mask[face]
        dif = jnp.zeros((8, 128), F32)
        for cl in range(CLASSES):
            dif = dif + jnp.where(faces[6] == cl, step_ref[:, cl:cl + 1], 0.0)
        tscale[at, 0] = DAMP * dif / (1.0 + 6.0 * dif)
        tscale[at, 1] = DAMP / (1.0 + 6.0 * dif)
        tscale[at, 2] = (1.0 + 6.0 * dif) / DAMP

    make_tables(0, tab_s[0])

    def coarse_of(row):
        high = lax.shift_right_logical(row, 5) * 2 + (row & 1)
        return high * 16 + (lax.shift_right_logical(row, 1) & 3) * 4 + (lax.shift_right_logical(row, 3) & 3)

    size = CLASSES * COARSE
    in_class = (lax.shift_right_logical(iota((size, size), 0), 6)
                == lax.shift_right_logical(iota((size, size), 1), 6))
    tall = jnp.where(in_class & (coarse_of(iota((size, size), 0) & 63) == (iota((size, size), 1) & 63)),
                     1.0, 0.0).astype(BF16)
    wide = jnp.where(coarse_of(iota((COARSE, COARSE), 1)) == iota((COARSE, COARSE), 0), 0.125, 0.0).astype(BF16)

    def made(given):
        parts = [dot(tall, dot(piece, wide).astype(BF16)).astype(BF16) for piece in split(given)]
        return jnp.concatenate(parts, axis=1)

    both = made(inv_ref[...])
    lanes = CLASSES * 2 * COARSE
    blocks = [
        jnp.concatenate([both[at * PLANE:(at + 1) * PLANE, part * COARSE:(part + 1) * COARSE]
                         for at in range(2 * CLASSES)], axis=1) for part in range(2)]
    at_row, at_lane = iota((lanes, lanes), 0), iota((lanes, lanes), 1)
    place_of = ((at_row & 63) * 8 + (lax.shift_right_logical(at_row, 6) & 1) * 4
                + lax.shift_right_logical(at_row, 7))
    moved = dot(jnp.concatenate(blocks, axis=0), jnp.where(place_of == at_lane, 1.0, 0.0).astype(BF16))
    moved = moved[:PLANE] + moved[PLANE:]
    for group in range(4):
        table[group] = moved[:, group * 128:(group + 1) * 128]
    start = jnp.broadcast_to(tab_s[0, 6:7], (8, 128)) + lax.shift_right_logical(lane, 6) * 4

    def make_entries(i, carry):
        for group in range(4):
            entries[group * 16 + i] = lanes_from(table[group], start + 8 * i)
        return carry

    lax.fori_loop(0, 16, make_entries, 0)

    def inverse(coarse):
        here = tiled(left, PLANE)
        turned = turn(coarse)
        spread_rows[:PLANE] = jnp.where(here, coarse, turned)
        spread_rows[PLANE:] = jnp.where(here, turned, coarse)

        def add(step, sums):
            first, second = sums
            for j in range(0, 8, 2):
                first = first + entries[8 * step + j] * spread_rows[pl.ds(8 * step + j, 1)]
                second = second + entries[8 * step + j + 1] * spread_rows[pl.ds(8 * step + j + 1, 1)]
            return first, second

        zero = jnp.zeros((PLANE, 128), F32)
        first, second = lax.fori_loop(0, 8, add, (zero, zero), unroll=True)
        return first + second

    power = cstep_ref[...]
    step_h, step_l = split(jnp.where(in_class, jnp.concatenate([power] * CLASSES, axis=1), 0.0))
    step_all = jnp.concatenate([step_h, step_h, step_l], axis=1)
    for d in range(last):
        if d > 0:
            power_h, power_l = split(power)
            power = dot(step_all, jnp.concatenate([power_h, power_l, power_h], axis=0))
        ms[:, d * 128:(d + 1) * 128] = made(power)

    def operands(coarse):
        high = coarse.astype(BF16).astype(F32)
        low = coarse - high
        here = tiled(left, PLANE)
        turned = turn(high)
        return jnp.concatenate([
            jnp.where(here, high, turn(low)), jnp.where(here, turned, low),
            jnp.where(here, high, 0.0), jnp.where(here, turned, 0.0)], axis=0).astype(BF16)

    def classes(mat, right):
        product = dot(mat, right)
        kinds = jnp.broadcast_to(tab_s[0, 6:7], (COARSE, 128))
        picked = jnp.where(kinds == 0, product[:COARSE], 0.0)
        for cl in range(1, CLASSES):
            picked = jnp.where(kinds == cl, product[cl * COARSE:(cl + 1) * COARSE], picked)
        picked = picked + turn(picked)
        return jnp.where(tiled(left, PLANE), picked[:PLANE], picked[PLANE:])

    even = (sub & 1) == 0

    def restrict(value):
        pairs = value.reshape(4, 2, 2, 2, 8, 128)
        pairs = pairs[:, 0] + pairs[:, 1]
        pairs = pairs[:, :, 0] + pairs[:, :, 1]
        first = pairs[:, 0].reshape(PLANE, 128)
        second = pairs[:, 1].reshape(PLANE, 128)
        return jnp.where(tiled(even, PLANE), first + along_y(first, -1), second + along_y(second, 1))

    def prolong(coarse):
        here = tiled(even, PLANE)
        first = jnp.where(here, coarse, along_y(coarse, 1)).reshape(4, 1, 1, 1, 8, 128)
        second = jnp.where(here, along_y(coarse, -1), coarse).reshape(4, 1, 1, 1, 8, 128)
        both = jnp.concatenate([first, second], axis=2)
        return jnp.broadcast_to(both, (4, 2, 2, 2, 8, 128)).reshape(256, 128)

    def ghost(plane, face, at):
        return jnp.where(tiled(tmask[at, face], PLANE) > 0.0, lanes_from(plane, tidx[at, face]), 0.0)

    def picked_from(value, face, at):
        return jnp.where(
            tiled(tmask[at, face], value.shape[0]) > 0.0, lanes_from(value, tidx[at, face]), 0.0)

    def beside_xy(value, at):
        size = value.shape[0]
        n = size // PLANE
        cube = value.reshape(n, 4, 8, 128)
        part = [cube[:, j].reshape(n * 8, 128) for j in range(4)]
        low = picked_from(part[3], 0, at)
        high = picked_from(part[0], 1, at)
        here = tiled(sub, n * 8)
        edges = along_y(part[0], 1)
        for j in range(1, 8):
            edges = jnp.where(here == j, along_y(part[j % 4], j + 1 if j < 4 else j), edges)
        edges = picked_from(edges, 2, at)
        sums = []
        for j in range(4):
            total = (part[j - 1] if j > 0 else low) + (part[j + 1] if j < 3 else high)
            total = total + jnp.where(here == 0, along_y(edges, -j), along_y(part[j], 1))
            total = total + jnp.where(here == 7, along_y(edges, 3 - j), along_y(part[j], -1))
            sums.append(total.reshape(n, 1, 8, 128))
        return jnp.concatenate(sums, axis=1).reshape(size, 128)

    def inner(value):
        zero = jnp.zeros((PLANE, 128), F32)
        total = beside_xy(value, 0)
        total = total + jnp.concatenate([zero, value[:-PLANE]], axis=0)
        return total + jnp.concatenate([value[PLANE:], zero], axis=0)

    def ended(total, below, above):
        return jnp.concatenate([
            total[:PLANE] + ghost(below, 4, 0), total[PLANE:-PLANE],
            total[-PLANE:] + ghost(above, 5, 0)], axis=0)

    def scaled(which, at, size):
        return tiled(tscale[at, which], size)

    def relax(value, driven, total, at):
        return (1.0 - DAMP) * value + driven + scaled(0, at, value.shape[0]) * total

    def slab_below(slab, driven, own):
        cross = ghost(own[:PLANE], 5, 1)
        near = slab[PLANE:]
        upper = jnp.concatenate([slab[2 * PLANE:], cross], axis=0) if slab.shape[0] > 2 * PLANE else cross
        return relax(near, driven, beside_xy(near, 1) + slab[:-PLANE] + upper, 1)

    def slab_above(slab, driven, own):
        cross = ghost(own[-PLANE:], 4, 2)
        near = slab[:-PLANE]
        lower = jnp.concatenate([cross, slab[:-2 * PLANE]], axis=0) if slab.shape[0] > 2 * PLANE else cross
        return relax(near, driven, beside_xy(near, 2) + slab[PLANE:] + lower, 2)

    def corrected(driven, total, below, above):
        x2 = relax(driven, driven, ended(total, below[-PLANE:], above[:PLANE]), 0)
        below2 = slab_below(below, below[PLANE:], driven)
        above2 = slab_above(above, above[:-PLANE], driven)
        total = ended(inner(x2), below2[-PLANE:], above2[:PLANE])
        rest = driven - DAMP * x2 + scaled(0, 0, 256) * total
        return x2 + prolong(inverse(scaled(2, 0, PLANE) * restrict(rest)))

    def swept(x3, driven, total, below, below_d, above, above_d):
        x4 = relax(x3, driven, ended(total, below[-PLANE:], above[:PLANE]), 0)
        below4 = slab_below(below, below_d, x3)
        above4 = slab_above(above, above_d, x3)
        x5 = relax(x4, driven, ended(inner(x4), below4[-PLANE:], above4[:PLANE]), 0)
        return x4, x5, below4, above4

    exchanged(table_message)
    for side in range(2):
        reached = (s > 0) if side == 0 else (s < n_sp - 1)
        make_tables(1 + side, jnp.where(reached, tab_r[side], -1))

    source_copy(0).wait_recv()
    put_source(0, 0, far[0])
    for off in range(1, n_sp):
        slots_landed(off)
    slots = jnp.sum(jnp.where(spot, slots_in[:, :1], 0.0), axis=2, keepdims=True)
    slots = jnp.broadcast_to(slots, (n_sp, bk, 128)).reshape(rows, 128)
    hit = slots == (iota((rows, 128), 1) & 63).astype(F32)
    place = jnp.sum(jnp.where(hit, iota((rows, 128), 0).astype(F32), 0.0), axis=0, keepdims=True)
    place = jnp.broadcast_to(place, (8, 128)).astype(jnp.int32)

    def settle(given, put):
        tiles = rows // 128
        for tile in range(tiles):
            shuffle[tile * CELLS:(tile + 1) * CELLS] = given[tile * 128:(tile + 1) * 128].T
        for z in range(8):
            plane = None
            for tile in range(tiles):
                both = shuffle[pl.ds(tile * CELLS + z, 64, stride=8), :]
                both = lanes_from(both, place & 127)
                both = jnp.where(tiled(left, PLANE), both[:PLANE], both[PLANE:])
                chosen_tile = tiled(lax.shift_right_logical(place, 7), PLANE) == tile
                plane = both if plane is None else jnp.where(chosen_tile, both, plane)
            put(z, plane)

    for off in range(1, n_sp):
        spread_landed(off)

    def put_start(z, plane):
        bs[z * PLANE:(z + 1) * PLANE] = plane

    settle(br[...].reshape(rows, CELLS), put_start)

    def init_copy():
        return pltpu.make_async_remote_copy(
            src_ref=bs, dst_ref=hand, send_sem=bk_sem.at[0], recv_sem=bq_sem.at[0],
            device_id=(after, s), device_id_type=MESH)

    def guess_copy():
        return pltpu.make_async_remote_copy(
            src_ref=rg_s, dst_ref=rg_r, send_sem=bk_sem.at[1], recv_sem=bq_sem.at[1],
            device_id=(before, s), device_id_type=MESH)

    def mine_copy():
        return pltpu.make_async_remote_copy(
            src_ref=hsrc, dst_ref=mine, send_sem=bk_sem.at[2], recv_sem=bq_sem.at[2],
            device_id=(after, s), device_id_type=MESH)

    ends = ((0, 3 * PLANE), (5 * PLANE, 3 * PLANE))
    middle = ((3 * PLANE, 2 * PLANE),)

    def hand_copy(at):
        first, count = (ends + middle)[at]
        return pltpu.make_async_remote_copy(
            src_ref=hsrc.at[pl.ds(first, count)], dst_ref=hand.at[pl.ds(first, count)],
            send_sem=ts_sem.at[at], recv_sem=tr_sem.at[at], device_id=(lax.rem(k + 2, n_tm), s),
            device_id_type=MESH)

    ahead = (after, k)

    def coarse_copy(it, off):
        return pltpu.make_async_remote_copy(
            src_ref=cs.at[it], dst_ref=cr.at[it, off - 1], send_sem=cs_sem.at[it, off - 1],
            recv_sem=cr_sem.at[it, off - 1], device_id=(lax.rem(ahead[it] + off, n_tm), s), device_id_type=MESH)

    def coarse_landed(it):
        rights = []
        for off in range(1, n_tm):
            if it > 0 or off < last:
                @pl.when(k >= off)
                def _():
                    coarse_copy(it, off).wait_recv()
            rights.append(operands(jnp.where(k >= off, cr[it, off - 1], 0.0)))
        return jnp.concatenate(rights, axis=0)

    def rows_of(part):
        return pl.ds(part[0], part[1])

    def plane_out(state, kept):
        for z in range(8):
            shuffle[pl.ds(z, PLANE, stride=8), :] = state[z * PLANE:(z + 1) * PLANE]
        flat = shuffle[0:256].T
        kept[0] = jnp.concatenate([flat[:64], flat[64:]], axis=1)


    rights = None
    for it in range(ITERS):
        if it == 0:
            drv[0] = scaled(1, 0, 256) * (bs[...] + src[0, 0])
            exchange(first_message(0))
            rg_s[...] = restrict(bs[...])

            @pl.when(k < last)
            def _():
                guess_copy().start()

            @pl.when(k == last)
            def _():
                init_copy().start()
            source_copy(1).wait_recv()
            put_source(0, 1, far[1])
            exchange(source_message(0))
        else:
            rights = coarse_landed(it - 1)
            pushed = prolong(classes(ms[:, :(last - 1) * 128], rights[128:]))
            for parts, wait_for in ((ends, (0, 1)), (middle, (2,))):
                @pl.when(k > 0)
                def _():
                    for at in wait_for:
                        hand_copy(at).wait_recv()

                if parts is ends:
                    @pl.when(k == 0)
                    def _():
                        init_copy().wait_recv()
                for part in parts:
                    first, count = part
                    given = hand[rows_of(part)] + pushed[first:first + count]
                    drv[it, rows_of(part)] = scaled(1, 0, count) * (given + src[1, 0, rows_of(part)])
                if parts is ends:
                    exchange(first_message(it))
            mine_copy().start()
        driven = drv[it]
        total = inner(driven)
        exchanged(first_message(it))
        below_d, above_d = e1[it, 0], e1[it, 1]
        x3a[it] = corrected(driven, total, below_d[PLANE:], above_d[:-PLANE])
        exchange(deep_message(it))
        x3 = x3a[it]
        total = inner(x3)
        exchanged(source_message(it))
        if it > 0:
            @pl.when(k == last)
            def _():
                init_copy().wait_send()
                for off in range(1, n_sp):
                    own_landed(off)
                settle(gr[...].reshape(rows, CELLS), put_start)
        exchanged(deep_message(it))
        below, above = e2[it, 0], e2[it, 1]
        x4, x5, below4, above4 = swept(x3, drv[it], total, below, e1[it, 0], above, e1[it, 1])
        below5 = slab_below(below4, e1[it, 0, PLANE:], x4)
        above5 = slab_above(above4, e1[it, 1, :-PLANE], x4)
        xf[...] = x5
        driven = scaled(1, 0, 256) * (x5 + src[it, 1])
        below_d = scaled(1, 1, 2 * PLANE) * (below5 + srch[it, 0])
        above_d = scaled(1, 2, 2 * PLANE) * (above5 + srch[it, 1])
        drv2[...] = driven
        x3b[it] = corrected(driven, inner(driven), below_d, above_d)
        exchange(second_message(it))
        total = inner(x3b[it])
        if it == 0:
            @pl.when(k != last - 1)
            def _():
                guess_copy().wait_recv()
        else:
            mine_copy().wait_recv()
            st[...] = bs[...] + (prolong(classes(ms[...], rights)) + (mine[...] - bs[...]))
        if it == ITERS - 1:
            plane_out(xf, f_ref)
        exchanged(second_message(it))
        _, x5, _, _ = swept(
            x3b[it], drv2[...], total, e4[it, 0], below_d[PLANE:], e4[it, 1], above_d[:-PLANE])
        if it < ITERS - 1:
            hsrc[...] = x5

            @pl.when(k != last - 1)
            def _():
                cs[it] = restrict(hsrc[...]) - rg_r[...]
                for off in range(1, last):
                    @pl.when(after + off < n_tm)
                    def _():
                        coarse_copy(it, off).start()
                for at in range(3):
                    hand_copy(at).start()

            @pl.when(k == last)
            def _():
                cr[it, last - 1] = cs[it]
                for off in range(1, n_sp):
                    own_copy(off).start()
            exchange(source_message(1))
        else:
            residual = x5 - st[...]
            cs[it] = restrict(residual)
            for off in range(1, n_tm):
                @pl.when(k + off < n_tm)
                def _():
                    coarse_copy(it, off).start()
            rights = coarse_landed(it)
            xf[...] = st[...] + (prolong(classes(ms[...], rights)) + residual)

    plane_out(xf, c_ref)

    for off in range(1, n_sp):
        slots_copy(off).wait_send()
        spread_copy(off).wait_send()
    for fine in range(2):
        source_copy(fine).wait_send()
    mine_copy().wait_send()

    @pl.when(k == last)
    def _():
        for off in range(1, n_sp):
            own_copy(off).wait_send()

    @pl.when(k < last)
    def _():
        guess_copy().wait_send()

    drained(table_message)
    for it in range(ITERS):
        drained(source_message(it))
        drained(first_message(it))
        drained(deep_message(it))
        drained(second_message(it))
    for off in range(1, n_tm):
        @pl.when(k + off < n_tm)
        def _():
            coarse_copy(1, off).wait_send()
    for off in range(1, last):
        @pl.when((k != last - 1) & (after + off < n_tm))
        def _():
            coarse_copy(0, off).wait_send()

    @pl.when(k != last - 1)
    def _():
        for at in range(3):
            hand_copy(at).wait_send()


def solution(mesh):
    n_tm, n_sp = mesh.shape["tm"], mesh.shape["space"]

    def body(init_state, guess, source, remap, neighbors, block_class, step_number, inverse, cstep):
        nb = init_state.shape[0]
        bk = -(-(2 * nb // n_sp) // 8) * 8
        tiles = n_sp * bk // 128
        slots = 3 + 3 * ITERS
        dma = pltpu.SemaphoreType.DMA
        full = 8 * PLANE

        def vmem(*shape, dtype=F32):
            return pltpu.VMEM(shape, dtype)

        return pl.pallas_call(
            functools.partial(kernel, n_tm, n_sp, bk),
            name="mgrit",
            out_shape=(vmem(1, nb, CELLS), vmem(1, nb, CELLS)),
            in_specs=[pl.BlockSpec(memory_space=pl.ANY)] * 9,
            out_specs=[pl.BlockSpec(memory_space=pltpu.VMEM)] * 2,
            scratch_shapes=[
                vmem(nb, CELLS), vmem(1, nb, CELLS), vmem(1, 2, nb, CELLS), vmem(1, nb, dtype=jnp.int32),
                vmem(6, nb, dtype=jnp.int32), vmem(1, nb, dtype=jnp.int32), vmem(1, CLASSES),
                vmem(CLASSES * COARSE, COARSE), vmem(CLASSES * COARSE, COARSE),
                vmem(2, n_sp, bk, CELLS), vmem(n_sp, bk, CELLS), vmem(n_sp, bk, CELLS), vmem(2, nb, CELLS),
                vmem(2, 8, 128, dtype=jnp.int32), vmem(2, 8, 128, dtype=jnp.int32),
                vmem(3, 6, 8, 128, dtype=jnp.int32), vmem(3, 6, 8, 128), vmem(3, 3, 8, 128),
                vmem(ITERS, 2, full, 128), vmem(ITERS, 2, 2 * PLANE, 128), vmem(tiles * CELLS, 128),
                vmem(full, 128), vmem(ITERS, full, 128), vmem(full, 128), vmem(ITERS, full, 128), vmem(ITERS, full, 128),
                vmem(ITERS, 2, 3 * PLANE, 128), vmem(ITERS, 2, 4 * PLANE, 128), vmem(ITERS, 2, 2 * PLANE, 128),
                vmem(full, 128), vmem(full, 128), vmem(full, 128), vmem(full, 128), vmem(full, 128),
                vmem(PLANE, 128), vmem(PLANE, 128),
                vmem(ITERS, PLANE, 128), vmem(ITERS, n_tm - 1, PLANE, 128),
                vmem(4, PLANE, 128), vmem(2 * PLANE, 128), vmem(COARSE, PLANE, 128), vmem(CLASSES * COARSE, (n_tm - 1) * 128, dtype=BF16),
                vmem(n_sp, 8, 128), vmem(n_sp, 8, 128),
                dma((9,)), dma((n_sp,)), dma((n_sp,)),
                dma((n_sp,)), dma((n_sp,)), dma((n_sp,)), dma((n_sp,)),
                dma((slots, 2)), dma((slots, 2)),
                dma((3,)), dma((3,)), dma((3,)), dma((3,)),
                dma((ITERS, n_tm - 1)), dma((ITERS, n_tm - 1)), dma((2,)), dma((2,)),
            ],
            compiler_params=pltpu.CompilerParams(collective_id=0, has_side_effects=True),
        )(
            init_state, guess, source, remap.reshape(1, nb), neighbors.T, block_class.reshape(1, nb),
            step_number.reshape(1, CLASSES), inverse.reshape(CLASSES * COARSE, COARSE),
            cstep.reshape(CLASSES * COARSE, COARSE),
        )

    placed = (
        P("space", None), P("tm", "space", None), P("tm", None, "space", None), P("space"),
        P("space", None), P("space"), P(), P(), P(),
    )
    return jax.shard_map(
        body, mesh=mesh, in_specs=placed,
        out_specs=(P("tm", "space", None), P("tm", "space", None)), check_vma=False,
    )
```

```python
import functools

import jax
import jax.numpy as jnp
from jax import lax
from jax.experimental import pallas as pl
from jax.experimental.pallas import tpu as pltpu
from jax.sharding import PartitionSpec as P

CELLS = 512
COARSE = 64
CLASSES = 4
ITERS = 2
DAMP = 0.8
PLANE = 32
MESH = pl.DeviceIdType.MESH
F32 = jnp.float32
BF16 = jnp.bfloat16


def split(value):
    high = value.astype(BF16)
    return high, (value - high.astype(F32)).astype(BF16)


def dot(left, right):
    return jnp.dot(left, right, preferred_element_type=F32)


def iota(shape, dim):
    return lax.broadcasted_iota(jnp.int32, shape, dim)


def turn(value):
    return pltpu.roll(value, 64, 1)


def along_y(value, shift):
    rows = value.shape[0]
    return pltpu.roll(value.reshape(rows // 8, 8, 128), shift % 8, 1).reshape(rows, 128)


def tiled(table, rows):
    return jnp.broadcast_to(table[None], (rows // 8, 8, 128)).reshape(rows, 128)


def lanes_from(value, index):
    return jnp.take_along_axis(
        value, tiled(index, value.shape[0]), axis=1, mode="promise_in_bounds")


def partner(s, off, n):
    if n & (n - 1):
        return lax.rem(s + off, n)
    to = s
    for bit in range(n.bit_length() - 1):
        if off >> bit & 1:
            to = to + (1 - 2 * lax.rem(lax.div(s, 1 << bit), 2)) * (1 << bit)
    return to


def kernel(
    n_tm, n_sp, bk,
    init_hbm, guess_hbm, source_hbm, remap_hbm, nb_hbm, class_hbm, step_hbm, inv_hbm, cstep_hbm,
    c_ref, f_ref,
    init_ref, guess_ref, source_ref, remap_ref, nb_ref, class_ref, step_ref, inv_ref, cstep_ref,
    gb, br, gr, far, tab_s, tab_r, tidx, tmask, tscale, src, srch, srcf, shuffle,
    bs, drv, drv2, x3a, x3b, e1, e2, e4, st, xf, hsrc, hand, hp, mine, rg_s, rg_r, cs, cr, crn, table, spread_rows, entries, ms,
    slots_out, slots_in, in_sem, so_sem, si_sem,
    gs_sem, gr_sem, ps_sem, br_sem, hs_sem, hr_sem, ts_sem, tr_sem, bk_sem, bq_sem, cs_sem, cr_sem, fs_sem, fr_sem,
    hps_sem, hpr_sem, cns_sem, cnr_sem,
):
    k = lax.axis_index("tm")
    s = lax.axis_index("space")
    nb = init_hbm.shape[0]
    rows = n_sp * bk
    bits = nb.bit_length() - 1
    last = n_tm - 1

    after, before = lax.rem(k + 1, n_tm), lax.rem(k + last, n_tm)

    barrier = pltpu.get_barrier_semaphore()

    def greet(tm, space):
        pl.semaphore_signal(barrier, inc=1, device_id=(tm, space), device_id_type=MESH)

    for off in range(1, n_sp):
        greet(k, partner(s, off, n_sp))
    for off in range(1, n_tm):
        greet(lax.rem(k + off, n_tm), s)

        @pl.when(s > 0)
        def _():
            greet(lax.rem(k + off, n_tm), s - 1)

        @pl.when(s < n_sp - 1)
        def _():
            greet(lax.rem(k + off, n_tm), s + 1)

    loads = [
        pltpu.make_async_copy(given, kept, in_sem.at[at]) for at, (given, kept) in enumerate((
            (remap_hbm, remap_ref), (guess_hbm, guess_ref), (init_hbm, init_ref), (nb_hbm, nb_ref),
            (class_hbm, class_ref), (step_hbm, step_ref), (source_hbm, source_ref), (inv_hbm, inv_ref),
            (cstep_hbm, cstep_ref)))]
    for load in loads:
        load.start()
    loads[0].wait()

    eye = iota((nb, nb), 0) == iota((nb, nb), 1)

    def column(row):
        return jnp.sum(jnp.where(eye, row, 0.0), axis=1, keepdims=True)

    remap_row = remap_ref[...]
    target_row = lax.shift_right_logical(remap_row, bits)
    slot_row = (remap_row - lax.shift_left(target_row, bits)).astype(F32)
    target_f = target_row.astype(F32)
    same = (column(target_f) == target_f) & (iota((nb, nb), 0) < iota((nb, nb), 1))
    pos_row = jnp.sum(jnp.where(same, 1.0, 0.0), axis=0, keepdims=True)
    send_row = target_f * float(bk) + pos_row
    chosen = iota((rows, nb), 0).astype(F32) == send_row
    send_mat = jnp.where(chosen, 1.0, 0.0)
    slot_col = jnp.sum(jnp.where(chosen, slot_row + 1.0, 0.0), axis=1, keepdims=True) - 1.0
    send_mat = jnp.concatenate([send_mat, send_mat], axis=1).astype(BF16)

    def bucketed(value):
        return dot(send_mat, jnp.concatenate(split(value), axis=0)).reshape(n_sp, bk, CELLS)

    spot = iota((n_sp, bk, 128), 1) == iota((n_sp, bk, 128), 2)
    slot_wide = jnp.broadcast_to(slot_col, (rows, 128)).reshape(n_sp, bk, 128)
    slot_lanes = jnp.sum(jnp.where(spot, slot_wide, 0.0), axis=1, keepdims=True)
    slots_out[...] = jnp.broadcast_to(slot_lanes, (n_sp, 8, 128))
    loads[1].wait()
    loads[2].wait()
    gb[0] = bucketed(guess_ref[0])

    @pl.when(k == last)
    def _():
        gb[1] = bucketed(init_ref[...])

    for load in loads[3:6]:
        load.wait()

    linked = nb_ref[...]
    face_no = iota((6, nb), 0)
    run = s + jnp.where(face_no == 4, -1, jnp.where(face_no == 5, 1, 0))
    linked = jnp.where(linked >= 0, linked - run * nb, -1)
    tab_s[0, 0:6] = jnp.concatenate([linked, linked], axis=1)
    kind = class_ref[...]
    tab_s[0, 6:7] = jnp.concatenate([kind, kind], axis=1)
    tab_s[0, 7:8] = jnp.zeros((1, 128), jnp.int32)
    tab_s[1] = tab_s[0]

    beside = jnp.minimum(s, 1) + jnp.minimum(n_sp - 1 - s, 1)
    pl.semaphore_wait(barrier, n_sp - 1 + (n_tm - 1) * (1 + beside))

    up_to = (k, lax.rem(s + 1, n_sp))
    down_to = (k, lax.rem(s + n_sp - 1, n_sp))

    def halo_up(slot, source, target):
        return pltpu.make_async_remote_copy(
            src_ref=source, dst_ref=target, send_sem=hs_sem.at[slot, 0],
            recv_sem=hr_sem.at[slot, 0], device_id=up_to, device_id_type=MESH)

    def halo_down(slot, source, target):
        return pltpu.make_async_remote_copy(
            src_ref=source, dst_ref=target, send_sem=hs_sem.at[slot, 1],
            recv_sem=hr_sem.at[slot, 1], device_id=down_to, device_id_type=MESH)

    def planes_message(slot, state, depth, target):
        size = depth * PLANE
        return (halo_up(slot, state.at[pl.ds(8 * PLANE - size, size)], target.at[0]),
                halo_down(slot, state.at[pl.ds(0, size)], target.at[1]))

    def exchange(message):
        up, down = message

        @pl.when(s < n_sp - 1)
        def _():
            up.start()

        @pl.when(s > 0)
        def _():
            down.start()

    def exchanged(message):
        up, down = message

        @pl.when(s > 0)
        def _():
            up.wait_recv()

        @pl.when(s < n_sp - 1)
        def _():
            down.wait_recv()

    def drained(message):
        up, down = message

        @pl.when(s < n_sp - 1)
        def _():
            up.wait_send()

        @pl.when(s > 0)
        def _():
            down.wait_send()

    table_message = (halo_up(0, tab_s.at[0], tab_r.at[0]), halo_down(0, tab_s.at[1], tab_r.at[1]))

    def source_message(it):
        return planes_message(1 + it, src.at[it, 1], 2, srch.at[it])

    first_source = planes_message(3 + 3 * ITERS, src.at[1, 0], 2, srcf)

    def first_message(it):
        if it == 0:
            return planes_message(3 + 3 * it, drv.at[it], 3, e1.at[it])
        return (halo_up(3 + 3 * it, drv.at[it, pl.ds(5 * PLANE, PLANE)], e1.at[it, 0, pl.ds(0, PLANE)]),
                halo_down(3 + 3 * it, drv.at[it, pl.ds(2 * PLANE, PLANE)], e1.at[it, 1, pl.ds(2 * PLANE, PLANE)]))

    def deep_message(it):
        return planes_message(4 + 3 * it, x3a.at[it], 4, e2.at[it])

    def second_message(it):
        return planes_message(5 + 3 * it, x3b.at[it], 2, e4.at[it])

    which = jnp.maximum(k - last + 1, 0)

    def spread_copy(off):
        to = partner(s, off, n_sp)
        return pltpu.make_async_remote_copy(
            src_ref=gb.at[which, to], dst_ref=br.at[s], send_sem=ps_sem.at[off], recv_sem=br_sem.at[s],
            device_id=(k, to), device_id_type=MESH)

    def spread_landed(off):
        origin = partner(s, off, n_sp)
        pltpu.make_async_remote_copy(
            src_ref=gb.at[0, origin], dst_ref=br.at[origin], send_sem=ps_sem.at[off],
            recv_sem=br_sem.at[origin], device_id=(k, origin), device_id_type=MESH).wait_recv()

    def own_copy(off):
        to = partner(s, off, n_sp)
        return pltpu.make_async_remote_copy(
            src_ref=gb.at[0, to], dst_ref=gr.at[s], send_sem=gs_sem.at[off],
            recv_sem=gr_sem.at[s], device_id=(k, to), device_id_type=MESH)

    def own_landed(off):
        origin = partner(s, off, n_sp)
        pltpu.make_async_remote_copy(
            src_ref=gb.at[0, origin], dst_ref=gr.at[origin],
            send_sem=gs_sem.at[off], recv_sem=gr_sem.at[origin], device_id=(k, origin),
            device_id_type=MESH).wait_recv()

    def slots_copy(off):
        to = partner(s, off, n_sp)
        return pltpu.make_async_remote_copy(
            src_ref=slots_out.at[to], dst_ref=slots_in.at[s], send_sem=so_sem.at[off],
            recv_sem=si_sem.at[s], device_id=(k, to), device_id_type=MESH)

    def slots_landed(off):
        origin = partner(s, off, n_sp)
        pltpu.make_async_remote_copy(
            src_ref=slots_out.at[origin], dst_ref=slots_in.at[origin], send_sem=so_sem.at[off],
            recv_sem=si_sem.at[origin], device_id=(k, origin), device_id_type=MESH).wait_recv()

    for off in reversed(range(1, n_sp)):
        slots_copy(off).start()
    exchange(table_message)
    for off in reversed(range(1, n_sp)):
        spread_copy(off).start()

    def source_copy(fine):
        return pltpu.make_async_remote_copy(
            src_ref=source_ref.at[0, fine], dst_ref=far.at[fine], send_sem=fs_sem.at[fine],
            recv_sem=fr_sem.at[fine], device_id=(before, s), device_id_type=MESH)

    for load in loads[6:]:
        load.wait()
    source_copy(0).start()
    source_copy(1).start()
    br[s] = gb[which, s]
    slots_in[s] = slots_out[s]
    gr[s] = gb[0, s]

    lane = iota((8, 128), 1)
    sub = iota((8, 128), 0)
    left = lane < 64
    half = lane & 64

    def blocks_in_lanes(value):
        return jnp.concatenate([value[:, :CELLS // 2], value[:, CELLS // 2:]], axis=0).T

    def put_source(it, fine, value):
        shuffle[0:256] = blocks_in_lanes(value)
        for z in range(8):
            src[it, fine, z * PLANE:(z + 1) * PLANE] = shuffle[pl.ds(z, PLANE, stride=8), :]

    def make_tables(at, table):
        faces = [jnp.broadcast_to(table[face:face + 1], (8, 128)) for face in range(7)]
        inside = [jnp.maximum(face, 0) for face in faces]
        index = [
            jnp.where(left, inside[0] + 64, lane - 64), jnp.where(left, lane + 64, inside[1]),
            half + jnp.where(sub < 4, inside[2], inside[3]), lane,
            half + inside[4], half + inside[5],
        ]
        known = [jnp.where(face >= 0, 1.0, 0.0) for face in faces[:6]]
        mask = [
            jnp.where(left, known[0], 1.0), jnp.where(left, 1.0, known[1]),
            jnp.where(sub < 4, known[2], known[3]), known[2],
            known[4], known[5],
        ]
        for face in range(6):
            tidx[at, face] = index[face]
            tmask[at, face] = mask[face]
        dif = jnp.zeros((8, 128), F32)
        for cl in range(CLASSES):
            dif = dif + jnp.where(faces[6] == cl, step_ref[:, cl:cl + 1], 0.0)
        tscale[at, 0] = DAMP * dif / (1.0 + 6.0 * dif)
        tscale[at, 1] = DAMP / (1.0 + 6.0 * dif)
        tscale[at, 2] = (1.0 + 6.0 * dif) / DAMP

    make_tables(0, tab_s[0])

    def coarse_of(row):
        high = lax.shift_right_logical(row, 5) * 2 + (row & 1)
        return high * 16 + (lax.shift_right_logical(row, 1) & 3) * 4 + (lax.shift_right_logical(row, 3) & 3)

    size = CLASSES * COARSE
    in_class = (lax.shift_right_logical(iota((size, size), 0), 6)
                == lax.shift_right_logical(iota((size, size), 1), 6))
    tall = jnp.where(in_class & (coarse_of(iota((size, size), 0) & 63) == (iota((size, size), 1) & 63)),
                     1.0, 0.0).astype(BF16)
    wide = jnp.where(coarse_of(iota((COARSE, COARSE), 1)) == iota((COARSE, COARSE), 0), 0.125, 0.0).astype(BF16)

    def made(given):
        parts = [dot(tall, dot(piece, wide).astype(BF16)).astype(BF16) for piece in split(given)]
        return jnp.concatenate(parts, axis=1)

    both = made(inv_ref[...])
    lanes = CLASSES * 2 * COARSE
    blocks = [
        jnp.concatenate([both[at * PLANE:(at + 1) * PLANE, part * COARSE:(part + 1) * COARSE]
                         for at in range(2 * CLASSES)], axis=1) for part in range(2)]
    at_row, at_lane = iota((lanes, lanes), 0), iota((lanes, lanes), 1)
    place_of = ((at_row & 63) * 8 + (lax.shift_right_logical(at_row, 6) & 1) * 4
                + lax.shift_right_logical(at_row, 7))
    moved = dot(jnp.concatenate(blocks, axis=0), jnp.where(place_of == at_lane, 1.0, 0.0).astype(BF16))
    moved = moved[:PLANE] + moved[PLANE:]
    for group in range(4):
        table[group] = moved[:, group * 128:(group + 1) * 128]
    start = jnp.broadcast_to(tab_s[0, 6:7], (8, 128)) + lax.shift_right_logical(lane, 6) * 4

    def make_entries(i, carry):
        for group in range(4):
            entries[group * 16 + i] = lanes_from(table[group], start + 8 * i)
        return carry

    lax.fori_loop(0, 16, make_entries, 0)


    def inverse(coarse):
        here = tiled(left, PLANE)
        turned = turn(coarse)
        spread_rows[:PLANE] = jnp.where(here, coarse, turned)
        spread_rows[PLANE:] = jnp.where(here, turned, coarse)

        def add(step, sums):
            first, second = sums
            for j in range(0, 8, 2):
                first = first + entries[8 * step + j] * spread_rows[pl.ds(8 * step + j, 1)]
                second = second + entries[8 * step + j + 1] * spread_rows[pl.ds(8 * step + j + 1, 1)]
            return first, second

        zero = jnp.zeros((PLANE, 128), F32)
        first, second = lax.fori_loop(0, 8, add, (zero, zero), unroll=True)
        return first + second

    def make_steps():
        power = cstep_ref[...]
        step_h, step_l = split(jnp.where(in_class, jnp.concatenate([power] * CLASSES, axis=1), 0.0))
        step_all = jnp.concatenate([step_h, step_h, step_l], axis=1)
        for d in range(last):
            if d > 0:
                power_h, power_l = split(power)
                power = dot(step_all, jnp.concatenate([power_h, power_l, power_h], axis=0))
            ms[:, d * 128:(d + 1) * 128] = made(power)

    def operands(coarse):
        high = coarse.astype(BF16).astype(F32)
        low = coarse - high
        here = tiled(left, PLANE)
        turned = turn(high)
        return jnp.concatenate([
            jnp.where(here, high, turn(low)), jnp.where(here, turned, low),
            jnp.where(here, high, 0.0), jnp.where(here, turned, 0.0)], axis=0).astype(BF16)

    def selected(product, kinds):
        kinds = jnp.broadcast_to(kinds, (COARSE, 128))
        picked = jnp.where(kinds == 0, product[:COARSE], 0.0)
        for cl in range(1, CLASSES):
            picked = jnp.where(kinds == cl, product[cl * COARSE:(cl + 1) * COARSE], picked)
        picked = picked + turn(picked)
        return jnp.where(tiled(left, PLANE), picked[:PLANE], picked[PLANE:])

    def classes(mat, right):
        return selected(dot(mat, right), tab_s[0, 6:7])

    even = (sub & 1) == 0

    def restrict(value):
        pairs = value.reshape(4, 2, 2, 2, 8, 128)
        pairs = pairs[:, 0] + pairs[:, 1]
        pairs = pairs[:, :, 0] + pairs[:, :, 1]
        first = pairs[:, 0].reshape(PLANE, 128)
        second = pairs[:, 1].reshape(PLANE, 128)
        return jnp.where(tiled(even, PLANE), first + along_y(first, -1), second + along_y(second, 1))

    def prolong(coarse):
        here = tiled(even, PLANE)
        first = jnp.where(here, coarse, along_y(coarse, 1)).reshape(4, 1, 1, 1, 8, 128)
        second = jnp.where(here, along_y(coarse, -1), coarse).reshape(4, 1, 1, 1, 8, 128)
        both = jnp.concatenate([first, second], axis=2)
        return jnp.broadcast_to(both, (4, 2, 2, 2, 8, 128)).reshape(256, 128)

    def ghost(plane, face, at):
        return jnp.where(tiled(tmask[at, face], PLANE) > 0.0, lanes_from(plane, tidx[at, face]), 0.0)

    def picked_from(value, face, at):
        return jnp.where(
            tiled(tmask[at, face], value.shape[0]) > 0.0, lanes_from(value, tidx[at, face]), 0.0)

    def beside_xy(value, at):
        size = value.shape[0]
        n = size // PLANE
        cube = value.reshape(n, 4, 8, 128)
        part = [cube[:, j].reshape(n * 8, 128) for j in range(4)]
        low = picked_from(part[3], 0, at)
        high = picked_from(part[0], 1, at)
        here = tiled(sub, n * 8)
        edges = along_y(part[0], 1)
        for j in range(1, 8):
            edges = jnp.where(here == j, along_y(part[j % 4], j + 1 if j < 4 else j), edges)
        edges = picked_from(edges, 2, at)
        sums = []
        for j in range(4):
            total = (part[j - 1] if j > 0 else low) + (part[j + 1] if j < 3 else high)
            total = total + jnp.where(here == 0, along_y(edges, -j), along_y(part[j], 1))
            total = total + jnp.where(here == 7, along_y(edges, 3 - j), along_y(part[j], -1))
            sums.append(total.reshape(n, 1, 8, 128))
        return jnp.concatenate(sums, axis=1).reshape(size, 128)

    def inner(value):
        zero = jnp.zeros((PLANE, 128), F32)
        total = beside_xy(value, 0)
        total = total + jnp.concatenate([zero, value[:-PLANE]], axis=0)
        return total + jnp.concatenate([value[PLANE:], zero], axis=0)

    def ended(total, below, above):
        return jnp.concatenate([
            total[:PLANE] + ghost(below, 4, 0), total[PLANE:-PLANE],
            total[-PLANE:] + ghost(above, 5, 0)], axis=0)

    def scaled(which, at, size):
        return tiled(tscale[at, which], size)

    def relax(value, driven, total, at):
        return (1.0 - DAMP) * value + driven + scaled(0, at, value.shape[0]) * total

    def slab_below(slab, driven, own):
        cross = ghost(own[:PLANE], 5, 1)
        near = slab[PLANE:]
        upper = jnp.concatenate([slab[2 * PLANE:], cross], axis=0) if slab.shape[0] > 2 * PLANE else cross
        return relax(near, driven, beside_xy(near, 1) + slab[:-PLANE] + upper, 1)

    def slab_above(slab, driven, own):
        cross = ghost(own[-PLANE:], 4, 2)
        near = slab[:-PLANE]
        lower = jnp.concatenate([cross, slab[:-2 * PLANE]], axis=0) if slab.shape[0] > 2 * PLANE else cross
        return relax(near, driven, beside_xy(near, 2) + slab[PLANE:] + lower, 2)

    def corrected(driven, total, below, above):
        x2 = relax(driven, driven, ended(total, below[-PLANE:], above[:PLANE]), 0)
        below2 = slab_below(below, below[PLANE:], driven)
        above2 = slab_above(above, above[:-PLANE], driven)
        total = ended(inner(x2), below2[-PLANE:], above2[:PLANE])
        rest = driven - DAMP * x2 + scaled(0, 0, 256) * total
        return x2 + prolong(inverse(scaled(2, 0, PLANE) * restrict(rest)))

    def swept(x3, driven, total, below, below_d, above, above_d):
        x4 = relax(x3, driven, ended(total, below[-PLANE:], above[:PLANE]), 0)
        below4 = slab_below(below, below_d, x3)
        above4 = slab_above(above, above_d, x3)
        x5 = relax(x4, driven, ended(inner(x4), below4[-PLANE:], above4[:PLANE]), 0)
        return x4, x5, below4, above4

    exchanged(table_message)
    for side in range(2):
        reached = (s > 0) if side == 0 else (s < n_sp - 1)
        make_tables(1 + side, jnp.where(reached, tab_r[side], -1))

    for off in range(1, n_sp):
        slots_landed(off)
    slots = jnp.sum(jnp.where(spot, slots_in[:, :1], 0.0), axis=2, keepdims=True)
    slots = jnp.broadcast_to(slots, (n_sp, bk, 128)).reshape(rows, 128)
    hit = slots == (iota((rows, 128), 1) & 63).astype(F32)
    place = jnp.sum(jnp.where(hit, iota((rows, 128), 0).astype(F32), 0.0), axis=0, keepdims=True)
    place = jnp.broadcast_to(place, (8, 128)).astype(jnp.int32)

    source_copy(0).wait_recv()
    put_source(0, 0, far[0])

    def settle(given, put):
        tiles = rows // 128
        for tile in range(tiles):
            shuffle[tile * CELLS:(tile + 1) * CELLS] = given[tile * 128:(tile + 1) * 128].T
        for z in range(8):
            plane = None
            for tile in range(tiles):
                both = shuffle[pl.ds(tile * CELLS + z, 64, stride=8), :]
                both = lanes_from(both, place & 127)
                both = jnp.where(tiled(left, PLANE), both[:PLANE], both[PLANE:])
                chosen_tile = tiled(lax.shift_right_logical(place, 7), PLANE) == tile
                plane = both if plane is None else jnp.where(chosen_tile, both, plane)
            put(z, plane)

    for off in range(1, n_sp):
        spread_landed(off)

    def put_start(z, plane):
        bs[z * PLANE:(z + 1) * PLANE] = plane

    settle(br[...].reshape(rows, CELLS), put_start)

    def init_copy():
        return pltpu.make_async_remote_copy(
            src_ref=bs, dst_ref=hand, send_sem=bk_sem.at[0], recv_sem=bq_sem.at[0],
            device_id=(after, s), device_id_type=MESH)

    def guess_copy():
        return pltpu.make_async_remote_copy(
            src_ref=rg_s, dst_ref=rg_r, send_sem=bk_sem.at[1], recv_sem=bq_sem.at[1],
            device_id=(before, s), device_id_type=MESH)

    def mine_copy():
        return pltpu.make_async_remote_copy(
            src_ref=hsrc, dst_ref=mine, send_sem=bk_sem.at[2], recv_sem=bq_sem.at[2],
            device_id=(after, s), device_id_type=MESH)

    def hand_copy():
        return pltpu.make_async_remote_copy(
            src_ref=hsrc, dst_ref=hand, send_sem=ts_sem.at[0], recv_sem=tr_sem.at[0],
            device_id=(lax.rem(k + 2, n_tm), s), device_id_type=MESH)

    def edges_message(state, col, at):
        up = pltpu.make_async_remote_copy(
            src_ref=state.at[pl.ds(6 * PLANE, 2 * PLANE)], dst_ref=hp.at[0], send_sem=hps_sem.at[at, 0],
            recv_sem=hpr_sem.at[0], device_id=(col, lax.rem(s + 1, n_sp)), device_id_type=MESH)
        down = pltpu.make_async_remote_copy(
            src_ref=state.at[pl.ds(0, 2 * PLANE)], dst_ref=hp.at[1], send_sem=hps_sem.at[at, 1],
            recv_sem=hpr_sem.at[1], device_id=(col, lax.rem(s + n_sp - 1, n_sp)), device_id_type=MESH)
        return up, down

    def hand_edges():
        return edges_message(hsrc, lax.rem(k + 2, n_tm), 0)

    def init_edges():
        return edges_message(bs, after, 1)

    def coarse_beside(off):
        col = lax.rem(after + off, n_tm)
        up = pltpu.make_async_remote_copy(
            src_ref=cs.at[0], dst_ref=crn.at[0, off - 2], send_sem=cns_sem.at[0, off - 2],
            recv_sem=cnr_sem.at[0, off - 2], device_id=(col, lax.rem(s + 1, n_sp)), device_id_type=MESH)
        down = pltpu.make_async_remote_copy(
            src_ref=cs.at[0], dst_ref=crn.at[1, off - 2], send_sem=cns_sem.at[1, off - 2],
            recv_sem=cnr_sem.at[1, off - 2], device_id=(col, lax.rem(s + n_sp - 1, n_sp)), device_id_type=MESH)
        return up, down

    def beside_landed():
        sides = []
        for side, reached in ((0, s > 0), (1, s < n_sp - 1)):
            rights = []
            for off in range(2, n_tm):
                there = (k >= off) & reached

                @pl.when(there)
                def _():
                    coarse_beside(off)[side].wait_recv()
                rights.append(operands(jnp.where(there, crn[side, off - 2], 0.0)))
            sides.append(jnp.concatenate(rights, axis=0))
        return sides

    def one_plane(coarse):
        first = jnp.where(even, coarse, along_y(coarse, 1))
        second = jnp.where(even, along_y(coarse, -1), coarse)
        return jnp.concatenate([first, first, second, second], axis=0)

    ahead = (after, k)

    def coarse_copy(it, off):
        return pltpu.make_async_remote_copy(
            src_ref=cs.at[it], dst_ref=cr.at[it, off - 1], send_sem=cs_sem.at[it, off - 1],
            recv_sem=cr_sem.at[it, off - 1], device_id=(lax.rem(ahead[it] + off, n_tm), s), device_id_type=MESH)

    def coarse_landed(it):
        rights = []
        for off in range(1, n_tm):
            if it > 0 or off < last:
                @pl.when(k >= off)
                def _():
                    coarse_copy(it, off).wait_recv()
            rights.append(operands(jnp.where(k >= off, cr[it, off - 1], 0.0)))
        return jnp.concatenate(rights, axis=0)

    def plane_out(state, kept):
        for z in range(8):
            shuffle[pl.ds(z, PLANE, stride=8), :] = state[z * PLANE:(z + 1) * PLANE]
        flat = shuffle[0:256].T
        kept[0] = jnp.concatenate([flat[:64], flat[64:]], axis=1)


    rights = None
    for it in range(ITERS):
        if it == 0:
            drv[0] = scaled(1, 0, 256) * (bs[...] + src[0, 0])
            exchange(first_message(0))
            rg_s[...] = restrict(bs[...])

            @pl.when(k < last)
            def _():
                guess_copy().start()

            @pl.when(k == last)
            def _():
                init_copy().start()
                exchange(init_edges())
        else:
            rights = coarse_landed(it - 1)
            beside_rights = beside_landed()
            product = dot(
                ms[:, :(last - 1) * 128], jnp.concatenate([rights[128:], *beside_rights], axis=1))
            pushed = prolong(selected(product[:, :128], tab_s[0, 6:7]))
            pushed_b = one_plane(selected(product[:, 128:256], tab_r[0, 6:7])[3 * 8:])
            pushed_a = one_plane(selected(product[:, 256:], tab_r[1, 6:7])[:8])
            exchanged(first_source)
            exchanged(hand_edges())
            below_d = scaled(1, 1, 2 * PLANE) * (hp[0] + jnp.concatenate([pushed_b] * 2, axis=0) + srcf[0])
            above_d = scaled(1, 2, 2 * PLANE) * (hp[1] + jnp.concatenate([pushed_a] * 2, axis=0) + srcf[1])
            e1[it, 0, PLANE:] = below_d
            e1[it, 1, :2 * PLANE] = above_d

            @pl.when(k > 0)
            def _():
                hand_copy().wait_recv()

            @pl.when(k == 0)
            def _():
                init_copy().wait_recv()
            drv[it] = scaled(1, 0, 256) * (hand[...] + pushed + src[1, 0])
            exchange(first_message(it))
            mine_copy().start()
        driven = drv[it]
        total = inner(driven)
        if it == 0:
            source_copy(1).wait_recv()
            put_source(0, 1, far[1])
            exchange(source_message(0))
            exchanged(first_message(it))
            below_d, above_d = e1[it, 0, PLANE:], e1[it, 1, :-PLANE]
        x3a[it] = corrected(driven, total, below_d, above_d)
        exchange(deep_message(it))
        x3 = x3a[it]
        total = inner(x3)
        if it == 0:
            make_steps()
        exchanged(source_message(it))
        if it > 0:
            @pl.when(k == last)
            def _():
                init_copy().wait_send()
                drained(init_edges())
                for off in range(1, n_sp):
                    own_landed(off)
                settle(gr[...].reshape(rows, CELLS), put_start)
        if it > 0:
            exchanged(first_message(it))
        exchanged(deep_message(it))
        below, above = e2[it, 0], e2[it, 1]
        x4, x5, below4, above4 = swept(x3, drv[it], total, below, e1[it, 0], above, e1[it, 1])
        below5 = slab_below(below4, e1[it, 0, PLANE:], x4)
        above5 = slab_above(above4, e1[it, 1, :-PLANE], x4)
        xf[...] = x5
        driven = scaled(1, 0, 256) * (x5 + src[it, 1])
        below_d = scaled(1, 1, 2 * PLANE) * (below5 + srch[it, 0])
        above_d = scaled(1, 2, 2 * PLANE) * (above5 + srch[it, 1])
        drv2[...] = driven
        x3b[it] = corrected(driven, inner(driven), below_d, above_d)
        exchange(second_message(it))
        total = inner(x3b[it])
        if it == 0:
            for fine in range(2):
                put_source(1, fine, source_ref[0, fine])
            exchange(first_source)

            @pl.when(k != last - 1)
            def _():
                guess_copy().wait_recv()
        else:
            mine_copy().wait_recv()
            st[...] = bs[...] + (prolong(classes(ms[...], rights)) + (mine[...] - bs[...]))
        if it == ITERS - 1:
            plane_out(xf, f_ref)
        exchanged(second_message(it))
        _, x5, _, _ = swept(
            x3b[it], drv2[...], total, e4[it, 0], below_d[PLANE:], e4[it, 1], above_d[:-PLANE])
        if it < ITERS - 1:
            hsrc[...] = x5

            @pl.when(k != last - 1)
            def _():
                cs[it] = restrict(hsrc[...]) - rg_r[...]
                for off in range(1, last):
                    @pl.when(after + off < n_tm)
                    def _():
                        coarse_copy(it, off).start()
                for off in range(2, n_tm):
                    @pl.when(after + off < n_tm)
                    def _():
                        exchange(coarse_beside(off))
                exchange(hand_edges())
                hand_copy().start()

            @pl.when(k == last)
            def _():
                cr[it, last - 1] = cs[it]
                for off in range(1, n_sp):
                    own_copy(off).start()
            exchange(source_message(1))
        else:
            residual = x5 - st[...]
            cs[it] = restrict(residual)
            for off in range(1, n_tm):
                @pl.when(k + off < n_tm)
                def _():
                    coarse_copy(it, off).start()
            rights = coarse_landed(it)
            xf[...] = st[...] + (prolong(classes(ms[...], rights)) + residual)

    plane_out(xf, c_ref)

    for off in range(1, n_sp):
        slots_copy(off).wait_send()
        spread_copy(off).wait_send()
    for fine in range(2):
        source_copy(fine).wait_send()
    mine_copy().wait_send()

    @pl.when(k == last)
    def _():
        for off in range(1, n_sp):
            own_copy(off).wait_send()

    @pl.when(k < last)
    def _():
        guess_copy().wait_send()

    drained(table_message)
    drained(first_source)
    for it in range(ITERS):
        drained(source_message(it))
        drained(first_message(it))
        drained(deep_message(it))
        drained(second_message(it))
    for off in range(1, n_tm):
        @pl.when(k + off < n_tm)
        def _():
            coarse_copy(1, off).wait_send()
    for off in range(1, last):
        @pl.when((k != last - 1) & (after + off < n_tm))
        def _():
            coarse_copy(0, off).wait_send()

    @pl.when(k != last - 1)
    def _():
        hand_copy().wait_send()
        drained(hand_edges())
        for off in range(2, n_tm):
            @pl.when(after + off < n_tm)
            def _():
                drained(coarse_beside(off))


def solution(mesh):
    n_tm, n_sp = mesh.shape["tm"], mesh.shape["space"]

    def body(init_state, guess, source, remap, neighbors, block_class, step_number, inverse, cstep):
        nb = init_state.shape[0]
        bk = -(-(2 * nb // n_sp) // 8) * 8
        tiles = n_sp * bk // 128
        slots = 4 + 3 * ITERS
        dma = pltpu.SemaphoreType.DMA
        full = 8 * PLANE

        def vmem(*shape, dtype=F32):
            return pltpu.VMEM(shape, dtype)

        return pl.pallas_call(
            functools.partial(kernel, n_tm, n_sp, bk),
            name="mgrit",
            out_shape=(vmem(1, nb, CELLS), vmem(1, nb, CELLS)),
            in_specs=[pl.BlockSpec(memory_space=pl.ANY)] * 9,
            out_specs=[pl.BlockSpec(memory_space=pltpu.VMEM)] * 2,
            scratch_shapes=[
                vmem(nb, CELLS), vmem(1, nb, CELLS), vmem(1, 2, nb, CELLS), vmem(1, nb, dtype=jnp.int32),
                vmem(6, nb, dtype=jnp.int32), vmem(1, nb, dtype=jnp.int32), vmem(1, CLASSES),
                vmem(CLASSES * COARSE, COARSE), vmem(CLASSES * COARSE, COARSE),
                vmem(2, n_sp, bk, CELLS), vmem(n_sp, bk, CELLS), vmem(n_sp, bk, CELLS), vmem(2, nb, CELLS),
                vmem(2, 8, 128, dtype=jnp.int32), vmem(2, 8, 128, dtype=jnp.int32),
                vmem(3, 6, 8, 128, dtype=jnp.int32), vmem(3, 6, 8, 128), vmem(3, 3, 8, 128),
                vmem(ITERS, 2, full, 128), vmem(ITERS, 2, 2 * PLANE, 128), vmem(2, 2 * PLANE, 128), vmem(tiles * CELLS, 128),
                vmem(full, 128), vmem(ITERS, full, 128), vmem(full, 128), vmem(ITERS, full, 128), vmem(ITERS, full, 128),
                vmem(ITERS, 2, 3 * PLANE, 128), vmem(ITERS, 2, 4 * PLANE, 128), vmem(ITERS, 2, 2 * PLANE, 128),
                vmem(full, 128), vmem(full, 128), vmem(full, 128), vmem(full, 128), vmem(2, 2 * PLANE, 128), vmem(full, 128),
                vmem(PLANE, 128), vmem(PLANE, 128),
                vmem(ITERS, PLANE, 128), vmem(ITERS, n_tm - 1, PLANE, 128), vmem(2, n_tm - 2, PLANE, 128),
                vmem(4, PLANE, 128), vmem(2 * PLANE, 128), vmem(COARSE, PLANE, 128), vmem(CLASSES * COARSE, (n_tm - 1) * 128, dtype=BF16),
                vmem(n_sp, 8, 128), vmem(n_sp, 8, 128),
                dma((9,)), dma((n_sp,)), dma((n_sp,)),
                dma((n_sp,)), dma((n_sp,)), dma((n_sp,)), dma((n_sp,)),
                dma((slots, 2)), dma((slots, 2)),
                dma((1,)), dma((1,)), dma((3,)), dma((3,)),
                dma((ITERS, n_tm - 1)), dma((ITERS, n_tm - 1)), dma((2,)), dma((2,)),
                dma((2, 2)), dma((2,)), dma((2, n_tm - 2)), dma((2, n_tm - 2)),
            ],
            compiler_params=pltpu.CompilerParams(collective_id=0, has_side_effects=True),
        )(
            init_state, guess, source, remap.reshape(1, nb), neighbors.T, block_class.reshape(1, nb),
            step_number.reshape(1, CLASSES), inverse.reshape(CLASSES * COARSE, COARSE),
            cstep.reshape(CLASSES * COARSE, COARSE),
        )

    placed = (
        P("space", None), P("tm", "space", None), P("tm", None, "space", None), P("space"),
        P("space", None), P("space"), P(), P(), P(),
    )
    return jax.shard_map(
        body, mesh=mesh, in_specs=placed,
        out_specs=(P("tm", "space", None), P("tm", "space", None)), check_vma=False,
    )
```

```python
import functools

import jax
import jax.numpy as jnp
from jax import lax
from jax.experimental import pallas as pl
from jax.experimental.pallas import tpu as pltpu
from jax.sharding import PartitionSpec as P

CELLS = 512
COARSE = 64
CLASSES = 4
ITERS = 2
DAMP = 0.8
PLANE = 32
MESH = pl.DeviceIdType.MESH
F32 = jnp.float32
BF16 = jnp.bfloat16


def split(value):
    high = value.astype(BF16)
    return high, (value - high.astype(F32)).astype(BF16)


def dot(left, right):
    return jnp.dot(left, right, preferred_element_type=F32)


def iota(shape, dim):
    return lax.broadcasted_iota(jnp.int32, shape, dim)


def turn(value):
    return pltpu.roll(value, 64, 1)


def along_y(value, shift):
    rows = value.shape[0]
    return pltpu.roll(value.reshape(rows // 8, 8, 128), shift % 8, 1).reshape(rows, 128)


def tiled(table, rows):
    return jnp.broadcast_to(table[None], (rows // 8, 8, 128)).reshape(rows, 128)


def lanes_from(value, index):
    return jnp.take_along_axis(
        value, tiled(index, value.shape[0]), axis=1, mode="promise_in_bounds")


def partner(s, off, n):
    if n & (n - 1):
        return lax.rem(s + off, n)
    to = s
    for bit in range(n.bit_length() - 1):
        if off >> bit & 1:
            to = to + (1 - 2 * lax.rem(lax.div(s, 1 << bit), 2)) * (1 << bit)
    return to


def kernel(
    n_tm, n_sp, bk,
    init_hbm, guess_hbm, source_hbm, remap_hbm, nb_hbm, class_hbm, step_hbm, inv_hbm, cstep_hbm,
    c_ref, f_ref,
    init_ref, guess_ref, source_ref, remap_ref, nb_ref, class_ref, step_ref, inv_ref, cstep_ref,
    gb, br, gr, far, tab_s, tab_r, tidx, tmask, tscale, src, srch, srcf, shuffle,
    bs, drv, x3a, x3b, e1, e2, e4, st, xf, hsrc, hand, hp, mine, rg_s, rg_r, cs, cr, crn, table, spread_rows, entries, ms,
    slots_out, slots_in, in_sem, so_sem, si_sem,
    gs_sem, gr_sem, ps_sem, br_sem, hs_sem, hr_sem, ts_sem, tr_sem, bk_sem, bq_sem, cs_sem, cr_sem, fs_sem, fr_sem,
    hps_sem, hpr_sem, cns_sem, cnr_sem,
):
    k = lax.axis_index("tm")
    s = lax.axis_index("space")
    nb = init_hbm.shape[0]
    rows = n_sp * bk
    bits = nb.bit_length() - 1
    last = n_tm - 1

    after, before = lax.rem(k + 1, n_tm), lax.rem(k + last, n_tm)

    barrier = pltpu.get_barrier_semaphore()

    def greet(tm, space):
        pl.semaphore_signal(barrier, inc=1, device_id=(tm, space), device_id_type=MESH)

    for off in range(1, n_sp):
        greet(k, partner(s, off, n_sp))
    for off in range(1, n_tm):
        greet(lax.rem(k + off, n_tm), s)

        @pl.when(s > 0)
        def _():
            greet(lax.rem(k + off, n_tm), s - 1)

        @pl.when(s < n_sp - 1)
        def _():
            greet(lax.rem(k + off, n_tm), s + 1)

    loads = [
        pltpu.make_async_copy(given, kept, in_sem.at[at]) for at, (given, kept) in enumerate((
            (remap_hbm, remap_ref), (guess_hbm, guess_ref), (init_hbm, init_ref), (nb_hbm, nb_ref),
            (class_hbm, class_ref), (step_hbm, step_ref), (source_hbm, source_ref), (inv_hbm, inv_ref),
            (cstep_hbm, cstep_ref)))]
    for load in loads:
        load.start()
    loads[0].wait()

    eye = iota((nb, nb), 0) == iota((nb, nb), 1)

    def column(row):
        return jnp.sum(jnp.where(eye, row, 0.0), axis=1, keepdims=True)

    remap_row = remap_ref[...]
    target_row = lax.shift_right_logical(remap_row, bits)
    slot_row = (remap_row - lax.shift_left(target_row, bits)).astype(F32)
    target_f = target_row.astype(F32)
    same = (column(target_f) == target_f) & (iota((nb, nb), 0) < iota((nb, nb), 1))
    pos_row = jnp.sum(jnp.where(same, 1.0, 0.0), axis=0, keepdims=True)
    send_row = target_f * float(bk) + pos_row
    chosen = iota((rows, nb), 0).astype(F32) == send_row
    send_mat = jnp.where(chosen, 1.0, 0.0)
    slot_col = jnp.sum(jnp.where(chosen, slot_row + 1.0, 0.0), axis=1, keepdims=True) - 1.0
    send_mat = jnp.concatenate([send_mat, send_mat], axis=1).astype(BF16)

    def bucketed(value):
        return dot(send_mat, jnp.concatenate(split(value), axis=0)).reshape(n_sp, bk, CELLS)

    spot = iota((n_sp, bk, 128), 1) == iota((n_sp, bk, 128), 2)
    slot_wide = jnp.broadcast_to(slot_col, (rows, 128)).reshape(n_sp, bk, 128)
    slot_lanes = jnp.sum(jnp.where(spot, slot_wide, 0.0), axis=1, keepdims=True)
    slots_out[...] = jnp.broadcast_to(slot_lanes, (n_sp, 8, 128))
    loads[1].wait()
    loads[2].wait()
    gb[0] = bucketed(guess_ref[0])

    @pl.when(k == last)
    def _():
        gb[1] = bucketed(init_ref[...])

    for load in loads[3:6]:
        load.wait()

    linked = nb_ref[...]
    face_no = iota((6, nb), 0)
    run = s + jnp.where(face_no == 4, -1, jnp.where(face_no == 5, 1, 0))
    linked = jnp.where(linked >= 0, linked - run * nb, -1)
    tab_s[0, 0:6] = jnp.concatenate([linked, linked], axis=1)
    kind = class_ref[...]
    tab_s[0, 6:7] = jnp.concatenate([kind, kind], axis=1)
    tab_s[0, 7:8] = jnp.zeros((1, 128), jnp.int32)
    tab_s[1] = tab_s[0]

    beside = jnp.minimum(s, 1) + jnp.minimum(n_sp - 1 - s, 1)
    pl.semaphore_wait(barrier, n_sp - 1 + (n_tm - 1) * (1 + beside))

    up_to = (k, lax.rem(s + 1, n_sp))
    down_to = (k, lax.rem(s + n_sp - 1, n_sp))

    def halo_up(slot, source, target):
        return pltpu.make_async_remote_copy(
            src_ref=source, dst_ref=target, send_sem=hs_sem.at[slot, 0],
            recv_sem=hr_sem.at[slot, 0], device_id=up_to, device_id_type=MESH)

    def halo_down(slot, source, target):
        return pltpu.make_async_remote_copy(
            src_ref=source, dst_ref=target, send_sem=hs_sem.at[slot, 1],
            recv_sem=hr_sem.at[slot, 1], device_id=down_to, device_id_type=MESH)

    def planes_message(slot, state, depth, target):
        size = depth * PLANE
        return (halo_up(slot, state.at[pl.ds(8 * PLANE - size, size)], target.at[0]),
                halo_down(slot, state.at[pl.ds(0, size)], target.at[1]))

    def exchange(message):
        up, down = message

        @pl.when(s < n_sp - 1)
        def _():
            up.start()

        @pl.when(s > 0)
        def _():
            down.start()

    def exchanged(message):
        up, down = message

        @pl.when(s > 0)
        def _():
            up.wait_recv()

        @pl.when(s < n_sp - 1)
        def _():
            down.wait_recv()

    def drained(message):
        up, down = message

        @pl.when(s < n_sp - 1)
        def _():
            up.wait_send()

        @pl.when(s > 0)
        def _():
            down.wait_send()

    table_message = (halo_up(0, tab_s.at[0], tab_r.at[0]), halo_down(0, tab_s.at[1], tab_r.at[1]))

    def source_message(it):
        return planes_message(1 + it, src.at[it, 1], 2, srch.at[it])

    first_source = planes_message(3 + 3 * ITERS, src.at[1, 0], 2, srcf)

    def first_message(it):
        if it == 0:
            return planes_message(3 + 3 * it, drv.at[it], 3, e1.at[it])
        return (halo_up(3 + 3 * it, drv.at[it, pl.ds(5 * PLANE, PLANE)], e1.at[it, 0, pl.ds(0, PLANE)]),
                halo_down(3 + 3 * it, drv.at[it, pl.ds(2 * PLANE, PLANE)], e1.at[it, 1, pl.ds(2 * PLANE, PLANE)]))

    def deep_message(it):
        return planes_message(4 + 3 * it, x3a.at[it], 4, e2.at[it])

    def second_message(it):
        return planes_message(5 + 3 * it, x3b.at[it], 2, e4.at[it])

    which = jnp.maximum(k - last + 1, 0)

    def spread_copy(off):
        to = partner(s, off, n_sp)
        return pltpu.make_async_remote_copy(
            src_ref=gb.at[which, to], dst_ref=br.at[s], send_sem=ps_sem.at[off], recv_sem=br_sem.at[s],
            device_id=(k, to), device_id_type=MESH)

    def spread_landed(off):
        origin = partner(s, off, n_sp)
        pltpu.make_async_remote_copy(
            src_ref=gb.at[0, origin], dst_ref=br.at[origin], send_sem=ps_sem.at[off],
            recv_sem=br_sem.at[origin], device_id=(k, origin), device_id_type=MESH).wait_recv()

    def own_copy(off):
        to = partner(s, off, n_sp)
        return pltpu.make_async_remote_copy(
            src_ref=gb.at[0, to], dst_ref=gr.at[s], send_sem=gs_sem.at[off],
            recv_sem=gr_sem.at[s], device_id=(k, to), device_id_type=MESH)

    def own_landed(off):
        origin = partner(s, off, n_sp)
        pltpu.make_async_remote_copy(
            src_ref=gb.at[0, origin], dst_ref=gr.at[origin],
            send_sem=gs_sem.at[off], recv_sem=gr_sem.at[origin], device_id=(k, origin),
            device_id_type=MESH).wait_recv()

    def slots_copy(off):
        to = partner(s, off, n_sp)
        return pltpu.make_async_remote_copy(
            src_ref=slots_out.at[to], dst_ref=slots_in.at[s], send_sem=so_sem.at[off],
            recv_sem=si_sem.at[s], device_id=(k, to), device_id_type=MESH)

    def slots_landed(off):
        origin = partner(s, off, n_sp)
        pltpu.make_async_remote_copy(
            src_ref=slots_out.at[origin], dst_ref=slots_in.at[origin], send_sem=so_sem.at[off],
            recv_sem=si_sem.at[origin], device_id=(k, origin), device_id_type=MESH).wait_recv()

    for off in reversed(range(1, n_sp)):
        slots_copy(off).start()
    exchange(table_message)
    for off in reversed(range(1, n_sp)):
        spread_copy(off).start()

    def source_copy(fine):
        return pltpu.make_async_remote_copy(
            src_ref=source_ref.at[0, fine], dst_ref=far.at[fine], send_sem=fs_sem.at[fine],
            recv_sem=fr_sem.at[fine], device_id=(before, s), device_id_type=MESH)

    for load in loads[6:]:
        load.wait()
    source_copy(0).start()
    source_copy(1).start()
    br[s] = gb[which, s]
    slots_in[s] = slots_out[s]
    gr[s] = gb[0, s]

    lane = iota((8, 128), 1)
    sub = iota((8, 128), 0)
    left = lane < 64
    half = lane & 64

    def blocks_in_lanes(value):
        return jnp.concatenate([value[:, :CELLS // 2], value[:, CELLS // 2:]], axis=0).T

    def put_source(it, fine, value):
        shuffle[0:256] = blocks_in_lanes(value)
        for z in range(8):
            src[it, fine, z * PLANE:(z + 1) * PLANE] = shuffle[pl.ds(z, PLANE, stride=8), :]

    def make_tables(at, table):
        faces = [jnp.broadcast_to(table[face:face + 1], (8, 128)) for face in range(7)]
        inside = [jnp.maximum(face, 0) for face in faces]
        index = [
            jnp.where(left, inside[0] + 64, lane - 64), jnp.where(left, lane + 64, inside[1]),
            half + jnp.where(sub < 4, inside[2], inside[3]), lane,
            half + inside[4], half + inside[5],
        ]
        known = [jnp.where(face >= 0, 1.0, 0.0) for face in faces[:6]]
        mask = [
            jnp.where(left, known[0], 1.0), jnp.where(left, 1.0, known[1]),
            jnp.where(sub < 4, known[2], known[3]), known[2],
            known[4], known[5],
        ]
        for face in range(6):
            tidx[at, face] = index[face]
            tmask[at, face] = mask[face]
        dif = jnp.zeros((8, 128), F32)
        for cl in range(CLASSES):
            dif = dif + jnp.where(faces[6] == cl, step_ref[:, cl:cl + 1], 0.0)
        tscale[at, 0] = DAMP * dif / (1.0 + 6.0 * dif)
        tscale[at, 1] = DAMP / (1.0 + 6.0 * dif)
        tscale[at, 2] = (1.0 + 6.0 * dif) / DAMP

    make_tables(0, tab_s[0])

    def coarse_of(row):
        high = lax.shift_right_logical(row, 5) * 2 + (row & 1)
        return high * 16 + (lax.shift_right_logical(row, 1) & 3) * 4 + (lax.shift_right_logical(row, 3) & 3)

    size = CLASSES * COARSE
    in_class = (lax.shift_right_logical(iota((size, size), 0), 6)
                == lax.shift_right_logical(iota((size, size), 1), 6))
    tall = jnp.where(in_class & (coarse_of(iota((size, size), 0) & 63) == (iota((size, size), 1) & 63)),
                     1.0, 0.0).astype(BF16)
    wide = jnp.where(coarse_of(iota((COARSE, COARSE), 1)) == iota((COARSE, COARSE), 0), 0.125, 0.0).astype(BF16)

    def made(given):
        parts = [dot(tall, dot(piece, wide).astype(BF16)).astype(BF16) for piece in split(given)]
        return jnp.concatenate(parts, axis=1)

    both = made(inv_ref[...])
    lanes = CLASSES * 2 * COARSE
    blocks = [
        jnp.concatenate([both[at * PLANE:(at + 1) * PLANE, part * COARSE:(part + 1) * COARSE]
                         for at in range(2 * CLASSES)], axis=1) for part in range(2)]
    at_row, at_lane = iota((lanes, lanes), 0), iota((lanes, lanes), 1)
    place_of = ((at_row & 63) * 8 + (lax.shift_right_logical(at_row, 6) & 1) * 4
                + lax.shift_right_logical(at_row, 7))
    moved = dot(jnp.concatenate(blocks, axis=0), jnp.where(place_of == at_lane, 1.0, 0.0).astype(BF16))
    moved = moved[:PLANE] + moved[PLANE:]
    for group in range(4):
        table[group] = moved[:, group * 128:(group + 1) * 128]
    start = jnp.broadcast_to(tab_s[0, 6:7], (8, 128)) + lax.shift_right_logical(lane, 6) * 4

    def make_entries(i, carry):
        for group in range(4):
            entries[group * 16 + i] = lanes_from(table[group], start + 8 * i)
        return carry

    lax.fori_loop(0, 16, make_entries, 0)


    def add_inverse(coarse, start_row, sums):
        count = coarse.shape[0]
        here = tiled(left, count)
        turned = turn(coarse)
        spread_rows[start_row:start_row + count] = jnp.where(here, coarse, turned)
        spread_rows[PLANE + start_row:PLANE + start_row + count] = jnp.where(here, turned, coarse)

        def add(row, sums):
            first, second = sums
            return (first + entries[row] * spread_rows[pl.ds(row, 1)],
                    second + entries[PLANE + row] * spread_rows[pl.ds(PLANE + row, 1)])

        return lax.fori_loop(start_row, start_row + count, add, sums, unroll=True)

    def make_steps():
        power = cstep_ref[...]
        step_h, step_l = split(jnp.where(in_class, jnp.concatenate([power] * CLASSES, axis=1), 0.0))
        step_all = jnp.concatenate([step_h, step_h, step_l], axis=1)
        for d in range(last):
            if d > 0:
                power_h, power_l = split(power)
                power = dot(step_all, jnp.concatenate([power_h, power_l, power_h], axis=0))
            ms[:, d * 128:(d + 1) * 128] = made(power)

    def operands(coarse):
        high = coarse.astype(BF16).astype(F32)
        low = coarse - high
        here = tiled(left, PLANE)
        turned = turn(high)
        return jnp.concatenate([
            jnp.where(here, high, turn(low)), jnp.where(here, turned, low),
            jnp.where(here, high, 0.0), jnp.where(here, turned, 0.0)], axis=0).astype(BF16)

    def selected(product, kinds):
        kinds = jnp.broadcast_to(kinds, (COARSE, 128))
        picked = jnp.where(kinds == 0, product[:COARSE], 0.0)
        for cl in range(1, CLASSES):
            picked = jnp.where(kinds == cl, product[cl * COARSE:(cl + 1) * COARSE], picked)
        picked = picked + turn(picked)
        return jnp.where(tiled(left, PLANE), picked[:PLANE], picked[PLANE:])

    def classes(mat, right):
        return selected(dot(mat, right), tab_s[0, 6:7])

    even = (sub & 1) == 0

    def restrict(value):
        n = value.shape[0] // 64
        pairs = value.reshape(n, 2, 2, 2, 8, 128)
        pairs = pairs[:, 0] + pairs[:, 1]
        pairs = pairs[:, :, 0] + pairs[:, :, 1]
        first = pairs[:, 0].reshape(n * 8, 128)
        second = pairs[:, 1].reshape(n * 8, 128)
        return jnp.where(tiled(even, n * 8), first + along_y(first, -1), second + along_y(second, 1))

    def prolong(coarse):
        here = tiled(even, PLANE)
        first = jnp.where(here, coarse, along_y(coarse, 1)).reshape(4, 1, 1, 1, 8, 128)
        second = jnp.where(here, along_y(coarse, -1), coarse).reshape(4, 1, 1, 1, 8, 128)
        both = jnp.concatenate([first, second], axis=2)
        return jnp.broadcast_to(both, (4, 2, 2, 2, 8, 128)).reshape(256, 128)

    def ghost(plane, face, at):
        return jnp.where(tiled(tmask[at, face], PLANE) > 0.0, lanes_from(plane, tidx[at, face]), 0.0)

    def picked_from(value, face, at):
        return jnp.where(
            tiled(tmask[at, face], value.shape[0]) > 0.0, lanes_from(value, tidx[at, face]), 0.0)

    def beside_xy(value, at):
        size = value.shape[0]
        n = size // PLANE
        cube = value.reshape(n, 4, 8, 128)
        part = [cube[:, j].reshape(n * 8, 128) for j in range(4)]
        low = picked_from(part[3], 0, at)
        high = picked_from(part[0], 1, at)
        here = tiled(sub, n * 8)
        edges = along_y(part[0], 1)
        for j in range(1, 8):
            edges = jnp.where(here == j, along_y(part[j % 4], j + 1 if j < 4 else j), edges)
        edges = picked_from(edges, 2, at)
        sums = []
        for j in range(4):
            total = (part[j - 1] if j > 0 else low) + (part[j + 1] if j < 3 else high)
            total = total + jnp.where(here == 0, along_y(edges, -j), along_y(part[j], 1))
            total = total + jnp.where(here == 7, along_y(edges, 3 - j), along_y(part[j], -1))
            sums.append(total.reshape(n, 1, 8, 128))
        return jnp.concatenate(sums, axis=1).reshape(size, 128)

    def inner(value):
        zero = jnp.zeros((PLANE, 128), F32)
        total = beside_xy(value, 0)
        total = total + jnp.concatenate([zero, value[:-PLANE]], axis=0)
        return total + jnp.concatenate([value[PLANE:], zero], axis=0)

    def ended(total, below, above):
        return jnp.concatenate([
            total[:PLANE] + ghost(below, 4, 0), total[PLANE:-PLANE],
            total[-PLANE:] + ghost(above, 5, 0)], axis=0)

    def scaled(which, at, size):
        return tiled(tscale[at, which], size)

    def relax(value, driven, total, at):
        return (1.0 - DAMP) * value + driven + scaled(0, at, value.shape[0]) * total

    def slab_below(slab, driven, own):
        cross = ghost(own[:PLANE], 5, 1)
        near = slab[PLANE:]
        upper = jnp.concatenate([slab[2 * PLANE:], cross], axis=0) if slab.shape[0] > 2 * PLANE else cross
        return relax(near, driven, beside_xy(near, 1) + slab[:-PLANE] + upper, 1)

    def slab_above(slab, driven, own):
        cross = ghost(own[-PLANE:], 4, 2)
        near = slab[:-PLANE]
        lower = jnp.concatenate([cross, slab[:-2 * PLANE]], axis=0) if slab.shape[0] > 2 * PLANE else cross
        return relax(near, driven, beside_xy(near, 2) + slab[PLANE:] + lower, 2)

    def begun(value, driven):
        total = inner(value)
        mid = relax(value[PLANE:-PLANE], driven[PLANE:-PLANE], total[PLANE:-PLANE], 0)
        around = beside_xy(mid, 0)
        deep = around[PLANE:-PLANE] + mid[:-2 * PLANE] + mid[2 * PLANE:]
        return total, mid, around, deep

    def ended2(value, driven, begin, below, above, below_d, above_d):
        total, mid, around, _ = begin
        low = relax(value[:PLANE], driven[:PLANE], total[:PLANE] + ghost(below[-PLANE:], 4, 0), 0)
        high = relax(value[-PLANE:], driven[-PLANE:], total[-PLANE:] + ghost(above[:PLANE], 5, 0), 0)
        below = slab_below(below, below_d, value)
        above = slab_above(above, above_d, value)
        sides = beside_xy(jnp.concatenate([low, high], axis=0), 0)
        sums_low = jnp.concatenate([
            sides[:PLANE] + mid[:PLANE] + ghost(below[-PLANE:], 4, 0),
            around[:PLANE] + low + mid[PLANE:2 * PLANE]], axis=0)
        sums_high = jnp.concatenate([
            around[-PLANE:] + mid[-2 * PLANE:-PLANE] + high,
            sides[PLANE:] + mid[-PLANE:] + ghost(above[:PLANE], 5, 0)], axis=0)
        return low, high, sums_low, sums_high, below, above

    def left_over(value, driven, sums):
        rest = driven - DAMP * value + scaled(0, 0, value.shape[0]) * sums
        return scaled(2, 0, value.shape[0] // 8) * restrict(rest)

    def correction_begun(driven):
        begin = begun(driven, driven)
        mid, deep = begin[1], begin[3]
        zero = jnp.zeros((PLANE, 128), F32)
        return begin, add_inverse(
            left_over(mid[PLANE:-PLANE], driven[2 * PLANE:-2 * PLANE], deep), 8, (zero, zero))

    def corrected(driven, begin, part, below, above):
        low, high, sums_low, sums_high, _, _ = ended2(
            driven, driven, begin, below, above, below[PLANE:], above[:-PLANE])
        mid = begin[1]
        part = add_inverse(left_over(
            jnp.concatenate([low, mid[:PLANE]], axis=0), driven[:2 * PLANE], sums_low), 0, part)
        part = add_inverse(left_over(
            jnp.concatenate([mid[-PLANE:], high], axis=0), driven[-2 * PLANE:], sums_high), 24, part)
        return jnp.concatenate([low, mid, high], axis=0) + prolong(part[0] + part[1])

    def sweep_middle(begin, driven):
        return relax(begin[1][PLANE:-PLANE], driven[2 * PLANE:-2 * PLANE], begin[3], 0)

    def sweep_ends(value, driven, begin, below, above, below_d, above_d):
        low, high, sums_low, sums_high, below, above = ended2(
            value, driven, begin, below, above, below_d, above_d)
        mid = begin[1]
        x5_low = relax(jnp.concatenate([low, mid[:PLANE]], axis=0), driven[:2 * PLANE], sums_low, 0)
        x5_high = relax(jnp.concatenate([mid[-PLANE:], high], axis=0), driven[-2 * PLANE:], sums_high, 0)
        return x5_low, x5_high, low, high, below, above

    exchanged(table_message)
    for side in range(2):
        reached = (s > 0) if side == 0 else (s < n_sp - 1)
        make_tables(1 + side, jnp.where(reached, tab_r[side], -1))

    for off in range(1, n_sp):
        slots_landed(off)
    slots = jnp.sum(jnp.where(spot, slots_in[:, :1], 0.0), axis=2, keepdims=True)
    slots = jnp.broadcast_to(slots, (n_sp, bk, 128)).reshape(rows, 128)
    hit = slots == (iota((rows, 128), 1) & 63).astype(F32)
    place = jnp.sum(jnp.where(hit, iota((rows, 128), 0).astype(F32), 0.0), axis=0, keepdims=True)
    place = jnp.broadcast_to(place, (8, 128)).astype(jnp.int32)

    source_copy(0).wait_recv()
    put_source(0, 0, far[0])

    def settle(given, put):
        tiles = rows // 128
        for tile in range(tiles):
            shuffle[tile * CELLS:(tile + 1) * CELLS] = given[tile * 128:(tile + 1) * 128].T
        for z in range(8):
            plane = None
            for tile in range(tiles):
                both = shuffle[pl.ds(tile * CELLS + z, 64, stride=8), :]
                both = lanes_from(both, place & 127)
                both = jnp.where(tiled(left, PLANE), both[:PLANE], both[PLANE:])
                chosen_tile = tiled(lax.shift_right_logical(place, 7), PLANE) == tile
                plane = both if plane is None else jnp.where(chosen_tile, both, plane)
            put(z, plane)

    for off in range(1, n_sp):
        spread_landed(off)

    def put_start(z, plane):
        bs[z * PLANE:(z + 1) * PLANE] = plane

    settle(br[...].reshape(rows, CELLS), put_start)

    def init_copy():
        return pltpu.make_async_remote_copy(
            src_ref=bs, dst_ref=hand, send_sem=bk_sem.at[0], recv_sem=bq_sem.at[0],
            device_id=(after, s), device_id_type=MESH)

    def guess_copy():
        return pltpu.make_async_remote_copy(
            src_ref=rg_s, dst_ref=rg_r, send_sem=bk_sem.at[1], recv_sem=bq_sem.at[1],
            device_id=(before, s), device_id_type=MESH)

    def mine_copy():
        return pltpu.make_async_remote_copy(
            src_ref=hsrc, dst_ref=mine, send_sem=bk_sem.at[2], recv_sem=bq_sem.at[2],
            device_id=(after, s), device_id_type=MESH)

    def hand_copy(at):
        first, count = ((2 * PLANE, 4 * PLANE), (0, 2 * PLANE), (6 * PLANE, 2 * PLANE))[at]
        return pltpu.make_async_remote_copy(
            src_ref=hsrc.at[pl.ds(first, count)], dst_ref=hand.at[pl.ds(first, count)],
            send_sem=ts_sem.at[at], recv_sem=tr_sem.at[at], device_id=(lax.rem(k + 2, n_tm), s),
            device_id_type=MESH)

    def edges_message(state, col, at):
        up = pltpu.make_async_remote_copy(
            src_ref=state.at[pl.ds(6 * PLANE, 2 * PLANE)], dst_ref=hp.at[0], send_sem=hps_sem.at[at, 0],
            recv_sem=hpr_sem.at[0], device_id=(col, lax.rem(s + 1, n_sp)), device_id_type=MESH)
        down = pltpu.make_async_remote_copy(
            src_ref=state.at[pl.ds(0, 2 * PLANE)], dst_ref=hp.at[1], send_sem=hps_sem.at[at, 1],
            recv_sem=hpr_sem.at[1], device_id=(col, lax.rem(s + n_sp - 1, n_sp)), device_id_type=MESH)
        return up, down

    def hand_edges():
        return edges_message(hsrc, lax.rem(k + 2, n_tm), 0)

    def init_edges():
        return edges_message(bs, after, 1)

    def coarse_beside(off):
        col = lax.rem(after + off, n_tm)
        up = pltpu.make_async_remote_copy(
            src_ref=cs.at[0], dst_ref=crn.at[0, off - 2], send_sem=cns_sem.at[0, off - 2],
            recv_sem=cnr_sem.at[0, off - 2], device_id=(col, lax.rem(s + 1, n_sp)), device_id_type=MESH)
        down = pltpu.make_async_remote_copy(
            src_ref=cs.at[0], dst_ref=crn.at[1, off - 2], send_sem=cns_sem.at[1, off - 2],
            recv_sem=cnr_sem.at[1, off - 2], device_id=(col, lax.rem(s + n_sp - 1, n_sp)), device_id_type=MESH)
        return up, down

    def beside_landed():
        sides = []
        for side, reached in ((0, s > 0), (1, s < n_sp - 1)):
            rights = []
            for off in range(2, n_tm):
                there = (k >= off) & reached

                @pl.when(there)
                def _():
                    coarse_beside(off)[side].wait_recv()
                rights.append(operands(jnp.where(there, crn[side, off - 2], 0.0)))
            sides.append(jnp.concatenate(rights, axis=0))
        return sides

    def one_plane(coarse):
        first = jnp.where(even, coarse, along_y(coarse, 1))
        second = jnp.where(even, along_y(coarse, -1), coarse)
        return jnp.concatenate([first, first, second, second], axis=0)

    ahead = (after, k)

    def coarse_copy(it, off):
        return pltpu.make_async_remote_copy(
            src_ref=cs.at[it], dst_ref=cr.at[it, off - 1], send_sem=cs_sem.at[it, off - 1],
            recv_sem=cr_sem.at[it, off - 1], device_id=(lax.rem(ahead[it] + off, n_tm), s), device_id_type=MESH)

    def coarse_landed(it):
        rights = []
        for off in range(1, n_tm):
            if it > 0 or off < last:
                @pl.when(k >= off)
                def _():
                    coarse_copy(it, off).wait_recv()
            rights.append(operands(jnp.where(k >= off, cr[it, off - 1], 0.0)))
        return jnp.concatenate(rights, axis=0)

    def plane_out(state, kept):
        for z in range(8):
            shuffle[pl.ds(z, PLANE, stride=8), :] = state[z * PLANE:(z + 1) * PLANE]
        flat = shuffle[0:256].T
        kept[0] = jnp.concatenate([flat[:64], flat[64:]], axis=1)


    rights = None
    for it in range(ITERS):
        if it == 0:
            drv[0] = scaled(1, 0, 256) * (bs[...] + src[0, 0])
            exchange(first_message(0))
            rg_s[...] = restrict(bs[...])

            @pl.when(k < last)
            def _():
                guess_copy().start()

            @pl.when(k == last)
            def _():
                init_copy().start()
                exchange(init_edges())
        else:
            rights = coarse_landed(it - 1)
            beside_rights = beside_landed()
            product = dot(
                ms[:, :(last - 1) * 128], jnp.concatenate([rights[128:], *beside_rights], axis=1))
            pushed = prolong(selected(product[:, :128], tab_s[0, 6:7]))
            pushed_b = one_plane(selected(product[:, 128:256], tab_r[0, 6:7])[3 * 8:])
            pushed_a = one_plane(selected(product[:, 256:], tab_r[1, 6:7])[:8])
            exchanged(first_source)
            exchanged(hand_edges())
            below_d = scaled(1, 1, 2 * PLANE) * (hp[0] + jnp.concatenate([pushed_b] * 2, axis=0) + srcf[0])
            above_d = scaled(1, 2, 2 * PLANE) * (hp[1] + jnp.concatenate([pushed_a] * 2, axis=0) + srcf[1])
            e1[it, 0, PLANE:] = below_d
            e1[it, 1, :2 * PLANE] = above_d

            @pl.when(k > 0)
            def _():
                for at in range(3):
                    hand_copy(at).wait_recv()

            @pl.when(k == 0)
            def _():
                init_copy().wait_recv()
            drv[it] = scaled(1, 0, 256) * (hand[...] + pushed + src[1, 0])
            exchange(first_message(it))
            mine_copy().start()
        driven = drv[it]
        begin, part = correction_begun(driven)
        if it == 0:
            source_copy(1).wait_recv()
            put_source(0, 1, far[1])
            exchange(source_message(0))
            exchanged(first_message(it))
            below_d, above_d = e1[it, 0, PLANE:], e1[it, 1, :-PLANE]
        x3a[it] = corrected(driven, begin, part, below_d, above_d)
        exchange(deep_message(it))
        x3 = x3a[it]
        begin = begun(x3, driven)
        x5_mid = sweep_middle(begin, driven)
        if it == 0:
            make_steps()
        exchanged(source_message(it))
        if it > 0:
            @pl.when(k == last)
            def _():
                init_copy().wait_send()
                drained(init_edges())
                for off in range(1, n_sp):
                    own_landed(off)
                settle(gr[...].reshape(rows, CELLS), put_start)
        if it > 0:
            exchanged(first_message(it))
        exchanged(deep_message(it))
        x5_low, x5_high, x4_low, x4_high, below4, above4 = sweep_ends(
            x3, driven, begin, e2[it, 0], e2[it, 1], e1[it, 0], e1[it, 1])
        x5 = jnp.concatenate([x5_low, x5_mid, x5_high], axis=0)
        below5 = slab_below(below4, e1[it, 0, PLANE:], x4_low)
        above5 = slab_above(above4, e1[it, 1, :-PLANE], x4_high)
        xf[...] = x5
        driven = scaled(1, 0, 256) * (x5 + src[it, 1])
        below_d = scaled(1, 1, 2 * PLANE) * (below5 + srch[it, 0])
        above_d = scaled(1, 2, 2 * PLANE) * (above5 + srch[it, 1])
        begin, part = correction_begun(driven)
        x3b[it] = corrected(driven, begin, part, below_d, above_d)
        exchange(second_message(it))
        x3 = x3b[it]
        begin = begun(x3, driven)
        x5_mid = sweep_middle(begin, driven)
        if it < ITERS - 1:
            hsrc[2 * PLANE:6 * PLANE] = x5_mid

            @pl.when(k != last - 1)
            def _():
                hand_copy(0).start()
        if it == 0:
            for fine in range(2):
                put_source(1, fine, source_ref[0, fine])
            exchange(first_source)

            @pl.when(k != last - 1)
            def _():
                guess_copy().wait_recv()
        else:
            mine_copy().wait_recv()
            st[...] = bs[...] + (prolong(classes(ms[...], rights)) + (mine[...] - bs[...]))
        if it == ITERS - 1:
            plane_out(xf, f_ref)
        exchanged(second_message(it))
        x5_low, x5_high, _, _, _, _ = sweep_ends(
            x3, driven, begin, e4[it, 0], e4[it, 1], below_d[PLANE:], above_d[:-PLANE])
        if it < ITERS - 1:
            hsrc[:2 * PLANE] = x5_low
            hsrc[6 * PLANE:] = x5_high

            @pl.when(k != last - 1)
            def _():
                exchange(hand_edges())
                cs[it] = restrict(hsrc[...]) - rg_r[...]
                for off in range(1, last):
                    @pl.when(after + off < n_tm)
                    def _():
                        coarse_copy(it, off).start()
                for off in range(2, n_tm):
                    @pl.when(after + off < n_tm)
                    def _():
                        exchange(coarse_beside(off))
                for at in (1, 2):
                    hand_copy(at).start()

            @pl.when(k == last)
            def _():
                cr[it, last - 1] = cs[it]
                for off in range(1, n_sp):
                    own_copy(off).start()
            exchange(source_message(1))
        else:
            residual = jnp.concatenate([x5_low, x5_mid, x5_high], axis=0) - st[...]
            cs[it] = restrict(residual)
            for off in range(1, n_tm):
                @pl.when(k + off < n_tm)
                def _():
                    coarse_copy(it, off).start()
            rights = coarse_landed(it)
            xf[...] = st[...] + (prolong(classes(ms[...], rights)) + residual)

    plane_out(xf, c_ref)

    for off in range(1, n_sp):
        slots_copy(off).wait_send()
        spread_copy(off).wait_send()
    for fine in range(2):
        source_copy(fine).wait_send()
    mine_copy().wait_send()

    @pl.when(k == last)
    def _():
        for off in range(1, n_sp):
            own_copy(off).wait_send()

    @pl.when(k < last)
    def _():
        guess_copy().wait_send()

    drained(table_message)
    drained(first_source)
    for it in range(ITERS):
        drained(source_message(it))
        drained(first_message(it))
        drained(deep_message(it))
        drained(second_message(it))
    for off in range(1, n_tm):
        @pl.when(k + off < n_tm)
        def _():
            coarse_copy(1, off).wait_send()
    for off in range(1, last):
        @pl.when((k != last - 1) & (after + off < n_tm))
        def _():
            coarse_copy(0, off).wait_send()

    @pl.when(k != last - 1)
    def _():
        for at in range(3):
            hand_copy(at).wait_send()
        drained(hand_edges())
        for off in range(2, n_tm):
            @pl.when(after + off < n_tm)
            def _():
                drained(coarse_beside(off))


def solution(mesh):
    n_tm, n_sp = mesh.shape["tm"], mesh.shape["space"]

    def body(init_state, guess, source, remap, neighbors, block_class, step_number, inverse, cstep):
        nb = init_state.shape[0]
        bk = -(-(2 * nb // n_sp) // 8) * 8
        tiles = n_sp * bk // 128
        slots = 4 + 3 * ITERS
        dma = pltpu.SemaphoreType.DMA
        full = 8 * PLANE

        def vmem(*shape, dtype=F32):
            return pltpu.VMEM(shape, dtype)

        return pl.pallas_call(
            functools.partial(kernel, n_tm, n_sp, bk),
            name="mgrit",
            out_shape=(vmem(1, nb, CELLS), vmem(1, nb, CELLS)),
            in_specs=[pl.BlockSpec(memory_space=pl.ANY)] * 9,
            out_specs=[pl.BlockSpec(memory_space=pltpu.VMEM)] * 2,
            scratch_shapes=[
                vmem(nb, CELLS), vmem(1, nb, CELLS), vmem(1, 2, nb, CELLS), vmem(1, nb, dtype=jnp.int32),
                vmem(6, nb, dtype=jnp.int32), vmem(1, nb, dtype=jnp.int32), vmem(1, CLASSES),
                vmem(CLASSES * COARSE, COARSE), vmem(CLASSES * COARSE, COARSE),
                vmem(2, n_sp, bk, CELLS), vmem(n_sp, bk, CELLS), vmem(n_sp, bk, CELLS), vmem(2, nb, CELLS),
                vmem(2, 8, 128, dtype=jnp.int32), vmem(2, 8, 128, dtype=jnp.int32),
                vmem(3, 6, 8, 128, dtype=jnp.int32), vmem(3, 6, 8, 128), vmem(3, 3, 8, 128),
                vmem(ITERS, 2, full, 128), vmem(ITERS, 2, 2 * PLANE, 128), vmem(2, 2 * PLANE, 128), vmem(tiles * CELLS, 128),
                vmem(full, 128), vmem(ITERS, full, 128), vmem(ITERS, full, 128), vmem(ITERS, full, 128),
                vmem(ITERS, 2, 3 * PLANE, 128), vmem(ITERS, 2, 4 * PLANE, 128), vmem(ITERS, 2, 2 * PLANE, 128),
                vmem(full, 128), vmem(full, 128), vmem(full, 128), vmem(full, 128), vmem(2, 2 * PLANE, 128), vmem(full, 128),
                vmem(PLANE, 128), vmem(PLANE, 128),
                vmem(ITERS, PLANE, 128), vmem(ITERS, n_tm - 1, PLANE, 128), vmem(2, n_tm - 2, PLANE, 128),
                vmem(4, PLANE, 128), vmem(2 * PLANE, 128), vmem(COARSE, PLANE, 128), vmem(CLASSES * COARSE, (n_tm - 1) * 128, dtype=BF16),
                vmem(n_sp, 8, 128), vmem(n_sp, 8, 128),
                dma((9,)), dma((n_sp,)), dma((n_sp,)),
                dma((n_sp,)), dma((n_sp,)), dma((n_sp,)), dma((n_sp,)),
                dma((slots, 2)), dma((slots, 2)),
                dma((3,)), dma((3,)), dma((3,)), dma((3,)),
                dma((ITERS, n_tm - 1)), dma((ITERS, n_tm - 1)), dma((2,)), dma((2,)),
                dma((2, 2)), dma((2,)), dma((2, n_tm - 2)), dma((2, n_tm - 2)),
            ],
            compiler_params=pltpu.CompilerParams(collective_id=0, has_side_effects=True),
        )(
            init_state, guess, source, remap.reshape(1, nb), neighbors.T, block_class.reshape(1, nb),
            step_number.reshape(1, CLASSES), inverse.reshape(CLASSES * COARSE, COARSE),
            cstep.reshape(CLASSES * COARSE, COARSE),
        )

    placed = (
        P("space", None), P("tm", "space", None), P("tm", None, "space", None), P("space"),
        P("space", None), P("space"), P(), P(), P(),
    )
    return jax.shard_map(
        body, mesh=mesh, in_specs=placed,
        out_specs=(P("tm", "space", None), P("tm", "space", None)), check_vma=False,
    )
```

```python
import functools

import jax
import jax.numpy as jnp
from jax import lax
from jax.experimental import pallas as pl
from jax.experimental.pallas import tpu as pltpu
from jax.sharding import PartitionSpec as P

CELLS = 512
COARSE = 64
CLASSES = 4
ITERS = 2
DAMP = 0.8
PLANE = 32
MESH = pl.DeviceIdType.MESH
F32 = jnp.float32
BF16 = jnp.bfloat16


def split(value):
    high = value.astype(BF16)
    return high, (value - high.astype(F32)).astype(BF16)


def dot(left, right):
    return jnp.dot(left, right, preferred_element_type=F32)


def iota(shape, dim):
    return lax.broadcasted_iota(jnp.int32, shape, dim)


def turn(value):
    return pltpu.roll(value, 64, 1)


def along_y(value, shift):
    rows = value.shape[0]
    return pltpu.roll(value.reshape(rows // 8, 8, 128), shift % 8, 1).reshape(rows, 128)


def tiled(table, rows):
    return jnp.broadcast_to(table[None], (rows // 8, 8, 128)).reshape(rows, 128)


def lanes_from(value, index):
    return jnp.take_along_axis(
        value, tiled(index, value.shape[0]), axis=1, mode="promise_in_bounds")


def partner(s, off, n):
    if n & (n - 1):
        return lax.rem(s + off, n)
    to = s
    for bit in range(n.bit_length() - 1):
        if off >> bit & 1:
            to = to + (1 - 2 * lax.rem(lax.div(s, 1 << bit), 2)) * (1 << bit)
    return to


def kernel(
    n_tm, n_sp, bk,
    init_hbm, guess_hbm, source_hbm, remap_hbm, nb_hbm, class_hbm, step_hbm, inv_hbm, cstep_hbm,
    both_ref,
    init_ref, guess_ref, source_ref, remap_ref, nb_ref, class_ref, step_ref, inv_ref, cstep_ref,
    gb, br, gr, far, tab_s, tab_r, tidx, tmask, tscale, src, srch, srcf, shuffle,
    bs, drv, x3a, x3b, e1, e2, e4, st, xf, hsrc, hand, hp, mine, rg_s, rg_r, cs, cr, crn, table, spread_rows, entries, ms,
    slots_out, slots_in, in_sem, so_sem, si_sem,
    gs_sem, gr_sem, ps_sem, br_sem, hs_sem, hr_sem, ts_sem, tr_sem, bk_sem, bq_sem, cs_sem, cr_sem, fs_sem, fr_sem,
    hps_sem, hpr_sem, cns_sem, cnr_sem,
):
    k = lax.axis_index("tm")
    s = lax.axis_index("space")
    nb = init_hbm.shape[0]
    rows = n_sp * bk
    bits = nb.bit_length() - 1
    last = n_tm - 1

    after, before = lax.rem(k + 1, n_tm), lax.rem(k + last, n_tm)

    barrier = pltpu.get_barrier_semaphore()

    def greet(tm, space):
        pl.semaphore_signal(barrier, inc=1, device_id=(tm, space), device_id_type=MESH)

    for off in range(1, n_sp):
        greet(k, partner(s, off, n_sp))
    for off in range(1, n_tm):
        greet(lax.rem(k + off, n_tm), s)

        @pl.when(s > 0)
        def _():
            greet(lax.rem(k + off, n_tm), s - 1)

        @pl.when(s < n_sp - 1)
        def _():
            greet(lax.rem(k + off, n_tm), s + 1)

    loads = [
        pltpu.make_async_copy(given, kept, in_sem.at[at]) for at, (given, kept) in enumerate((
            (remap_hbm, remap_ref), (guess_hbm, guess_ref), (init_hbm, init_ref), (nb_hbm, nb_ref),
            (class_hbm, class_ref), (step_hbm, step_ref), (source_hbm, source_ref), (inv_hbm, inv_ref),
            (cstep_hbm, cstep_ref)))]
    for load in loads:
        load.start()
    loads[0].wait()

    eye = iota((nb, nb), 0) == iota((nb, nb), 1)

    def column(row):
        return jnp.sum(jnp.where(eye, row, 0.0), axis=1, keepdims=True)

    remap_row = remap_ref[...]
    target_row = lax.shift_right_logical(remap_row, bits)
    slot_row = (remap_row - lax.shift_left(target_row, bits)).astype(F32)
    target_f = target_row.astype(F32)
    same = (column(target_f) == target_f) & (iota((nb, nb), 0) < iota((nb, nb), 1))
    pos_row = jnp.sum(jnp.where(same, 1.0, 0.0), axis=0, keepdims=True)
    send_row = target_f * float(bk) + pos_row
    chosen = iota((rows, nb), 0).astype(F32) == send_row
    send_mat = jnp.where(chosen, 1.0, 0.0)
    slot_col = jnp.sum(jnp.where(chosen, slot_row + 1.0, 0.0), axis=1, keepdims=True) - 1.0
    send_mat = jnp.concatenate([send_mat, send_mat], axis=1).astype(BF16)

    def bucketed(value):
        return dot(send_mat, jnp.concatenate(split(value), axis=0)).reshape(n_sp, bk, CELLS)

    spot = iota((n_sp, bk, 128), 1) == iota((n_sp, bk, 128), 2)
    slot_wide = jnp.broadcast_to(slot_col, (rows, 128)).reshape(n_sp, bk, 128)
    slot_lanes = jnp.sum(jnp.where(spot, slot_wide, 0.0), axis=1, keepdims=True)
    slots_out[...] = jnp.broadcast_to(slot_lanes, (n_sp, 8, 128))
    loads[1].wait()
    loads[2].wait()
    gb[0] = bucketed(guess_ref[0])

    @pl.when(k == last)
    def _():
        gb[1] = bucketed(init_ref[...])

    for load in loads[3:6]:
        load.wait()

    linked = nb_ref[...]
    face_no = iota((6, nb), 0)
    run = s + jnp.where(face_no == 4, -1, jnp.where(face_no == 5, 1, 0))
    linked = jnp.where(linked >= 0, linked - run * nb, -1)
    tab_s[0, 0:6] = jnp.concatenate([linked, linked], axis=1)
    kind = class_ref[...]
    tab_s[0, 6:7] = jnp.concatenate([kind, kind], axis=1)
    tab_s[0, 7:8] = jnp.zeros((1, 128), jnp.int32)
    tab_s[1] = tab_s[0]

    beside = jnp.minimum(s, 1) + jnp.minimum(n_sp - 1 - s, 1)
    pl.semaphore_wait(barrier, n_sp - 1 + (n_tm - 1) * (1 + beside))

    up_to = (k, lax.rem(s + 1, n_sp))
    down_to = (k, lax.rem(s + n_sp - 1, n_sp))

    def halo_up(slot, source, target):
        return pltpu.make_async_remote_copy(
            src_ref=source, dst_ref=target, send_sem=hs_sem.at[slot, 0],
            recv_sem=hr_sem.at[slot, 0], device_id=up_to, device_id_type=MESH)

    def halo_down(slot, source, target):
        return pltpu.make_async_remote_copy(
            src_ref=source, dst_ref=target, send_sem=hs_sem.at[slot, 1],
            recv_sem=hr_sem.at[slot, 1], device_id=down_to, device_id_type=MESH)

    def planes_message(slot, state, depth, target):
        size = depth * PLANE
        return (halo_up(slot, state.at[pl.ds(8 * PLANE - size, size)], target.at[0]),
                halo_down(slot, state.at[pl.ds(0, size)], target.at[1]))

    def exchange(message):
        up, down = message

        @pl.when(s < n_sp - 1)
        def _():
            up.start()

        @pl.when(s > 0)
        def _():
            down.start()

    def exchanged(message):
        up, down = message

        @pl.when(s > 0)
        def _():
            up.wait_recv()

        @pl.when(s < n_sp - 1)
        def _():
            down.wait_recv()

    def drained(message):
        up, down = message

        @pl.when(s < n_sp - 1)
        def _():
            up.wait_send()

        @pl.when(s > 0)
        def _():
            down.wait_send()

    table_message = (halo_up(0, tab_s.at[0], tab_r.at[0]), halo_down(0, tab_s.at[1], tab_r.at[1]))

    def source_message(it):
        return planes_message(1 + it, src.at[it, 1], 2, srch.at[it])

    first_source = planes_message(3 + 3 * ITERS, src.at[1, 0], 2, srcf)

    def first_message(it):
        if it == 0:
            return planes_message(3 + 3 * it, drv.at[it], 3, e1.at[it])
        return (halo_up(3 + 3 * it, drv.at[it, pl.ds(5 * PLANE, PLANE)], e1.at[it, 0, pl.ds(0, PLANE)]),
                halo_down(3 + 3 * it, drv.at[it, pl.ds(2 * PLANE, PLANE)], e1.at[it, 1, pl.ds(2 * PLANE, PLANE)]))

    def deep_message(it):
        return planes_message(4 + 3 * it, x3a.at[it], 4, e2.at[it])

    def second_message(it):
        return planes_message(5 + 3 * it, x3b.at[it], 2, e4.at[it])

    which = jnp.maximum(k - last + 1, 0)

    def spread_copy(off):
        to = partner(s, off, n_sp)
        return pltpu.make_async_remote_copy(
            src_ref=gb.at[which, to], dst_ref=br.at[s], send_sem=ps_sem.at[off], recv_sem=br_sem.at[s],
            device_id=(k, to), device_id_type=MESH)

    def spread_landed(off):
        origin = partner(s, off, n_sp)
        pltpu.make_async_remote_copy(
            src_ref=gb.at[0, origin], dst_ref=br.at[origin], send_sem=ps_sem.at[off],
            recv_sem=br_sem.at[origin], device_id=(k, origin), device_id_type=MESH).wait_recv()

    def own_copy(off):
        to = partner(s, off, n_sp)
        return pltpu.make_async_remote_copy(
            src_ref=gb.at[0, to], dst_ref=gr.at[s], send_sem=gs_sem.at[off],
            recv_sem=gr_sem.at[s], device_id=(k, to), device_id_type=MESH)

    def own_landed(off):
        origin = partner(s, off, n_sp)
        pltpu.make_async_remote_copy(
            src_ref=gb.at[0, origin], dst_ref=gr.at[origin],
            send_sem=gs_sem.at[off], recv_sem=gr_sem.at[origin], device_id=(k, origin),
            device_id_type=MESH).wait_recv()

    def slots_copy(off):
        to = partner(s, off, n_sp)
        return pltpu.make_async_remote_copy(
            src_ref=slots_out.at[to, pl.ds(0, 1)], dst_ref=slots_in.at[s, pl.ds(0, 1)], send_sem=so_sem.at[off],
            recv_sem=si_sem.at[s], device_id=(k, to), device_id_type=MESH)

    def slots_landed(off):
        origin = partner(s, off, n_sp)
        pltpu.make_async_remote_copy(
            src_ref=slots_out.at[origin, pl.ds(0, 1)], dst_ref=slots_in.at[origin, pl.ds(0, 1)], send_sem=so_sem.at[off],
            recv_sem=si_sem.at[origin], device_id=(k, origin), device_id_type=MESH).wait_recv()

    for off in reversed(range(1, n_sp)):
        slots_copy(off).start()
    exchange(table_message)
    for off in reversed(range(1, n_sp)):
        spread_copy(off).start()

    def source_copy(fine):
        return pltpu.make_async_remote_copy(
            src_ref=source_ref.at[0, fine], dst_ref=far.at[fine], send_sem=fs_sem.at[fine],
            recv_sem=fr_sem.at[fine], device_id=(before, s), device_id_type=MESH)

    for load in loads[6:]:
        load.wait()
    source_copy(0).start()
    source_copy(1).start()
    br[s] = gb[which, s]
    slots_in[s] = slots_out[s]
    gr[s] = gb[0, s]

    lane = iota((8, 128), 1)
    sub = iota((8, 128), 0)
    left = lane < 64
    half = lane & 64

    def blocks_in_lanes(value):
        return jnp.concatenate([value[:, :CELLS // 2], value[:, CELLS // 2:]], axis=0).T

    def put_source(it, fine, value):
        shuffle[0:256] = blocks_in_lanes(value)
        for z in range(8):
            src[it, fine, z * PLANE:(z + 1) * PLANE] = shuffle[pl.ds(z, PLANE, stride=8), :]

    def make_tables(at, table):
        faces = [jnp.broadcast_to(table[face:face + 1], (8, 128)) for face in range(7)]
        inside = [jnp.maximum(face, 0) for face in faces]
        index = [
            jnp.where(left, inside[0] + 64, lane - 64), jnp.where(left, lane + 64, inside[1]),
            half + jnp.where(sub < 4, inside[2], inside[3]), lane,
            half + inside[4], half + inside[5],
        ]
        known = [jnp.where(face >= 0, 1.0, 0.0) for face in faces[:6]]
        mask = [
            jnp.where(left, known[0], 1.0), jnp.where(left, 1.0, known[1]),
            jnp.where(sub < 4, known[2], known[3]), known[2],
            known[4], known[5],
        ]
        for face in range(6):
            tidx[at, face] = index[face]
            tmask[at, face] = mask[face]
        dif = jnp.zeros((8, 128), F32)
        for cl in range(CLASSES):
            dif = dif + jnp.where(faces[6] == cl, step_ref[:, cl:cl + 1], 0.0)
        tscale[at, 0] = DAMP * dif / (1.0 + 6.0 * dif)
        tscale[at, 1] = DAMP / (1.0 + 6.0 * dif)
        tscale[at, 2] = (1.0 + 6.0 * dif) / DAMP

    make_tables(0, tab_s[0])

    def coarse_of(row):
        high = lax.shift_right_logical(row, 5) * 2 + (row & 1)
        return high * 16 + (lax.shift_right_logical(row, 1) & 3) * 4 + (lax.shift_right_logical(row, 3) & 3)

    size = CLASSES * COARSE
    in_class = (lax.shift_right_logical(iota((size, size), 0), 6)
                == lax.shift_right_logical(iota((size, size), 1), 6))
    tall = jnp.where(in_class & (coarse_of(iota((size, size), 0) & 63) == (iota((size, size), 1) & 63)),
                     1.0, 0.0).astype(BF16)
    wide = jnp.where(coarse_of(iota((COARSE, COARSE), 1)) == iota((COARSE, COARSE), 0), 0.125, 0.0).astype(BF16)

    def made(given):
        parts = [dot(tall, dot(piece, wide).astype(BF16)).astype(BF16) for piece in split(given)]
        return jnp.concatenate(parts, axis=1)

    both = made(inv_ref[...])
    lanes = CLASSES * 2 * COARSE
    blocks = [
        jnp.concatenate([both[at * PLANE:(at + 1) * PLANE, part * COARSE:(part + 1) * COARSE]
                         for at in range(2 * CLASSES)], axis=1) for part in range(2)]
    at_row, at_lane = iota((lanes, lanes), 0), iota((lanes, lanes), 1)
    place_of = ((at_row & 63) * 8 + (lax.shift_right_logical(at_row, 6) & 1) * 4
                + lax.shift_right_logical(at_row, 7))
    moved = dot(jnp.concatenate(blocks, axis=0), jnp.where(place_of == at_lane, 1.0, 0.0).astype(BF16))
    moved = moved[:PLANE] + moved[PLANE:]
    for group in range(4):
        table[group] = moved[:, group * 128:(group + 1) * 128]
    start = jnp.broadcast_to(tab_s[0, 6:7], (8, 128)) + lax.shift_right_logical(lane, 6) * 4

    def make_entries(i, carry):
        for group in range(4):
            entries[group * 16 + i] = lanes_from(table[group], start + 8 * i)
        return carry

    lax.fori_loop(0, 16, make_entries, 0)


    def add_inverse(coarse, start_row, sums):
        count = coarse.shape[0]
        here = tiled(left, count)
        turned = turn(coarse)
        spread_rows[start_row:start_row + count] = jnp.where(here, coarse, turned)
        spread_rows[PLANE + start_row:PLANE + start_row + count] = jnp.where(here, turned, coarse)

        def add(row, sums):
            first, second = sums
            return (first + entries[row] * spread_rows[pl.ds(row, 1)],
                    second + entries[PLANE + row] * spread_rows[pl.ds(PLANE + row, 1)])

        return lax.fori_loop(start_row, start_row + count, add, sums, unroll=True)

    def make_steps():
        power = cstep_ref[...]
        step_h, step_l = split(jnp.where(in_class, jnp.concatenate([power] * CLASSES, axis=1), 0.0))
        step_all = jnp.concatenate([step_h, step_h, step_l], axis=1)
        for d in range(last):
            if d > 0:
                power_h, power_l = split(power)
                power = dot(step_all, jnp.concatenate([power_h, power_l, power_h], axis=0))
            ms[:, d * 128:(d + 1) * 128] = made(power)

    def operands(coarse):
        high = coarse.astype(BF16).astype(F32)
        low = coarse - high
        here = tiled(left, PLANE)
        turned = turn(high)
        return jnp.concatenate([
            jnp.where(here, high, turn(low)), jnp.where(here, turned, low),
            jnp.where(here, high, 0.0), jnp.where(here, turned, 0.0)], axis=0).astype(BF16)

    def selected(product, kinds):
        kinds = jnp.broadcast_to(kinds, (COARSE, 128))
        picked = jnp.where(kinds == 0, product[:COARSE], 0.0)
        for cl in range(1, CLASSES):
            picked = jnp.where(kinds == cl, product[cl * COARSE:(cl + 1) * COARSE], picked)
        picked = picked + turn(picked)
        return jnp.where(tiled(left, PLANE), picked[:PLANE], picked[PLANE:])

    def classes(mat, right):
        return selected(dot(mat, right), tab_s[0, 6:7])

    even = (sub & 1) == 0

    def restrict(value):
        n = value.shape[0] // 64
        pairs = value.reshape(n, 2, 2, 2, 8, 128)
        pairs = pairs[:, 0] + pairs[:, 1]
        pairs = pairs[:, :, 0] + pairs[:, :, 1]
        first = pairs[:, 0].reshape(n * 8, 128)
        second = pairs[:, 1].reshape(n * 8, 128)
        return jnp.where(tiled(even, n * 8), first + along_y(first, -1), second + along_y(second, 1))

    def prolong(coarse):
        here = tiled(even, PLANE)
        first = jnp.where(here, coarse, along_y(coarse, 1)).reshape(4, 1, 1, 1, 8, 128)
        second = jnp.where(here, along_y(coarse, -1), coarse).reshape(4, 1, 1, 1, 8, 128)
        both = jnp.concatenate([first, second], axis=2)
        return jnp.broadcast_to(both, (4, 2, 2, 2, 8, 128)).reshape(256, 128)

    def ghost(plane, face, at):
        return jnp.where(tiled(tmask[at, face], PLANE) > 0.0, lanes_from(plane, tidx[at, face]), 0.0)

    def picked_from(value, face, at):
        return jnp.where(
            tiled(tmask[at, face], value.shape[0]) > 0.0, lanes_from(value, tidx[at, face]), 0.0)

    def beside_xy(value, at):
        size = value.shape[0]
        n = size // PLANE
        cube = value.reshape(n, 4, 8, 128)
        part = [cube[:, j].reshape(n * 8, 128) for j in range(4)]
        low = picked_from(part[3], 0, at)
        high = picked_from(part[0], 1, at)
        here = tiled(sub, n * 8)
        edges = along_y(part[0], 1)
        for j in range(1, 8):
            edges = jnp.where(here == j, along_y(part[j % 4], j + 1 if j < 4 else j), edges)
        edges = picked_from(edges, 2, at)
        sums = []
        for j in range(4):
            total = (part[j - 1] if j > 0 else low) + (part[j + 1] if j < 3 else high)
            total = total + jnp.where(here == 0, along_y(edges, -j), along_y(part[j], 1))
            total = total + jnp.where(here == 7, along_y(edges, 3 - j), along_y(part[j], -1))
            sums.append(total.reshape(n, 1, 8, 128))
        return jnp.concatenate(sums, axis=1).reshape(size, 128)

    def inner(value):
        zero = jnp.zeros((PLANE, 128), F32)
        total = beside_xy(value, 0)
        total = total + jnp.concatenate([zero, value[:-PLANE]], axis=0)
        return total + jnp.concatenate([value[PLANE:], zero], axis=0)

    def ended(total, below, above):
        return jnp.concatenate([
            total[:PLANE] + ghost(below, 4, 0), total[PLANE:-PLANE],
            total[-PLANE:] + ghost(above, 5, 0)], axis=0)

    def scaled(which, at, size):
        return tiled(tscale[at, which], size)

    def relax(value, driven, total, at):
        return (1.0 - DAMP) * value + driven + scaled(0, at, value.shape[0]) * total

    def slab_below(slab, driven, own):
        cross = ghost(own[:PLANE], 5, 1)
        near = slab[PLANE:]
        upper = jnp.concatenate([slab[2 * PLANE:], cross], axis=0) if slab.shape[0] > 2 * PLANE else cross
        return relax(near, driven, beside_xy(near, 1) + slab[:-PLANE] + upper, 1)

    def slab_above(slab, driven, own):
        cross = ghost(own[-PLANE:], 4, 2)
        near = slab[:-PLANE]
        lower = jnp.concatenate([cross, slab[:-2 * PLANE]], axis=0) if slab.shape[0] > 2 * PLANE else cross
        return relax(near, driven, beside_xy(near, 2) + slab[PLANE:] + lower, 2)

    def begun(value, driven):
        total = inner(value)
        mid = relax(value[PLANE:-PLANE], driven[PLANE:-PLANE], total[PLANE:-PLANE], 0)
        around = beside_xy(mid, 0)
        deep = around[PLANE:-PLANE] + mid[:-2 * PLANE] + mid[2 * PLANE:]
        return total, mid, around, deep

    def ended2(value, driven, begin, below, above, below_d, above_d):
        total, mid, around, _ = begin
        low = relax(value[:PLANE], driven[:PLANE], total[:PLANE] + ghost(below[-PLANE:], 4, 0), 0)
        high = relax(value[-PLANE:], driven[-PLANE:], total[-PLANE:] + ghost(above[:PLANE], 5, 0), 0)
        below = slab_below(below, below_d, value)
        above = slab_above(above, above_d, value)
        sides = beside_xy(jnp.concatenate([low, high], axis=0), 0)
        sums_low = jnp.concatenate([
            sides[:PLANE] + mid[:PLANE] + ghost(below[-PLANE:], 4, 0),
            around[:PLANE] + low + mid[PLANE:2 * PLANE]], axis=0)
        sums_high = jnp.concatenate([
            around[-PLANE:] + mid[-2 * PLANE:-PLANE] + high,
            sides[PLANE:] + mid[-PLANE:] + ghost(above[:PLANE], 5, 0)], axis=0)
        return low, high, sums_low, sums_high, below, above

    def left_over(value, driven, sums):
        rest = driven - DAMP * value + scaled(0, 0, value.shape[0]) * sums
        return scaled(2, 0, value.shape[0] // 8) * restrict(rest)

    def correction_begun(driven):
        begin = begun(driven, driven)
        mid, deep = begin[1], begin[3]
        zero = jnp.zeros((PLANE, 128), F32)
        return begin, add_inverse(
            left_over(mid[PLANE:-PLANE], driven[2 * PLANE:-2 * PLANE], deep), 8, (zero, zero))

    def corrected(driven, begin, part, below, above):
        low, high, sums_low, sums_high, _, _ = ended2(
            driven, driven, begin, below, above, below[PLANE:], above[:-PLANE])
        mid = begin[1]
        part = add_inverse(left_over(
            jnp.concatenate([low, mid[:PLANE]], axis=0), driven[:2 * PLANE], sums_low), 0, part)
        part = add_inverse(left_over(
            jnp.concatenate([mid[-PLANE:], high], axis=0), driven[-2 * PLANE:], sums_high), 24, part)
        return jnp.concatenate([low, mid, high], axis=0) + prolong(part[0] + part[1])

    def sweep_middle(begin, driven):
        return relax(begin[1][PLANE:-PLANE], driven[2 * PLANE:-2 * PLANE], begin[3], 0)

    def sweep_ends(value, driven, begin, below, above, below_d, above_d):
        low, high, sums_low, sums_high, below, above = ended2(
            value, driven, begin, below, above, below_d, above_d)
        mid = begin[1]
        x5_low = relax(jnp.concatenate([low, mid[:PLANE]], axis=0), driven[:2 * PLANE], sums_low, 0)
        x5_high = relax(jnp.concatenate([mid[-PLANE:], high], axis=0), driven[-2 * PLANE:], sums_high, 0)
        return x5_low, x5_high, low, high, below, above

    exchanged(table_message)
    for side in range(2):
        reached = (s > 0) if side == 0 else (s < n_sp - 1)
        make_tables(1 + side, jnp.where(reached, tab_r[side], -1))

    for off in range(1, n_sp):
        slots_landed(off)
    slots = jnp.sum(jnp.where(spot, slots_in[:, :1], 0.0), axis=2, keepdims=True)
    slots = jnp.broadcast_to(slots, (n_sp, bk, 128)).reshape(rows, 128)
    hit = slots == (iota((rows, 128), 1) & 63).astype(F32)
    place = jnp.sum(jnp.where(hit, iota((rows, 128), 0).astype(F32), 0.0), axis=0, keepdims=True)
    place = jnp.broadcast_to(place, (8, 128)).astype(jnp.int32)

    source_copy(0).wait_recv()
    put_source(0, 0, far[0])

    def settle(given, put):
        tiles = rows // 128
        for tile in range(tiles):
            shuffle[tile * CELLS:(tile + 1) * CELLS] = given[tile * 128:(tile + 1) * 128].T
        for z in range(8):
            plane = None
            for tile in range(tiles):
                both = shuffle[pl.ds(tile * CELLS + z, 64, stride=8), :]
                both = lanes_from(both, place & 127)
                both = jnp.where(tiled(left, PLANE), both[:PLANE], both[PLANE:])
                chosen_tile = tiled(lax.shift_right_logical(place, 7), PLANE) == tile
                plane = both if plane is None else jnp.where(chosen_tile, both, plane)
            put(z, plane)

    for off in range(1, n_sp):
        spread_landed(off)

    def put_start(z, plane):
        bs[z * PLANE:(z + 1) * PLANE] = plane

    settle(br[...].reshape(rows, CELLS), put_start)

    def init_copy():
        return pltpu.make_async_remote_copy(
            src_ref=bs, dst_ref=hand, send_sem=bk_sem.at[0], recv_sem=bq_sem.at[0],
            device_id=(after, s), device_id_type=MESH)

    def guess_copy():
        return pltpu.make_async_remote_copy(
            src_ref=rg_s, dst_ref=rg_r, send_sem=bk_sem.at[1], recv_sem=bq_sem.at[1],
            device_id=(before, s), device_id_type=MESH)

    def mine_copy():
        return pltpu.make_async_remote_copy(
            src_ref=hsrc, dst_ref=mine, send_sem=bk_sem.at[2], recv_sem=bq_sem.at[2],
            device_id=(after, s), device_id_type=MESH)

    def hand_copy(at):
        first, count = ((2 * PLANE, 4 * PLANE), (0, 2 * PLANE), (6 * PLANE, 2 * PLANE))[at]
        return pltpu.make_async_remote_copy(
            src_ref=hsrc.at[pl.ds(first, count)], dst_ref=hand.at[pl.ds(first, count)],
            send_sem=ts_sem.at[at], recv_sem=tr_sem.at[at], device_id=(lax.rem(k + 2, n_tm), s),
            device_id_type=MESH)

    def edges_message(state, col, at):
        up = pltpu.make_async_remote_copy(
            src_ref=state.at[pl.ds(6 * PLANE, 2 * PLANE)], dst_ref=hp.at[0], send_sem=hps_sem.at[at, 0],
            recv_sem=hpr_sem.at[0], device_id=(col, lax.rem(s + 1, n_sp)), device_id_type=MESH)
        down = pltpu.make_async_remote_copy(
            src_ref=state.at[pl.ds(0, 2 * PLANE)], dst_ref=hp.at[1], send_sem=hps_sem.at[at, 1],
            recv_sem=hpr_sem.at[1], device_id=(col, lax.rem(s + n_sp - 1, n_sp)), device_id_type=MESH)
        return up, down

    def hand_edges():
        return edges_message(hsrc, lax.rem(k + 2, n_tm), 0)

    def init_edges():
        return edges_message(bs, after, 1)

    def coarse_beside(off):
        col = lax.rem(after + off, n_tm)
        up = pltpu.make_async_remote_copy(
            src_ref=cs.at[0], dst_ref=crn.at[0, off - 2], send_sem=cns_sem.at[0, off - 2],
            recv_sem=cnr_sem.at[0, off - 2], device_id=(col, lax.rem(s + 1, n_sp)), device_id_type=MESH)
        down = pltpu.make_async_remote_copy(
            src_ref=cs.at[0], dst_ref=crn.at[1, off - 2], send_sem=cns_sem.at[1, off - 2],
            recv_sem=cnr_sem.at[1, off - 2], device_id=(col, lax.rem(s + n_sp - 1, n_sp)), device_id_type=MESH)
        return up, down

    def beside_landed():
        sides = []
        for side, reached in ((0, s > 0), (1, s < n_sp - 1)):
            rights = []
            for off in range(2, n_tm):
                there = (k >= off) & reached

                @pl.when(there)
                def _():
                    coarse_beside(off)[side].wait_recv()
                rights.append(operands(jnp.where(there, crn[side, off - 2], 0.0)))
            sides.append(jnp.concatenate(rights, axis=0))
        return sides

    def one_plane(coarse):
        first = jnp.where(even, coarse, along_y(coarse, 1))
        second = jnp.where(even, along_y(coarse, -1), coarse)
        return jnp.concatenate([first, first, second, second], axis=0)

    ahead = (after, k)

    def coarse_copy(it, off):
        return pltpu.make_async_remote_copy(
            src_ref=cs.at[it], dst_ref=cr.at[it, off - 1], send_sem=cs_sem.at[it, off - 1],
            recv_sem=cr_sem.at[it, off - 1], device_id=(lax.rem(ahead[it] + off, n_tm), s), device_id_type=MESH)

    def coarse_landed(it):
        rights = []
        for off in range(1, n_tm):
            if it > 0 or off < last:
                @pl.when(k >= off)
                def _():
                    coarse_copy(it, off).wait_recv()
            rights.append(operands(jnp.where(k >= off, cr[it, off - 1], 0.0)))
        return jnp.concatenate(rights, axis=0)

    def plane_out(state, kept, at):
        for z in range(8):
            shuffle[pl.ds(z, PLANE, stride=8), :] = state[z * PLANE:(z + 1) * PLANE]
        flat = shuffle[0:256].T
        kept[at] = jnp.concatenate([flat[:64], flat[64:]], axis=1)


    rights = None
    for it in range(ITERS):
        if it == 0:
            drv[0] = scaled(1, 0, 256) * (bs[...] + src[0, 0])
            exchange(first_message(0))
            rg_s[...] = restrict(bs[...])

            @pl.when(k < last)
            def _():
                guess_copy().start()

            @pl.when(k == last)
            def _():
                init_copy().start()
                exchange(init_edges())
        else:
            rights = coarse_landed(it - 1)
            beside_rights = beside_landed()
            product = dot(
                ms[:, :(last - 1) * 128], jnp.concatenate([rights[128:], *beside_rights], axis=1))
            pushed = prolong(selected(product[:, :128], tab_s[0, 6:7]))
            pushed_b = one_plane(selected(product[:, 128:256], tab_r[0, 6:7])[3 * 8:])
            pushed_a = one_plane(selected(product[:, 256:], tab_r[1, 6:7])[:8])
            exchanged(first_source)
            exchanged(hand_edges())
            below_d = scaled(1, 1, 2 * PLANE) * (hp[0] + jnp.concatenate([pushed_b] * 2, axis=0) + srcf[0])
            above_d = scaled(1, 2, 2 * PLANE) * (hp[1] + jnp.concatenate([pushed_a] * 2, axis=0) + srcf[1])
            e1[it, 0, PLANE:] = below_d
            e1[it, 1, :2 * PLANE] = above_d

            @pl.when(k > 0)
            def _():
                for at in range(3):
                    hand_copy(at).wait_recv()

            @pl.when(k == 0)
            def _():
                init_copy().wait_recv()
            drv[it] = scaled(1, 0, 256) * (hand[...] + pushed + src[1, 0])
            exchange(first_message(it))
            mine_copy().start()
        driven = drv[it]
        begin, part = correction_begun(driven)
        if it == 0:
            source_copy(1).wait_recv()
            put_source(0, 1, far[1])
            exchange(source_message(0))
            exchanged(first_message(it))
            below_d, above_d = e1[it, 0, PLANE:], e1[it, 1, :-PLANE]
        x3a[it] = corrected(driven, begin, part, below_d, above_d)
        exchange(deep_message(it))
        x3 = x3a[it]
        begin = begun(x3, driven)
        x5_mid = sweep_middle(begin, driven)
        if it == 0:
            make_steps()
        exchanged(source_message(it))
        if it > 0:
            @pl.when(k == last)
            def _():
                init_copy().wait_send()
                drained(init_edges())
                for off in range(1, n_sp):
                    own_landed(off)
                settle(gr[...].reshape(rows, CELLS), put_start)
        if it > 0:
            exchanged(first_message(it))
        exchanged(deep_message(it))
        x5_low, x5_high, x4_low, x4_high, below4, above4 = sweep_ends(
            x3, driven, begin, e2[it, 0], e2[it, 1], e1[it, 0], e1[it, 1])
        x5 = jnp.concatenate([x5_low, x5_mid, x5_high], axis=0)
        below5 = slab_below(below4, e1[it, 0, PLANE:], x4_low)
        above5 = slab_above(above4, e1[it, 1, :-PLANE], x4_high)
        xf[...] = x5
        driven = scaled(1, 0, 256) * (x5 + src[it, 1])
        below_d = scaled(1, 1, 2 * PLANE) * (below5 + srch[it, 0])
        above_d = scaled(1, 2, 2 * PLANE) * (above5 + srch[it, 1])
        begin, part = correction_begun(driven)
        x3b[it] = corrected(driven, begin, part, below_d, above_d)
        exchange(second_message(it))
        x3 = x3b[it]
        begin = begun(x3, driven)
        x5_mid = sweep_middle(begin, driven)
        if it < ITERS - 1:
            hsrc[2 * PLANE:6 * PLANE] = x5_mid

            @pl.when(k != last - 1)
            def _():
                hand_copy(0).start()
        if it == 0:
            for fine in range(2):
                put_source(1, fine, source_ref[0, fine])
            exchange(first_source)

            @pl.when(k != last - 1)
            def _():
                guess_copy().wait_recv()
        else:
            mine_copy().wait_recv()
            st[...] = bs[...] + (prolong(classes(ms[...], rights)) + (mine[...] - bs[...]))
        if it == ITERS - 1:
            plane_out(xf, both_ref, 1)
        exchanged(second_message(it))
        x5_low, x5_high, _, _, _, _ = sweep_ends(
            x3, driven, begin, e4[it, 0], e4[it, 1], below_d[PLANE:], above_d[:-PLANE])
        if it < ITERS - 1:
            hsrc[:2 * PLANE] = x5_low
            hsrc[6 * PLANE:] = x5_high

            @pl.when(k != last - 1)
            def _():
                exchange(hand_edges())
                cs[it] = restrict(hsrc[...]) - rg_r[...]
                for off in range(1, last):
                    @pl.when(after + off < n_tm)
                    def _():
                        coarse_copy(it, off).start()
                for off in range(2, n_tm):
                    @pl.when(after + off < n_tm)
                    def _():
                        exchange(coarse_beside(off))
                for at in (1, 2):
                    hand_copy(at).start()

            @pl.when(k == last)
            def _():
                cr[it, last - 1] = cs[it]
                for off in range(1, n_sp):
                    own_copy(off).start()
            exchange(source_message(1))
        else:
            residual = jnp.concatenate([x5_low, x5_mid, x5_high], axis=0) - st[...]
            cs[it] = restrict(residual)
            for off in range(1, n_tm):
                @pl.when(k + off < n_tm)
                def _():
                    coarse_copy(it, off).start()
            rights = coarse_landed(it)
            xf[...] = st[...] + (prolong(classes(ms[...], rights)) + residual)

    plane_out(xf, both_ref, 0)

    for off in range(1, n_sp):
        slots_copy(off).wait_send()
        spread_copy(off).wait_send()
    for fine in range(2):
        source_copy(fine).wait_send()
    mine_copy().wait_send()

    @pl.when(k == last)
    def _():
        for off in range(1, n_sp):
            own_copy(off).wait_send()

    @pl.when(k < last)
    def _():
        guess_copy().wait_send()

    drained(table_message)
    drained(first_source)
    for it in range(ITERS):
        drained(source_message(it))
        drained(first_message(it))
        drained(deep_message(it))
        drained(second_message(it))
    for off in range(1, n_tm):
        @pl.when(k + off < n_tm)
        def _():
            coarse_copy(1, off).wait_send()
    for off in range(1, last):
        @pl.when((k != last - 1) & (after + off < n_tm))
        def _():
            coarse_copy(0, off).wait_send()

    @pl.when(k != last - 1)
    def _():
        for at in range(3):
            hand_copy(at).wait_send()
        drained(hand_edges())
        for off in range(2, n_tm):
            @pl.when(after + off < n_tm)
            def _():
                drained(coarse_beside(off))


def solution(mesh):
    n_tm, n_sp = mesh.shape["tm"], mesh.shape["space"]

    def body(init_state, guess, source, remap, neighbors, block_class, step_number, inverse, cstep):
        nb = init_state.shape[0]
        bk = -(-(2 * nb // n_sp) // 8) * 8
        tiles = n_sp * bk // 128
        slots = 4 + 3 * ITERS
        dma = pltpu.SemaphoreType.DMA
        full = 8 * PLANE

        def vmem(*shape, dtype=F32):
            return pltpu.VMEM(shape, dtype)

        both = pl.pallas_call(
            functools.partial(kernel, n_tm, n_sp, bk),
            name="mgrit",
            out_shape=vmem(2, nb, CELLS),
            in_specs=[pl.BlockSpec(memory_space=pl.ANY)] * 9,
            out_specs=pl.BlockSpec(memory_space=pltpu.VMEM),
            scratch_shapes=[
                vmem(nb, CELLS), vmem(1, nb, CELLS), vmem(1, 2, nb, CELLS), vmem(1, nb, dtype=jnp.int32),
                vmem(6, nb, dtype=jnp.int32), vmem(1, nb, dtype=jnp.int32), vmem(1, CLASSES),
                vmem(CLASSES * COARSE, COARSE), vmem(CLASSES * COARSE, COARSE),
                vmem(2, n_sp, bk, CELLS), vmem(n_sp, bk, CELLS), vmem(n_sp, bk, CELLS), vmem(2, nb, CELLS),
                vmem(2, 8, 128, dtype=jnp.int32), vmem(2, 8, 128, dtype=jnp.int32),
                vmem(3, 6, 8, 128, dtype=jnp.int32), vmem(3, 6, 8, 128), vmem(3, 3, 8, 128),
                vmem(ITERS, 2, full, 128), vmem(ITERS, 2, 2 * PLANE, 128), vmem(2, 2 * PLANE, 128), vmem(tiles * CELLS, 128),
                vmem(full, 128), vmem(ITERS, full, 128), vmem(ITERS, full, 128), vmem(ITERS, full, 128),
                vmem(ITERS, 2, 3 * PLANE, 128), vmem(ITERS, 2, 4 * PLANE, 128), vmem(ITERS, 2, 2 * PLANE, 128),
                vmem(full, 128), vmem(full, 128), vmem(full, 128), vmem(full, 128), vmem(2, 2 * PLANE, 128), vmem(full, 128),
                vmem(PLANE, 128), vmem(PLANE, 128),
                vmem(ITERS, PLANE, 128), vmem(ITERS, n_tm - 1, PLANE, 128), vmem(2, n_tm - 2, PLANE, 128),
                vmem(4, PLANE, 128), vmem(2 * PLANE, 128), vmem(COARSE, PLANE, 128), vmem(CLASSES * COARSE, (n_tm - 1) * 128, dtype=BF16),
                vmem(n_sp, 8, 128), vmem(n_sp, 8, 128),
                dma((9,)), dma((n_sp,)), dma((n_sp,)),
                dma((n_sp,)), dma((n_sp,)), dma((n_sp,)), dma((n_sp,)),
                dma((slots, 2)), dma((slots, 2)),
                dma((3,)), dma((3,)), dma((3,)), dma((3,)),
                dma((ITERS, n_tm - 1)), dma((ITERS, n_tm - 1)), dma((2,)), dma((2,)),
                dma((2, 2)), dma((2,)), dma((2, n_tm - 2)), dma((2, n_tm - 2)),
            ],
            compiler_params=pltpu.CompilerParams(collective_id=0, has_side_effects=True),
        )(
            init_state, guess, source, remap.reshape(1, nb), neighbors.T, block_class.reshape(1, nb),
            step_number.reshape(1, CLASSES), inverse.reshape(CLASSES * COARSE, COARSE),
            cstep.reshape(CLASSES * COARSE, COARSE),
        )
        return both[:1], both[1:]

    placed = (
        P("space", None), P("tm", "space", None), P("tm", None, "space", None), P("space"),
        P("space", None), P("space"), P(), P(), P(),
    )
    return jax.shard_map(
        body, mesh=mesh, in_specs=placed,
        out_specs=(P("tm", "space", None), P("tm", "space", None)), check_vma=False,
    )
```

```python
import functools

import jax
import jax.numpy as jnp
from jax import lax
from jax.experimental import pallas as pl
from jax.experimental.pallas import tpu as pltpu
from jax.sharding import PartitionSpec as P

CELLS = 512
COARSE = 64
CLASSES = 4
ITERS = 2
DAMP = 0.8
PLANE = 32
MESH = pl.DeviceIdType.MESH
F32 = jnp.float32
BF16 = jnp.bfloat16


def split(value):
    high = value.astype(BF16)
    return high, (value - high.astype(F32)).astype(BF16)


def dot(left, right):
    return jnp.dot(left, right, preferred_element_type=F32)


def iota(shape, dim):
    return lax.broadcasted_iota(jnp.int32, shape, dim)


def turn(value):
    return pltpu.roll(value, 64, 1)


def along_y(value, shift):
    rows = value.shape[0]
    return pltpu.roll(value.reshape(rows // 8, 8, 128), shift % 8, 1).reshape(rows, 128)


def tiled(table, rows):
    return jnp.broadcast_to(table[None], (rows // 8, 8, 128)).reshape(rows, 128)


def lanes_from(value, index):
    return jnp.take_along_axis(
        value, tiled(index, value.shape[0]), axis=1, mode="promise_in_bounds")


def partner(s, off, n):
    if n & (n - 1):
        return lax.rem(s + off, n)
    to = s
    for bit in range(n.bit_length() - 1):
        if off >> bit & 1:
            to = to + (1 - 2 * lax.rem(lax.div(s, 1 << bit), 2)) * (1 << bit)
    return to


def kernel(
    n_tm, n_sp, bk,
    init_hbm, guess_hbm, source_hbm, remap_hbm, nb_hbm, class_hbm, step_hbm, inv_hbm, cstep_hbm,
    both_ref,
    init_ref, guess_ref, source_ref, remap_ref, nb_ref, class_ref, step_ref, inv_ref, cstep_ref,
    gb, br, gr, far, tab_s, tab_r, tidx, tmask, tscale, src, srch, srcf, shuffle,
    bs, drv, x3a, x3b, e1, e2, e4, st, xf, hsrc, hand, hp, mine, rg_s, rg_r, cs, cr, crn, table, spread_rows, entries, ms,
    slots_out, slots_in, in_sem, so_sem, si_sem,
    gs_sem, gr_sem, ps_sem, br_sem, hs_sem, hr_sem, ts_sem, tr_sem, bk_sem, bq_sem, cs_sem, cr_sem, fs_sem, fr_sem,
    hps_sem, hpr_sem, cns_sem, cnr_sem,
):
    k = lax.axis_index("tm")
    s = lax.axis_index("space")
    nb = init_hbm.shape[0]
    rows = n_sp * bk
    bits = nb.bit_length() - 1
    last = n_tm - 1

    after, before = lax.rem(k + 1, n_tm), lax.rem(k + last, n_tm)

    barrier = pltpu.get_barrier_semaphore()

    def greet(tm, space):
        pl.semaphore_signal(barrier, inc=1, device_id=(tm, space), device_id_type=MESH)

    for off in range(1, n_sp):
        greet(k, partner(s, off, n_sp))
    for off in range(1, n_tm):
        greet(lax.rem(k + off, n_tm), s)

        @pl.when(s > 0)
        def _():
            greet(lax.rem(k + off, n_tm), s - 1)

        @pl.when(s < n_sp - 1)
        def _():
            greet(lax.rem(k + off, n_tm), s + 1)

    loads = [
        pltpu.make_async_copy(given, kept, in_sem.at[at]) for at, (given, kept) in enumerate((
            (remap_hbm, remap_ref), (guess_hbm, guess_ref), (init_hbm, init_ref), (nb_hbm, nb_ref),
            (class_hbm, class_ref), (step_hbm, step_ref), (source_hbm, source_ref), (inv_hbm, inv_ref),
            (cstep_hbm, cstep_ref)))]
    for load in loads:
        load.start()
    loads[0].wait()

    eye = iota((nb, nb), 0) == iota((nb, nb), 1)

    def column(row):
        return jnp.sum(jnp.where(eye, row, 0.0), axis=1, keepdims=True)

    remap_row = remap_ref[...]
    target_row = lax.shift_right_logical(remap_row, bits)
    slot_row = (remap_row - lax.shift_left(target_row, bits)).astype(F32)
    target_f = target_row.astype(F32)
    same = (column(target_f) == target_f) & (iota((nb, nb), 0) < iota((nb, nb), 1))
    pos_row = jnp.sum(jnp.where(same, 1.0, 0.0), axis=0, keepdims=True)
    send_row = target_f * float(bk) + pos_row
    chosen = iota((rows, nb), 0).astype(F32) == send_row
    send_mat = jnp.where(chosen, 1.0, 0.0)
    slot_col = jnp.sum(jnp.where(chosen, slot_row + 1.0, 0.0), axis=1, keepdims=True) - 1.0
    send_mat = jnp.concatenate([send_mat, send_mat], axis=1).astype(BF16)

    def bucketed(value):
        return dot(send_mat, jnp.concatenate(split(value), axis=0)).reshape(n_sp, bk, CELLS)

    spot = iota((n_sp, bk, 128), 1) == iota((n_sp, bk, 128), 2)
    slot_wide = jnp.broadcast_to(slot_col, (rows, 128)).reshape(n_sp, bk, 128)
    slot_lanes = jnp.sum(jnp.where(spot, slot_wide, 0.0), axis=1, keepdims=True)
    slots_out[...] = jnp.broadcast_to(slot_lanes, (n_sp, 8, 128))
    loads[1].wait()
    loads[2].wait()
    gb[0] = bucketed(guess_ref[0])

    @pl.when(k == last)
    def _():
        gb[1] = bucketed(init_ref[...])

    for load in loads[3:6]:
        load.wait()

    linked = nb_ref[...]
    face_no = iota((6, nb), 0)
    run = s + jnp.where(face_no == 4, -1, jnp.where(face_no == 5, 1, 0))
    linked = jnp.where(linked >= 0, linked - run * nb, -1)
    tab_s[0, 0:6] = jnp.concatenate([linked, linked], axis=1)
    kind = class_ref[...]
    tab_s[0, 6:7] = jnp.concatenate([kind, kind], axis=1)
    tab_s[0, 7:8] = jnp.zeros((1, 128), jnp.int32)
    tab_s[1] = tab_s[0]

    beside = jnp.minimum(s, 1) + jnp.minimum(n_sp - 1 - s, 1)
    pl.semaphore_wait(barrier, n_sp - 1 + (n_tm - 1) * (1 + beside))

    up_to = (k, lax.rem(s + 1, n_sp))
    down_to = (k, lax.rem(s + n_sp - 1, n_sp))

    def halo_up(slot, source, target):
        return pltpu.make_async_remote_copy(
            src_ref=source, dst_ref=target, send_sem=hs_sem.at[slot, 0],
            recv_sem=hr_sem.at[slot, 0], device_id=up_to, device_id_type=MESH)

    def halo_down(slot, source, target):
        return pltpu.make_async_remote_copy(
            src_ref=source, dst_ref=target, send_sem=hs_sem.at[slot, 1],
            recv_sem=hr_sem.at[slot, 1], device_id=down_to, device_id_type=MESH)

    def planes_message(slot, state, depth, target):
        size = depth * PLANE
        return (halo_up(slot, state.at[pl.ds(8 * PLANE - size, size)], target.at[0]),
                halo_down(slot, state.at[pl.ds(0, size)], target.at[1]))

    def exchange(message):
        up, down = message

        @pl.when(s < n_sp - 1)
        def _():
            up.start()

        @pl.when(s > 0)
        def _():
            down.start()

    def exchanged(message):
        up, down = message

        @pl.when(s > 0)
        def _():
            up.wait_recv()

        @pl.when(s < n_sp - 1)
        def _():
            down.wait_recv()

    def drained(message):
        up, down = message

        @pl.when(s < n_sp - 1)
        def _():
            up.wait_send()

        @pl.when(s > 0)
        def _():
            down.wait_send()

    table_message = (halo_up(0, tab_s.at[0], tab_r.at[0]), halo_down(0, tab_s.at[1], tab_r.at[1]))

    def source_message(it):
        return planes_message(1 + it, src.at[it, 1], 2, srch.at[it])

    first_source = planes_message(3 + 3 * ITERS, src.at[1, 0], 2, srcf)

    near_message = (
        halo_up(4 + 3 * ITERS, drv.at[0, pl.ds(6 * PLANE, 2 * PLANE)], e1.at[0, 0, pl.ds(PLANE, 2 * PLANE)]),
        halo_down(4 + 3 * ITERS, drv.at[0, pl.ds(0, 2 * PLANE)], e1.at[0, 1, pl.ds(0, 2 * PLANE)]))

    def first_message(it):
        return (halo_up(3 + 3 * it, drv.at[it, pl.ds(5 * PLANE, PLANE)], e1.at[it, 0, pl.ds(0, PLANE)]),
                halo_down(3 + 3 * it, drv.at[it, pl.ds(2 * PLANE, PLANE)], e1.at[it, 1, pl.ds(2 * PLANE, PLANE)]))

    def deep_message(it):
        return planes_message(4 + 3 * it, x3a.at[it], 4, e2.at[it])

    def second_message(it):
        return planes_message(5 + 3 * it, x3b.at[it], 2, e4.at[it])

    which = jnp.maximum(k - last + 1, 0)

    def spread_copy(off):
        to = partner(s, off, n_sp)
        return pltpu.make_async_remote_copy(
            src_ref=gb.at[which, to], dst_ref=br.at[s], send_sem=ps_sem.at[off], recv_sem=br_sem.at[s],
            device_id=(k, to), device_id_type=MESH)

    def spread_landed(off):
        origin = partner(s, off, n_sp)
        pltpu.make_async_remote_copy(
            src_ref=gb.at[0, origin], dst_ref=br.at[origin], send_sem=ps_sem.at[off],
            recv_sem=br_sem.at[origin], device_id=(k, origin), device_id_type=MESH).wait_recv()

    def own_copy(off):
        to = partner(s, off, n_sp)
        return pltpu.make_async_remote_copy(
            src_ref=gb.at[0, to], dst_ref=gr.at[s], send_sem=gs_sem.at[off],
            recv_sem=gr_sem.at[s], device_id=(k, to), device_id_type=MESH)

    def own_landed(off):
        origin = partner(s, off, n_sp)
        pltpu.make_async_remote_copy(
            src_ref=gb.at[0, origin], dst_ref=gr.at[origin],
            send_sem=gs_sem.at[off], recv_sem=gr_sem.at[origin], device_id=(k, origin),
            device_id_type=MESH).wait_recv()

    def slots_copy(off):
        to = partner(s, off, n_sp)
        return pltpu.make_async_remote_copy(
            src_ref=slots_out.at[to, pl.ds(0, 1)], dst_ref=slots_in.at[s, pl.ds(0, 1)], send_sem=so_sem.at[off],
            recv_sem=si_sem.at[s], device_id=(k, to), device_id_type=MESH)

    def slots_landed(off):
        origin = partner(s, off, n_sp)
        pltpu.make_async_remote_copy(
            src_ref=slots_out.at[origin, pl.ds(0, 1)], dst_ref=slots_in.at[origin, pl.ds(0, 1)], send_sem=so_sem.at[off],
            recv_sem=si_sem.at[origin], device_id=(k, origin), device_id_type=MESH).wait_recv()

    for off in reversed(range(1, n_sp)):
        slots_copy(off).start()
    exchange(table_message)
    for off in reversed(range(1, n_sp)):
        spread_copy(off).start()

    def source_copy(fine):
        return pltpu.make_async_remote_copy(
            src_ref=source_ref.at[0, fine], dst_ref=far.at[fine], send_sem=fs_sem.at[fine],
            recv_sem=fr_sem.at[fine], device_id=(before, s), device_id_type=MESH)

    for load in loads[6:]:
        load.wait()
    source_copy(0).start()
    source_copy(1).start()
    br[s] = gb[which, s]
    slots_in[s] = slots_out[s]
    gr[s] = gb[0, s]

    lane = iota((8, 128), 1)
    sub = iota((8, 128), 0)
    left = lane < 64
    half = lane & 64

    def blocks_in_lanes(value):
        return jnp.concatenate([value[:, :CELLS // 2], value[:, CELLS // 2:]], axis=0).T

    def put_source(it, fine, value):
        shuffle[0:256] = blocks_in_lanes(value)
        for z in range(8):
            src[it, fine, z * PLANE:(z + 1) * PLANE] = shuffle[pl.ds(z, PLANE, stride=8), :]

    def make_tables(at, table):
        faces = [jnp.broadcast_to(table[face:face + 1], (8, 128)) for face in range(7)]
        inside = [jnp.maximum(face, 0) for face in faces]
        index = [
            jnp.where(left, inside[0] + 64, lane - 64), jnp.where(left, lane + 64, inside[1]),
            half + jnp.where(sub < 4, inside[2], inside[3]), lane,
            half + inside[4], half + inside[5],
        ]
        known = [jnp.where(face >= 0, 1.0, 0.0) for face in faces[:6]]
        mask = [
            jnp.where(left, known[0], 1.0), jnp.where(left, 1.0, known[1]),
            jnp.where(sub < 4, known[2], known[3]), known[2],
            known[4], known[5],
        ]
        for face in range(6):
            tidx[at, face] = index[face]
            tmask[at, face] = mask[face]
        dif = jnp.zeros((8, 128), F32)
        for cl in range(CLASSES):
            dif = dif + jnp.where(faces[6] == cl, step_ref[:, cl:cl + 1], 0.0)
        tscale[at, 0] = DAMP * dif / (1.0 + 6.0 * dif)
        tscale[at, 1] = DAMP / (1.0 + 6.0 * dif)
        tscale[at, 2] = (1.0 + 6.0 * dif) / DAMP

    make_tables(0, tab_s[0])

    def coarse_of(row):
        high = lax.shift_right_logical(row, 5) * 2 + (row & 1)
        return high * 16 + (lax.shift_right_logical(row, 1) & 3) * 4 + (lax.shift_right_logical(row, 3) & 3)

    size = CLASSES * COARSE
    in_class = (lax.shift_right_logical(iota((size, size), 0), 6)
                == lax.shift_right_logical(iota((size, size), 1), 6))
    tall = jnp.where(in_class & (coarse_of(iota((size, size), 0) & 63) == (iota((size, size), 1) & 63)),
                     1.0, 0.0).astype(BF16)
    wide = jnp.where(coarse_of(iota((COARSE, COARSE), 1)) == iota((COARSE, COARSE), 0), 0.125, 0.0).astype(BF16)

    def made(given):
        parts = [dot(tall, dot(piece, wide).astype(BF16)).astype(BF16) for piece in split(given)]
        return jnp.concatenate(parts, axis=1)

    both = made(inv_ref[...])
    lanes = CLASSES * 2 * COARSE
    blocks = [
        jnp.concatenate([both[at * PLANE:(at + 1) * PLANE, part * COARSE:(part + 1) * COARSE]
                         for at in range(2 * CLASSES)], axis=1) for part in range(2)]
    at_row, at_lane = iota((lanes, lanes), 0), iota((lanes, lanes), 1)
    place_of = ((at_row & 63) * 8 + (lax.shift_right_logical(at_row, 6) & 1) * 4
                + lax.shift_right_logical(at_row, 7))
    moved = dot(jnp.concatenate(blocks, axis=0), jnp.where(place_of == at_lane, 1.0, 0.0).astype(BF16))
    moved = moved[:PLANE] + moved[PLANE:]
    for group in range(4):
        table[group] = moved[:, group * 128:(group + 1) * 128]
    start = jnp.broadcast_to(tab_s[0, 6:7], (8, 128)) + lax.shift_right_logical(lane, 6) * 4

    def make_entries(i, carry):
        for group in range(4):
            entries[group * 16 + i] = lanes_from(table[group], start + 8 * i)
        return carry

    lax.fori_loop(0, 16, make_entries, 0)


    def add_inverse(coarse, start_row, sums):
        count = coarse.shape[0]
        here = tiled(left, count)
        turned = turn(coarse)
        spread_rows[start_row:start_row + count] = jnp.where(here, coarse, turned)
        spread_rows[PLANE + start_row:PLANE + start_row + count] = jnp.where(here, turned, coarse)

        def add(row, sums):
            first, second = sums
            return (first + entries[row] * spread_rows[pl.ds(row, 1)],
                    second + entries[PLANE + row] * spread_rows[pl.ds(PLANE + row, 1)])

        return lax.fori_loop(start_row, start_row + count, add, sums, unroll=True)

    def make_steps():
        power = cstep_ref[...]
        step_h, step_l = split(jnp.where(in_class, jnp.concatenate([power] * CLASSES, axis=1), 0.0))
        step_all = jnp.concatenate([step_h, step_h, step_l], axis=1)
        for d in range(last):
            if d > 0:
                power_h, power_l = split(power)
                power = dot(step_all, jnp.concatenate([power_h, power_l, power_h], axis=0))
            ms[:, d * 128:(d + 1) * 128] = made(power)

    def operands(coarse):
        high = coarse.astype(BF16).astype(F32)
        low = coarse - high
        here = tiled(left, PLANE)
        turned = turn(high)
        return jnp.concatenate([
            jnp.where(here, high, turn(low)), jnp.where(here, turned, low),
            jnp.where(here, high, 0.0), jnp.where(here, turned, 0.0)], axis=0).astype(BF16)

    def selected(product, kinds):
        kinds = jnp.broadcast_to(kinds, (COARSE, 128))
        picked = jnp.where(kinds == 0, product[:COARSE], 0.0)
        for cl in range(1, CLASSES):
            picked = jnp.where(kinds == cl, product[cl * COARSE:(cl + 1) * COARSE], picked)
        picked = picked + turn(picked)
        return jnp.where(tiled(left, PLANE), picked[:PLANE], picked[PLANE:])

    def classes(mat, right):
        return selected(dot(mat, right), tab_s[0, 6:7])

    even = (sub & 1) == 0

    def restrict(value):
        n = value.shape[0] // 64
        pairs = value.reshape(n, 2, 2, 2, 8, 128)
        pairs = pairs[:, 0] + pairs[:, 1]
        pairs = pairs[:, :, 0] + pairs[:, :, 1]
        first = pairs[:, 0].reshape(n * 8, 128)
        second = pairs[:, 1].reshape(n * 8, 128)
        return jnp.where(tiled(even, n * 8), first + along_y(first, -1), second + along_y(second, 1))

    def prolong(coarse):
        here = tiled(even, PLANE)
        first = jnp.where(here, coarse, along_y(coarse, 1)).reshape(4, 1, 1, 1, 8, 128)
        second = jnp.where(here, along_y(coarse, -1), coarse).reshape(4, 1, 1, 1, 8, 128)
        both = jnp.concatenate([first, second], axis=2)
        return jnp.broadcast_to(both, (4, 2, 2, 2, 8, 128)).reshape(256, 128)

    def ghost(plane, face, at):
        return jnp.where(tiled(tmask[at, face], PLANE) > 0.0, lanes_from(plane, tidx[at, face]), 0.0)

    def picked_from(value, face, at):
        return jnp.where(
            tiled(tmask[at, face], value.shape[0]) > 0.0, lanes_from(value, tidx[at, face]), 0.0)

    def beside_xy(value, at):
        size = value.shape[0]
        n = size // PLANE
        cube = value.reshape(n, 4, 8, 128)
        part = [cube[:, j].reshape(n * 8, 128) for j in range(4)]
        low = picked_from(part[3], 0, at)
        high = picked_from(part[0], 1, at)
        here = tiled(sub, n * 8)
        edges = along_y(part[0], 1)
        for j in range(1, 8):
            edges = jnp.where(here == j, along_y(part[j % 4], j + 1 if j < 4 else j), edges)
        edges = picked_from(edges, 2, at)
        sums = []
        for j in range(4):
            total = (part[j - 1] if j > 0 else low) + (part[j + 1] if j < 3 else high)
            total = total + jnp.where(here == 0, along_y(edges, -j), along_y(part[j], 1))
            total = total + jnp.where(here == 7, along_y(edges, 3 - j), along_y(part[j], -1))
            sums.append(total.reshape(n, 1, 8, 128))
        return jnp.concatenate(sums, axis=1).reshape(size, 128)

    def inner(value):
        zero = jnp.zeros((PLANE, 128), F32)
        total = beside_xy(value, 0)
        total = total + jnp.concatenate([zero, value[:-PLANE]], axis=0)
        return total + jnp.concatenate([value[PLANE:], zero], axis=0)

    def ended(total, below, above):
        return jnp.concatenate([
            total[:PLANE] + ghost(below, 4, 0), total[PLANE:-PLANE],
            total[-PLANE:] + ghost(above, 5, 0)], axis=0)

    def scaled(which, at, size):
        return tiled(tscale[at, which], size)

    def relax(value, driven, total, at):
        return (1.0 - DAMP) * value + driven + scaled(0, at, value.shape[0]) * total

    def slab_below(slab, driven, own):
        cross = ghost(own[:PLANE], 5, 1)
        near = slab[PLANE:]
        upper = jnp.concatenate([slab[2 * PLANE:], cross], axis=0) if slab.shape[0] > 2 * PLANE else cross
        return relax(near, driven, beside_xy(near, 1) + slab[:-PLANE] + upper, 1)

    def slab_above(slab, driven, own):
        cross = ghost(own[-PLANE:], 4, 2)
        near = slab[:-PLANE]
        lower = jnp.concatenate([cross, slab[:-2 * PLANE]], axis=0) if slab.shape[0] > 2 * PLANE else cross
        return relax(near, driven, beside_xy(near, 2) + slab[PLANE:] + lower, 2)

    def begun(value, driven):
        total = inner(value)
        mid = relax(value[PLANE:-PLANE], driven[PLANE:-PLANE], total[PLANE:-PLANE], 0)
        around = beside_xy(mid, 0)
        deep = around[PLANE:-PLANE] + mid[:-2 * PLANE] + mid[2 * PLANE:]
        return total, mid, around, deep

    def early_part(driven):
        around = beside_xy(driven, 0)
        two = driven[PLANE:-PLANE]
        two = relax(two, two, around[PLANE:-PLANE] + driven[:-2 * PLANE] + driven[2 * PLANE:], 0)
        return around, two, beside_xy(two, 0)

    def begun_later(driven, early):
        known, two, two_around = early
        zero = jnp.zeros((PLANE, 128), F32)
        sides = beside_xy(jnp.concatenate([driven[:2 * PLANE], driven[-2 * PLANE:]], axis=0), 0)
        total = jnp.concatenate([sides[:2 * PLANE], known, sides[2 * PLANE:]], axis=0)
        total = total + jnp.concatenate([zero, driven[:-PLANE]], axis=0)
        total = total + jnp.concatenate([driven[PLANE:], zero], axis=0)
        low, high = driven[PLANE:3 * PLANE], driven[-3 * PLANE:-PLANE]
        low = relax(low, low, total[PLANE:3 * PLANE], 0)
        high = relax(high, high, total[-3 * PLANE:-PLANE], 0)
        sides = beside_xy(jnp.concatenate([low, high], axis=0), 0)
        mid = jnp.concatenate([low, two, high], axis=0)
        around = jnp.concatenate([sides[:2 * PLANE], two_around, sides[2 * PLANE:]], axis=0)
        deep = around[PLANE:-PLANE] + mid[:-2 * PLANE] + mid[2 * PLANE:]
        return total, mid, around, deep

    def ended2(value, driven, begin, below, above, below_d, above_d):
        total, mid, around, _ = begin
        low = relax(value[:PLANE], driven[:PLANE], total[:PLANE] + ghost(below[-PLANE:], 4, 0), 0)
        high = relax(value[-PLANE:], driven[-PLANE:], total[-PLANE:] + ghost(above[:PLANE], 5, 0), 0)
        below = slab_below(below, below_d, value)
        above = slab_above(above, above_d, value)
        sides = beside_xy(jnp.concatenate([low, high], axis=0), 0)
        sums_low = jnp.concatenate([
            sides[:PLANE] + mid[:PLANE] + ghost(below[-PLANE:], 4, 0),
            around[:PLANE] + low + mid[PLANE:2 * PLANE]], axis=0)
        sums_high = jnp.concatenate([
            around[-PLANE:] + mid[-2 * PLANE:-PLANE] + high,
            sides[PLANE:] + mid[-PLANE:] + ghost(above[:PLANE], 5, 0)], axis=0)
        return low, high, sums_low, sums_high, below, above

    def left_over(value, driven, sums):
        rest = driven - DAMP * value + scaled(0, 0, value.shape[0]) * sums
        return scaled(2, 0, value.shape[0] // 8) * restrict(rest)

    def correction_begun(driven, early=None):
        begin = begun(driven, driven) if early is None else begun_later(driven, early)
        mid, deep = begin[1], begin[3]
        zero = jnp.zeros((PLANE, 128), F32)
        return begin, add_inverse(
            left_over(mid[PLANE:-PLANE], driven[2 * PLANE:-2 * PLANE], deep), 8, (zero, zero))

    def corrected(driven, begin, part, below, above):
        low, high, sums_low, sums_high, _, _ = ended2(
            driven, driven, begin, below, above, below[PLANE:], above[:-PLANE])
        mid = begin[1]
        part = add_inverse(left_over(
            jnp.concatenate([low, mid[:PLANE]], axis=0), driven[:2 * PLANE], sums_low), 0, part)
        part = add_inverse(left_over(
            jnp.concatenate([mid[-PLANE:], high], axis=0), driven[-2 * PLANE:], sums_high), 24, part)
        return jnp.concatenate([low, mid, high], axis=0) + prolong(part[0] + part[1])

    def sweep_middle(begin, driven):
        return relax(begin[1][PLANE:-PLANE], driven[2 * PLANE:-2 * PLANE], begin[3], 0)

    def sweep_ends(value, driven, begin, below, above, below_d, above_d):
        low, high, sums_low, sums_high, below, above = ended2(
            value, driven, begin, below, above, below_d, above_d)
        mid = begin[1]
        x5_low = relax(jnp.concatenate([low, mid[:PLANE]], axis=0), driven[:2 * PLANE], sums_low, 0)
        x5_high = relax(jnp.concatenate([mid[-PLANE:], high], axis=0), driven[-2 * PLANE:], sums_high, 0)
        return x5_low, x5_high, low, high, below, above

    exchanged(table_message)
    for side in range(2):
        reached = (s > 0) if side == 0 else (s < n_sp - 1)
        make_tables(1 + side, jnp.where(reached, tab_r[side], -1))

    for off in range(1, n_sp):
        slots_landed(off)
    slots = jnp.sum(jnp.where(spot, slots_in[:, :1], 0.0), axis=2, keepdims=True)
    slots = jnp.broadcast_to(slots, (n_sp, bk, 128)).reshape(rows, 128)
    hit = slots == (iota((rows, 128), 1) & 63).astype(F32)
    place = jnp.sum(jnp.where(hit, iota((rows, 128), 0).astype(F32), 0.0), axis=0, keepdims=True)
    place = jnp.broadcast_to(place, (8, 128)).astype(jnp.int32)

    source_copy(0).wait_recv()
    put_source(0, 0, far[0])

    def settle(given, put):
        tiles = rows // 128
        for tile in range(tiles):
            shuffle[tile * CELLS:(tile + 1) * CELLS] = given[tile * 128:(tile + 1) * 128].T
        for z in range(8):
            plane = None
            for tile in range(tiles):
                both = shuffle[pl.ds(tile * CELLS + z, 64, stride=8), :]
                both = lanes_from(both, place & 127)
                both = jnp.where(tiled(left, PLANE), both[:PLANE], both[PLANE:])
                chosen_tile = tiled(lax.shift_right_logical(place, 7), PLANE) == tile
                plane = both if plane is None else jnp.where(chosen_tile, both, plane)
            put(z, plane)

    for off in range(1, n_sp):
        spread_landed(off)

    def put_start(z, plane):
        bs[z * PLANE:(z + 1) * PLANE] = plane

    settle(br[...].reshape(rows, CELLS), put_start)

    def init_copy():
        return pltpu.make_async_remote_copy(
            src_ref=bs, dst_ref=hand, send_sem=bk_sem.at[0], recv_sem=bq_sem.at[0],
            device_id=(after, s), device_id_type=MESH)

    def guess_copy():
        return pltpu.make_async_remote_copy(
            src_ref=rg_s, dst_ref=rg_r, send_sem=bk_sem.at[1], recv_sem=bq_sem.at[1],
            device_id=(before, s), device_id_type=MESH)

    def mine_copy():
        return pltpu.make_async_remote_copy(
            src_ref=hsrc, dst_ref=mine, send_sem=bk_sem.at[2], recv_sem=bq_sem.at[2],
            device_id=(after, s), device_id_type=MESH)

    def hand_copy(at):
        first, count = ((2 * PLANE, 4 * PLANE), (0, 2 * PLANE), (6 * PLANE, 2 * PLANE))[at]
        return pltpu.make_async_remote_copy(
            src_ref=hsrc.at[pl.ds(first, count)], dst_ref=hand.at[pl.ds(first, count)],
            send_sem=ts_sem.at[at], recv_sem=tr_sem.at[at], device_id=(lax.rem(k + 2, n_tm), s),
            device_id_type=MESH)

    def edges_message(state, col, at):
        up = pltpu.make_async_remote_copy(
            src_ref=state.at[pl.ds(6 * PLANE, 2 * PLANE)], dst_ref=hp.at[0], send_sem=hps_sem.at[at, 0],
            recv_sem=hpr_sem.at[0], device_id=(col, lax.rem(s + 1, n_sp)), device_id_type=MESH)
        down = pltpu.make_async_remote_copy(
            src_ref=state.at[pl.ds(0, 2 * PLANE)], dst_ref=hp.at[1], send_sem=hps_sem.at[at, 1],
            recv_sem=hpr_sem.at[1], device_id=(col, lax.rem(s + n_sp - 1, n_sp)), device_id_type=MESH)
        return up, down

    def hand_edges():
        return edges_message(hsrc, lax.rem(k + 2, n_tm), 0)

    def init_edges():
        return edges_message(bs, after, 1)

    def coarse_beside(off):
        col = lax.rem(after + off, n_tm)
        up = pltpu.make_async_remote_copy(
            src_ref=cs.at[0], dst_ref=crn.at[0, off - 2], send_sem=cns_sem.at[0, off - 2],
            recv_sem=cnr_sem.at[0, off - 2], device_id=(col, lax.rem(s + 1, n_sp)), device_id_type=MESH)
        down = pltpu.make_async_remote_copy(
            src_ref=cs.at[0], dst_ref=crn.at[1, off - 2], send_sem=cns_sem.at[1, off - 2],
            recv_sem=cnr_sem.at[1, off - 2], device_id=(col, lax.rem(s + n_sp - 1, n_sp)), device_id_type=MESH)
        return up, down

    def beside_landed():
        sides = []
        for side, reached in ((0, s > 0), (1, s < n_sp - 1)):
            rights = []
            for off in range(2, n_tm):
                there = (k >= off) & reached

                @pl.when(there)
                def _():
                    coarse_beside(off)[side].wait_recv()
                rights.append(operands(jnp.where(there, crn[side, off - 2], 0.0)))
            sides.append(jnp.concatenate(rights, axis=0))
        return sides

    def one_plane(coarse):
        first = jnp.where(even, coarse, along_y(coarse, 1))
        second = jnp.where(even, along_y(coarse, -1), coarse)
        return jnp.concatenate([first, first, second, second], axis=0)

    ahead = (after, k)

    def coarse_copy(it, off):
        return pltpu.make_async_remote_copy(
            src_ref=cs.at[it], dst_ref=cr.at[it, off - 1], send_sem=cs_sem.at[it, off - 1],
            recv_sem=cr_sem.at[it, off - 1], device_id=(lax.rem(ahead[it] + off, n_tm), s), device_id_type=MESH)

    def coarse_landed(it):
        rights = []
        for off in range(1, n_tm):
            if it > 0 or off < last:
                @pl.when(k >= off)
                def _():
                    coarse_copy(it, off).wait_recv()
            rights.append(operands(jnp.where(k >= off, cr[it, off - 1], 0.0)))
        return jnp.concatenate(rights, axis=0)

    def plane_out(state, kept, at):
        for z in range(8):
            shuffle[pl.ds(z, PLANE, stride=8), :] = state[z * PLANE:(z + 1) * PLANE]
        flat = shuffle[0:256].T
        kept[at] = jnp.concatenate([flat[:64], flat[64:]], axis=1)


    rights = None
    for it in range(ITERS):
        if it == 0:
            drv[0] = scaled(1, 0, 256) * (bs[...] + src[0, 0])
            exchange(near_message)
            rg_s[...] = restrict(bs[...])

            @pl.when(k < last)
            def _():
                guess_copy().start()

            @pl.when(k == last)
            def _():
                init_copy().start()
                exchange(init_edges())
        else:
            rights = coarse_landed(it - 1)
            beside_rights = beside_landed()
            product = dot(
                ms[:, :(last - 1) * 128], jnp.concatenate([rights[128:], *beside_rights], axis=1))
            pushed = prolong(selected(product[:, :128], tab_s[0, 6:7]))
            pushed_b = one_plane(selected(product[:, 128:256], tab_r[0, 6:7])[3 * 8:])
            pushed_a = one_plane(selected(product[:, 256:], tab_r[1, 6:7])[:8])
            exchanged(first_source)
            exchanged(hand_edges())
            below_d = scaled(1, 1, 2 * PLANE) * (hp[0] + jnp.concatenate([pushed_b] * 2, axis=0) + srcf[0])
            above_d = scaled(1, 2, 2 * PLANE) * (hp[1] + jnp.concatenate([pushed_a] * 2, axis=0) + srcf[1])
            e1[it, 0, PLANE:] = below_d
            e1[it, 1, :2 * PLANE] = above_d

            @pl.when(k > 0)
            def _():
                for at in range(3):
                    hand_copy(at).wait_recv()

            @pl.when(k == 0)
            def _():
                init_copy().wait_recv()
            drv[it] = scaled(1, 0, 256) * (hand[...] + pushed + src[1, 0])
            exchange(first_message(it))
            mine_copy().start()
        driven = drv[it]
        begin, part = correction_begun(driven)
        if it == 0:
            source_copy(1).wait_recv()
            put_source(0, 1, far[1])
            exchange(source_message(0))
            exchange(first_message(it))
            exchanged(near_message)
            below_d, above_d = e1[it, 0, PLANE:], e1[it, 1, :-PLANE]
        x3a[it] = corrected(driven, begin, part, below_d, above_d)
        exchange(deep_message(it))
        x3 = x3a[it]
        begin = begun(x3, driven)
        x5_mid = sweep_middle(begin, driven)
        if it == 0:
            make_steps()
        exchanged(source_message(it))
        if it > 0:
            @pl.when(k == last)
            def _():
                init_copy().wait_send()
                drained(init_edges())
                for off in range(1, n_sp):
                    own_landed(off)
                settle(gr[...].reshape(rows, CELLS), put_start)
        driven_mid = scaled(1, 0, 128) * (x5_mid + src[it, 1, 2 * PLANE:6 * PLANE])
        early = early_part(driven_mid)
        exchanged(first_message(it))
        exchanged(deep_message(it))
        x5_low, x5_high, x4_low, x4_high, below4, above4 = sweep_ends(
            x3, driven, begin, e2[it, 0], e2[it, 1], e1[it, 0], e1[it, 1])
        x5 = jnp.concatenate([x5_low, x5_mid, x5_high], axis=0)
        below5 = slab_below(below4, e1[it, 0, PLANE:], x4_low)
        above5 = slab_above(above4, e1[it, 1, :-PLANE], x4_high)
        xf[...] = x5
        driven = jnp.concatenate([
            scaled(1, 0, 64) * (x5_low + src[it, 1, :2 * PLANE]), driven_mid,
            scaled(1, 0, 64) * (x5_high + src[it, 1, 6 * PLANE:])], axis=0)
        below_d = scaled(1, 1, 2 * PLANE) * (below5 + srch[it, 0])
        above_d = scaled(1, 2, 2 * PLANE) * (above5 + srch[it, 1])
        begin, part = correction_begun(driven, early)
        x3b[it] = corrected(driven, begin, part, below_d, above_d)
        exchange(second_message(it))
        x3 = x3b[it]
        begin = begun(x3, driven)
        x5_mid = sweep_middle(begin, driven)
        if it < ITERS - 1:
            hsrc[2 * PLANE:6 * PLANE] = x5_mid

            @pl.when(k != last - 1)
            def _():
                hand_copy(0).start()
        if it == 0:
            for fine in range(2):
                put_source(1, fine, source_ref[0, fine])
            exchange(first_source)
            exchange(source_message(1))

            @pl.when(k != last - 1)
            def _():
                guess_copy().wait_recv()
        else:
            mine_copy().wait_recv()
            st[...] = bs[...] + (prolong(classes(ms[...], rights)) + (mine[...] - bs[...]))
        if it == ITERS - 1:
            plane_out(xf, both_ref, 1)
        exchanged(second_message(it))
        x5_low, x5_high, _, _, _, _ = sweep_ends(
            x3, driven, begin, e4[it, 0], e4[it, 1], below_d[PLANE:], above_d[:-PLANE])
        if it < ITERS - 1:
            hsrc[:2 * PLANE] = x5_low
            hsrc[6 * PLANE:] = x5_high

            @pl.when(k != last - 1)
            def _():
                exchange(hand_edges())
                cs[it] = restrict(hsrc[...]) - rg_r[...]
                for off in range(1, last):
                    @pl.when(after + off < n_tm)
                    def _():
                        coarse_copy(it, off).start()
                for off in range(2, n_tm):
                    @pl.when(after + off < n_tm)
                    def _():
                        exchange(coarse_beside(off))
                for at in (1, 2):
                    hand_copy(at).start()

            @pl.when(k == last)
            def _():
                cr[it, last - 1] = cs[it]
                for off in range(1, n_sp):
                    own_copy(off).start()
        else:
            residual = jnp.concatenate([x5_low, x5_mid, x5_high], axis=0) - st[...]
            cs[it] = restrict(residual)
            for off in range(1, n_tm):
                @pl.when(k + off < n_tm)
                def _():
                    coarse_copy(it, off).start()
            rights = coarse_landed(it)
            xf[...] = st[...] + (prolong(classes(ms[...], rights)) + residual)

    plane_out(xf, both_ref, 0)

    for off in range(1, n_sp):
        slots_copy(off).wait_send()
        spread_copy(off).wait_send()
    for fine in range(2):
        source_copy(fine).wait_send()
    mine_copy().wait_send()

    @pl.when(k == last)
    def _():
        for off in range(1, n_sp):
            own_copy(off).wait_send()

    @pl.when(k < last)
    def _():
        guess_copy().wait_send()

    drained(table_message)
    drained(first_source)
    drained(near_message)
    for it in range(ITERS):
        drained(source_message(it))
        drained(first_message(it))
        drained(deep_message(it))
        drained(second_message(it))
    for off in range(1, n_tm):
        @pl.when(k + off < n_tm)
        def _():
            coarse_copy(1, off).wait_send()
    for off in range(1, last):
        @pl.when((k != last - 1) & (after + off < n_tm))
        def _():
            coarse_copy(0, off).wait_send()

    @pl.when(k != last - 1)
    def _():
        for at in range(3):
            hand_copy(at).wait_send()
        drained(hand_edges())
        for off in range(2, n_tm):
            @pl.when(after + off < n_tm)
            def _():
                drained(coarse_beside(off))


def solution(mesh):
    n_tm, n_sp = mesh.shape["tm"], mesh.shape["space"]

    def body(init_state, guess, source, remap, neighbors, block_class, step_number, inverse, cstep):
        nb = init_state.shape[0]
        bk = -(-(2 * nb // n_sp) // 8) * 8
        tiles = n_sp * bk // 128
        slots = 5 + 3 * ITERS
        dma = pltpu.SemaphoreType.DMA
        full = 8 * PLANE

        def vmem(*shape, dtype=F32):
            return pltpu.VMEM(shape, dtype)

        both = pl.pallas_call(
            functools.partial(kernel, n_tm, n_sp, bk),
            name="mgrit",
            out_shape=vmem(2, nb, CELLS),
            in_specs=[pl.BlockSpec(memory_space=pl.ANY)] * 9,
            out_specs=pl.BlockSpec(memory_space=pltpu.VMEM),
            scratch_shapes=[
                vmem(nb, CELLS), vmem(1, nb, CELLS), vmem(1, 2, nb, CELLS), vmem(1, nb, dtype=jnp.int32),
                vmem(6, nb, dtype=jnp.int32), vmem(1, nb, dtype=jnp.int32), vmem(1, CLASSES),
                vmem(CLASSES * COARSE, COARSE), vmem(CLASSES * COARSE, COARSE),
                vmem(2, n_sp, bk, CELLS), vmem(n_sp, bk, CELLS), vmem(n_sp, bk, CELLS), vmem(2, nb, CELLS),
                vmem(2, 8, 128, dtype=jnp.int32), vmem(2, 8, 128, dtype=jnp.int32),
                vmem(3, 6, 8, 128, dtype=jnp.int32), vmem(3, 6, 8, 128), vmem(3, 3, 8, 128),
                vmem(ITERS, 2, full, 128), vmem(ITERS, 2, 2 * PLANE, 128), vmem(2, 2 * PLANE, 128), vmem(tiles * CELLS, 128),
                vmem(full, 128), vmem(ITERS, full, 128), vmem(ITERS, full, 128), vmem(ITERS, full, 128),
                vmem(ITERS, 2, 3 * PLANE, 128), vmem(ITERS, 2, 4 * PLANE, 128), vmem(ITERS, 2, 2 * PLANE, 128),
                vmem(full, 128), vmem(full, 128), vmem(full, 128), vmem(full, 128), vmem(2, 2 * PLANE, 128), vmem(full, 128),
                vmem(PLANE, 128), vmem(PLANE, 128),
                vmem(ITERS, PLANE, 128), vmem(ITERS, n_tm - 1, PLANE, 128), vmem(2, n_tm - 2, PLANE, 128),
                vmem(4, PLANE, 128), vmem(2 * PLANE, 128), vmem(COARSE, PLANE, 128), vmem(CLASSES * COARSE, (n_tm - 1) * 128, dtype=BF16),
                vmem(n_sp, 8, 128), vmem(n_sp, 8, 128),
                dma((9,)), dma((n_sp,)), dma((n_sp,)),
                dma((n_sp,)), dma((n_sp,)), dma((n_sp,)), dma((n_sp,)),
                dma((slots, 2)), dma((slots, 2)),
                dma((3,)), dma((3,)), dma((3,)), dma((3,)),
                dma((ITERS, n_tm - 1)), dma((ITERS, n_tm - 1)), dma((2,)), dma((2,)),
                dma((2, 2)), dma((2,)), dma((2, n_tm - 2)), dma((2, n_tm - 2)),
            ],
            compiler_params=pltpu.CompilerParams(collective_id=0, has_side_effects=True),
        )(
            init_state, guess, source, remap.reshape(1, nb), neighbors.T, block_class.reshape(1, nb),
            step_number.reshape(1, CLASSES), inverse.reshape(CLASSES * COARSE, COARSE),
            cstep.reshape(CLASSES * COARSE, COARSE),
        )
        return both[:1], both[1:]

    placed = (
        P("space", None), P("tm", "space", None), P("tm", None, "space", None), P("space"),
        P("space", None), P("space"), P(), P(), P(),
    )
    return jax.shard_map(
        body, mesh=mesh, in_specs=placed,
        out_specs=(P("tm", "space", None), P("tm", "space", None)), check_vma=False,
    )
```
